256 devices in a mesh: seq: 64 (over y, z, core), head: 4 (over x).
Axes of the slice: x: 4, y: 4, z: 8, core: 2. Of those that a mesh axis runs over, the one named last changes fastest.
Arguments:
- queries: bfloat16 [65536, 512], P('seq', 'head'), may hold values from -6 to 6
- keys: bfloat16 [65536, 512], P('seq', 'head'), may hold values from -6 to 6
- values: bfloat16 [65536, 512], P('seq', 'head'), may hold values from -6 to 6
- outputs: bfloat16 [65536, 512], P('seq', 'head'), may hold values from -6 to 6
- d_outputs: bfloat16 [65536, 512], P('seq', 'head'), may hold values from -6 to 6
- log_norm: float32 [8, 65536], P('head', 'seq'), may hold values from 4 to 5.5
- rand_owner: int32 [512, 3], P('seq'), may hold values from 0 to 63, all different within a row; in each aligned block of 8 rows (0 to 7, 8 to 15, ...) at most 2 rows name the same one
- rand_local: int32 [512, 3], P('seq'), may hold values from 0 to 7
- glob_blocks: int32 [2], replicated, may hold values from 0 to 511
Outputs:
- d_queries: bfloat16 [65536, 512], P('seq', 'head')
- d_keys: bfloat16 [65536, 512], P('seq', 'head')
- d_values: bfloat16 [65536, 512], P('seq', 'head')
The draws below stay inside these ranges and needn't reach their ends.
Inputs may be any that keep to these rules, and one draw needn't show every extreme that they name: `rand_owner`: each row names 3 different seq indices; within the 8 rows of one seq index no value is named more than 2 times, a bound that some block reaches.
All inputs are finite; a program needn't handle non-finite values.
Results may differ from the reference program's by a relative error of at most 0.0085.
Values may be sent and summed in bfloat16 or wider, within the bound.
A program may use at most 128 MiB of HBM per device.

```python
import math
import jax
import jax.numpy as jnp
import numpy as np
from jax import lax

BLOCK = 128
DH = 64
HEADS = 8
G = 2
R = 3
QB_DEV = 8
NB = 512
TOKENS = 65536
RCAP = 2
N_SEQ = 64


def set_ends(result, rng, least, largest):
    index_at = [jax.random.randint(jax.random.fold_in(rng, axis), (), 0, length) for axis, length in enumerate(result.shape)]
    main_axis = result.shape.index(max(result.shape))
    next_to = index_at[:main_axis] + [(index_at[main_axis] + 1) % result.shape[main_axis]] + index_at[main_axis + 1:]
    return result.at[tuple(index_at)].set(least).at[tuple(next_to)].set(largest)


def levels(key, dims, cuts, low, top_value):
    level = 1.0
    for dim, shards_of in cuts:
        steps = jax.random.uniform(jax.random.fold_in(jax.random.fold_in(key, 6), dim), (shards_of,), jnp.float32, low / len(cuts), top_value / len(cuts))
        level = level * jnp.repeat(jnp.exp(steps), dims[dim] // shards_of).reshape((-1,) + (1,) * (len(dims) - 1 - dim))
    return level


def assign_block(own_key, own, number, rows, count, top, reach, slope):
    order = jax.random.permutation(own_key, count)
    packed, usual = portions_of(count, rows * top, reach, slope, True), portions_of(count, rows * top, reach, slope, False)
    places = jnp.arange(count)

    def named(sizes, turn):
        used = int((sizes > 0).sum())
        fixed = max(1, used // 4)
        shifted = fixed + (places - fixed + turn * (used - fixed)) % max(1, count - fixed)
        return jnp.zeros((count,), jnp.int32).at[order[jnp.where(places < fixed, places, shifted)]].set(jnp.asarray(sizes, jnp.int32))

    sizes = jnp.where(number % 4 == 0, named(packed, number // 4), named(usual, number - number // 4 - 1))
    mixed = jax.random.permutation(jax.random.fold_in(own, 3), count)
    source_of, taker = mixed[0:count // 2 * 2:2], mixed[1:count // 2 * 2:2]
    slack = jnp.minimum(sizes[source_of] - 1, reach - sizes[taker]) // 2
    slack = jnp.where((source_of == order[0]) | (taker == order[0]) | (sizes[taker] == 0), 0, jnp.maximum(slack, 0))
    shifted = jax.random.randint(jax.random.fold_in(own, 4), (count // 2,), 0, 1 << 20) % (slack + 1)
    sizes = sizes.at[source_of].add(-shifted).at[taker].add(shifted)
    members = jnp.searchsorted(jnp.cumsum(sizes), jnp.arange(rows * top), side="right").astype(jnp.int32)
    grid = members.reshape(top, rows).T
    grid = grid[jax.random.permutation(jax.random.fold_in(own, 1), rows)]
    turn = jax.random.randint(jax.random.fold_in(own, 2), (rows, 1), 0, top)
    return jnp.take_along_axis(grid, (jnp.arange(top)[None, :] + turn) % top, axis=1)


def portions_of(count, total, bound, slope, full):
    portions = [(1 << 20) // math.isqrt(standing ** slope) + 1 for standing in range(1, count + 1)]
    largest = bound if full else min(bound, max(-(-total // count), total * portions[0] // sum(portions)))
    least = 1 if total - largest >= count - 1 else 0
    holding, surplus = [largest] + [least] * (count - 1), total - largest - least * (count - 1)
    while surplus > 0:
        movable = [i for i in range(1, count) if holding[i] < largest] or [i for i in range(1, count) if holding[i] < bound]
        whole, budget = sum([portions[i] for i in movable]), surplus
        for i in movable:
            more = min(bound - holding[i], max(1, budget * portions[i] // whole), surplus)
            holding[i] = holding[i] + more
            surplus = surplus - more
    return np.array(holding)


def gaussian(stream_key, extent, spread, bound, split=(), kind=jnp.bfloat16):
    level = levels(stream_key, extent, split, -0.22, 0.18) if split else 1.0
    drawn = jax.random.normal(stream_key, extent, jnp.float32) * spread * level
    return jnp.minimum(jnp.maximum(drawn, -bound), bound).astype(kind)


def setup_inputs(seed: int = 0) -> dict:
    key_of = jax.random.split(jax.random.key(seed), 10)
    queries = gaussian(key_of[0], (TOKENS, HEADS * DH), 1.0, 6.0, ((0, 64), (1, 4)))
    keys = gaussian(key_of[1], (TOKENS, HEADS * DH), 1.0, 6.0, ((0, 64), (1, 4)))
    values = gaussian(key_of[2], (TOKENS, HEADS * DH), 1.0, 6.0, ((0, 64), (1, 4)))
    outputs = gaussian(key_of[3], (TOKENS, HEADS * DH), 1.0, 6.0, ((0, 64), (1, 4)))
    d_outputs = gaussian(key_of[4], (TOKENS, HEADS * DH), 1.0, 6.0, ((0, 64), (1, 4)))
    log_norm = jnp.clip(4.0 + 1.5 * jax.random.uniform(key_of[5], (HEADS, TOKENS), jnp.float32) ** levels(key_of[5], (HEADS, TOKENS), ((0, 4), (1, 64)), -0.2, 0.2), 4.0, 5.5)
    rand_owner_keys = jax.random.split(jax.random.fold_in(key_of[6], 1), NB // QB_DEV)
    rand_owner_turns = jax.random.permutation(jax.random.fold_in(key_of[6], 3), NB // QB_DEV)
    rand_owner = jax.vmap(lambda own, number: assign_block(jax.random.fold_in(key_of[6], 2), own, number, QB_DEV, N_SEQ, R, RCAP, 2))(rand_owner_keys, rand_owner_turns).reshape((NB, R))
    rand_local = set_ends(jax.random.randint(key_of[7], (NB, R), 0, QB_DEV), jax.random.fold_in(key_of[7], 1), 0, QB_DEV - 1).astype(jnp.int32)
    glob_blocks = jax.random.randint(key_of[8], (G,), 0, NB).astype(jnp.int32)
    return {"queries": queries, "keys": keys, "values": values, "outputs": outputs, "d_outputs": d_outputs, "log_norm": log_norm, "rand_owner": rand_owner, "rand_local": rand_local, "glob_blocks": glob_blocks}


def rounded(value):
    return lax.optimization_barrier(value.astype(jnp.bfloat16)).astype(jnp.float32)

def reference(queries, keys, values, outputs, d_outputs, log_norm, rand_owner, rand_local, glob_blocks):
    factor = 1.0 / math.sqrt(DH)
    blocks = TOKENS // BLOCK
    block_shape = (blocks, BLOCK, HEADS, DH)
    query_all = queries.astype(jnp.float32).reshape(block_shape)
    key_all = keys.astype(jnp.float32).reshape(block_shape)
    value_all = values.astype(jnp.float32).reshape(block_shape)
    output_all = outputs.astype(jnp.float32).reshape(block_shape)
    grad_all = d_outputs.astype(jnp.float32).reshape(block_shape)
    delta_all = lax.optimization_barrier(jnp.sum(output_all * grad_all, axis=-1)).transpose(0, 2, 1)
    norm_all = log_norm.reshape(HEADS, blocks, BLOCK).transpose(1, 0, 2)
    border = jnp.zeros((1, BLOCK, HEADS, DH), jnp.float32)
    keys_pad = jnp.concatenate([border, key_all, border], axis=0)
    values_pad = jnp.concatenate([border, value_all, border], axis=0)
    block_ids = jnp.arange(blocks, dtype=jnp.int32)
    window = block_ids[:, None] + jnp.arange(3, dtype=jnp.int32)[None, :]
    global_ids = jnp.broadcast_to(glob_blocks.astype(jnp.int32)[None, :] + 1, (blocks, G))
    randoms = (rand_owner * QB_DEV + rand_local + 1).astype(jnp.int32)
    listing = jnp.concatenate([window, global_ids, randoms], axis=1).astype(jnp.int32)
    groups = blocks // QB_DEV

    def regroup(array):
        return array.reshape((groups, QB_DEV) + array.shape[1:])

    def group_step(running, slices):
        acc_keys, acc_values = running
        query_rows, grad_rows, norm_rows, delta_rows, ids_rows = slices
        key_rows = keys_pad[ids_rows]
        value_rows = values_pad[ids_rows]
        scores = jnp.einsum('nqhd,nmkhd->nmhqk', query_rows, key_rows) * factor
        weights = jnp.exp(scores - norm_rows[:, None, :, :, None])
        grad_weights = jnp.einsum('nqhd,nmkhd->nmhqk', grad_rows, value_rows)
        grad_scores = weights * (grad_weights - delta_rows[:, None, :, :, None])
        weights_low = rounded(weights)
        scores_low = rounded(grad_scores)
        grad_query = jnp.einsum('nmhqk,nmkhd->nqhd', scores_low, key_rows) * factor
        grad_key = jnp.einsum('nmhqk,nqhd->nmkhd', scores_low, query_rows) * factor
        grad_value = jnp.einsum('nmhqk,nqhd->nmkhd', weights_low, grad_rows)
        flat_ids = ids_rows.reshape(-1)
        acc_keys = acc_keys.at[flat_ids].add(grad_key.reshape((-1, BLOCK, HEADS, DH)))
        acc_values = acc_values.at[flat_ids].add(grad_value.reshape((-1, BLOCK, HEADS, DH)))
        return ((acc_keys, acc_values), grad_query)
    empty_acc = jnp.zeros((blocks + 2, BLOCK, HEADS, DH), jnp.float32)
    (acc_keys, acc_values), grad_queries = lax.scan(group_step, (empty_acc, empty_acc), (regroup(query_all), regroup(grad_all), regroup(norm_all), regroup(delta_all), regroup(listing)))
    features = HEADS * DH
    d_queries = grad_queries.reshape(TOKENS, features).astype(jnp.bfloat16)
    d_keys = acc_keys[1:-1].reshape(TOKENS, features).astype(jnp.bfloat16)
    d_values = acc_values[1:-1].reshape(TOKENS, features).astype(jnp.bfloat16)
    return (d_queries, d_keys, d_values)
```

```python
import functools
import math

import jax
import jax.numpy as jnp
from jax import lax
from jax.experimental import pallas as pl
from jax.experimental.pallas import tpu as pltpu
from jax.sharding import PartitionSpec as P

BLOCK = 128
NY, NZ, NC = 4, 8, 2
MESH = pl.DeviceIdType.MESH
F32 = jnp.float32
BF16 = jnp.bfloat16


def place():
    seq = lax.axis_index("seq")
    core = lax.rem(seq, NC)
    z = lax.rem(seq // NC, NZ)
    y = seq // (NC * NZ)
    return y, z, core


def device(y, z, core):
    return {"seq": (y * NZ + z) * NC + core}


def side_kernel(out_ref, grad_ref, norm_ref, owner_ref, local_ref, nd_ref, refs_ref):
    blocks = nd_ref.shape[0]
    for b in range(blocks):
        rows = pl.ds(b * BLOCK, BLOCK)
        product = out_ref[rows, :].astype(F32) * grad_ref[rows, :].astype(F32)
        turned = product.T
        half = turned.shape[0] // 2
        nd_ref[b, 0:2, :] = norm_ref[:, rows]
        nd_ref[b, 2:3, :] = jnp.sum(turned[:half], axis=0, keepdims=True)
        nd_ref[b, 3:4, :] = jnp.sum(turned[half:], axis=0, keepdims=True)
        nd_ref[b, 4:8, :] = jnp.zeros((4, BLOCK), F32)
    refs_ref[...] = jnp.zeros(refs_ref.shape, jnp.int32)
    refs_ref[:, 0:3] = owner_ref[...] * blocks + local_ref[...]


def gather_kernel(
    q_ref, d_ref, k_ref, v_ref, nd_ref, rf_ref,
    qd_out, kv_out, nd_out, rf_out,
    zsend, zrecv, ysend, yrecv, csend, crecv, lsem,
):
    y, z, c = place()
    zdev = [device(y, lax.rem(z + 1, NZ), c), device(y, lax.rem(z + NZ - 1, NZ), c)]
    ydev = [device(lax.rem(y + 1, NY), z, c), device(lax.rem(y + NY - 1, NY), z, c)]
    cdev = device(y, z, 1 - c)

    barrier = pltpu.get_barrier_semaphore()
    for target in zdev + ydev + [cdev]:
        pl.semaphore_signal(barrier, inc=1, device_id=target, device_id_type=MESH)
    pl.semaphore_wait(barrier, 5)

    own = [q_ref, d_ref, nd_ref, rf_ref]

    def zslot(part, slot):
        if part < 2:
            return qd_out.at[slot, part]
        return (nd_out, rf_out)[part - 2].at[slot]

    def zcopy(way, step, part):
        slot = lax.rem(z + (NZ - step + 1 if way == 0 else step - 1), NZ)
        return pltpu.make_async_remote_copy(
            src_ref=own[part] if step == 1 else zslot(part, slot),
            dst_ref=zslot(part, slot),
            send_sem=zsend.at[way, step - 1, part],
            recv_sem=zrecv.at[way, step - 1, part],
            device_id=zdev[way],
            device_id_type=MESH,
        )

    def zparts(way, step):
        if step < 4:
            return (2, 3, 0, 1)
        return (2, 3, 0) if way == 0 else (1,)

    def ycopy(way, step, part):
        row = lax.rem(y + ((NY if step == 1 else NY - 1) if way == 0 else step - 1), NY)
        slot = row * NC + c
        return pltpu.make_async_remote_copy(
            src_ref=(k_ref, v_ref)[part] if step == 1 else kv_out.at[slot, part],
            dst_ref=kv_out.at[slot, part],
            send_sem=ysend.at[way, step - 1, part],
            recv_sem=yrecv.at[way, step - 1, part],
            device_id=ydev[way],
            device_id_type=MESH,
        )

    def ccopy(offset, part):
        slot = lax.rem(y + offset, NY) * NC + c
        return pltpu.make_async_remote_copy(
            src_ref=(k_ref, v_ref)[part] if offset == 0 else kv_out.at[slot, part],
            dst_ref=kv_out.at[slot, part],
            send_sem=csend.at[offset, part],
            recv_sem=crecv.at[offset, part],
            device_id=cdev,
            device_id_type=MESH,
        )

    for part in (2, 3, 0, 1):
        for way in (0, 1):
            zcopy(way, 1, part).start()
    for part in (0, 1):
        for way in (0, 1):
            ycopy(way, 1, part).start()
        ccopy(0, part).start()
    local = [
        pltpu.make_async_copy(q_ref, qd_out.at[z, 0], lsem.at[0]),
        pltpu.make_async_copy(d_ref, qd_out.at[z, 1], lsem.at[1]),
        pltpu.make_async_copy(nd_ref, nd_out.at[z], lsem.at[2]),
        pltpu.make_async_copy(rf_ref, rf_out.at[z], lsem.at[3]),
        pltpu.make_async_copy(k_ref, kv_out.at[y * NC + c, 0], lsem.at[4]),
        pltpu.make_async_copy(v_ref, kv_out.at[y * NC + c, 1], lsem.at[5]),
    ]
    for copy in local:
        copy.start()

    def zround(step):
        for part in (2, 3, 0, 1):
            for way in (0, 1):
                if part in zparts(way, step):
                    zcopy(way, step, part).wait_recv()
                    if step < 4 and part in zparts(way, step + 1):
                        zcopy(way, step + 1, part).start()

    zround(1)
    for part in (0, 1):
        for way in (0, 1):
            ycopy(way, 1, part).wait_recv()
            if part == way:
                ycopy(way, 2, part).start()
            ccopy(NY - 1 if way == 0 else 1, part).start()
    zround(2)
    for way in (0, 1):
        ycopy(way, 2, way).wait_recv()
        ccopy(2, way).start()
    zround(3)
    zround(4)
    for offset in range(NY):
        for part in (0, 1):
            ccopy(offset, part).wait()
    for way in (0, 1):
        for step in range(1, 5):
            for part in zparts(way, step):
                zcopy(way, step, part).wait_send()
        for part in (0, 1):
            ycopy(way, 1, part).wait_send()
        ycopy(way, 2, way).wait_send()
    for copy in local:
        copy.wait()


def pair_terms(q, d, nd, k, v, factor):
    lane = lax.broadcasted_iota(jnp.int32, k.shape, 1)
    half = k.shape[1] // 2
    zero = jnp.zeros_like(k)
    k2 = jnp.concatenate([jnp.where(lane < half, k, zero), jnp.where(lane < half, zero, k)], axis=0)
    v2 = jnp.concatenate([jnp.where(lane < half, v, zero), jnp.where(lane < half, zero, v)], axis=0)
    across = (((1,), (1,)), ((), ()))
    scores = lax.dot_general(k2, q, across, preferred_element_type=F32)
    grads = lax.dot_general(v2, d, across, preferred_element_type=F32)
    rows = k.shape[0]

    def per_head(first):
        return jnp.concatenate(
            [jnp.broadcast_to(nd[i : i + 1, :], (rows, BLOCK)) for i in (first, first + 1)], axis=0
        )

    weights = jnp.exp(scores * factor - per_head(0))
    grad_scores = weights * (grads - per_head(2))
    weights_low = weights.astype(BF16)
    scores_low = grad_scores.astype(BF16)
    dv2 = jnp.dot(weights_low, d, preferred_element_type=F32)
    dk2 = jnp.dot(scores_low, q, preferred_element_type=F32)
    dq = lax.dot_general(scores_low, k2, (((0,), (0,)), ((), ())), preferred_element_type=F32)
    dv = jnp.where(lane < half, dv2[:rows], dv2[rows:])
    dk = jnp.where(lane < half, dk2[:rows], dk2[rows:])
    return dq * factor, dk * factor, dv


def pair_kernel(
    glob_ref, rf_ref, qd_ref, kv_ref, nd_ref, dq_out, dkv_out, dq_acc, dk_acc, dv_acc, list_ref, *, factor
):
    y, z, c = place()
    blocks = nd_ref.shape[1]
    chunk = 8

    @pl.loop(0, NZ * blocks)
    def _(i):
        zero = jnp.zeros((BLOCK, BLOCK), F32)
        dq_acc[i] = zero
        dk_acc[i] = zero
        dv_acc[i] = zero

    def key_place(key):
        owner = key // blocks
        here = lax.rem(owner // NC, NZ) == z
        slot = (owner // (NC * NZ)) * NC + lax.rem(owner, NC)
        return here, slot * blocks + lax.rem(key, blocks)

    def add(n, query, key, wanted):
        here, where = key_place(key)
        list_ref[n] = query * (NZ * blocks) + where
        return n + jnp.where(jnp.logical_and(here, wanted), 1, 0).astype(jnp.int32)

    last = NY * NZ * NC * blocks - 1

    def per_query(i, n):
        slot = i // blocks
        b = lax.rem(i, blocks)
        for r in range(3):
            n = add(n, i, rf_ref[slot, b, r], True)
        block = ((y * NZ + slot) * NC + c) * blocks + b
        for key in (block - 1, block, block + 1):
            n = add(n, i, jnp.clip(key, 0, last), jnp.logical_and(key >= 0, key <= last))
        for g in range(2):
            n = add(n, i, glob_ref[g], True)
        return n

    count = lax.fori_loop(0, NZ * blocks, per_query, jnp.int32(0))

    @pl.loop(0, count)
    def _(i):
        item = list_ref[i]
        query = item // (NZ * blocks)
        key = lax.rem(item, NZ * blocks)
        qs = query // blocks
        qb = lax.rem(query, blocks)
        qrows = pl.ds(pl.multiple_of(qb * BLOCK, BLOCK), BLOCK)
        ks = key // blocks
        krows = pl.ds(pl.multiple_of(lax.rem(key, blocks) * BLOCK, BLOCK), BLOCK)
        dq, dk, dv = pair_terms(
            qd_ref[qs, 0, qrows, :],
            qd_ref[qs, 1, qrows, :],
            nd_ref[qs, qb],
            kv_ref[ks, 0, krows, :],
            kv_ref[ks, 1, krows, :],
            factor,
        )
        dq_acc[query] += dq
        dk_acc[key] += dk
        dv_acc[key] += dv

    @pl.loop(0, NZ * blocks)
    def _(i):
        slot = i // blocks
        rows = pl.ds(pl.multiple_of(lax.rem(i, blocks) * BLOCK, BLOCK), BLOCK)
        dq_out[slot, rows, :] = dq_acc[i].astype(BF16)
        dkv_out[slot, 0, rows, :] = dk_acc[i].astype(BF16)
        dkv_out[slot, 1, rows, :] = dv_acc[i].astype(BF16)


def reduce_kernel(
    dq_in, dkv_in, dq_out, dk_out, dv_out,
    zbuf, zin, cin, csum, ybuf, yin,
    zsend, zrecv, ysend, yrecv, csend, crecv,
):
    y, z, c = place()
    half = dq_out.shape[0] // 2
    zdev = [device(y, lax.rem(z + 1, NZ), c), device(y, lax.rem(z + NZ - 1, NZ), c)]
    ydev = [device(lax.rem(y + 1, NY), z, c), device(lax.rem(y + NY - 1, NY), z, c)]
    cdev = device(y, z, 1 - c)

    barrier = pltpu.get_barrier_semaphore()
    for target in zdev + ydev + [cdev]:
        pl.semaphore_signal(barrier, inc=1, device_id=target, device_id_type=MESH)
    pl.semaphore_wait(barrier, 5)

    def zparts(way, step):
        return (way,) if step == 1 else (0, 1)

    def zplain(way, step, part):
        return step == 1 or (step == 2 and part != way)

    def ztarget(way, step):
        return lax.rem(z + (5 - step if way == 0 else NZ - 5 + step), NZ)

    def zcopy(way, step, part):
        rows = pl.ds(part * half, half)
        if zplain(way, step, part):
            source = dq_in.at[ztarget(way, step), rows]
        else:
            source = zbuf.at[way, step - 1, rows]
        return pltpu.make_async_remote_copy(
            src_ref=source,
            dst_ref=zin.at[way, step - 1, rows],
            send_sem=zsend.at[way, step - 1, part],
            recv_sem=zrecv.at[way, step - 1, part],
            device_id=zdev[way],
            device_id_type=MESH,
        )

    def ccopy(offset, part):
        row = lax.rem(y + offset, NY)
        return pltpu.make_async_remote_copy(
            src_ref=dkv_in.at[row * NC + 1 - c, part],
            dst_ref=cin.at[offset, part],
            send_sem=csend.at[offset, part],
            recv_sem=crecv.at[offset, part],
            device_id=cdev,
            device_id_type=MESH,
        )

    def ycopy(way, step, part):
        return pltpu.make_async_remote_copy(
            src_ref=csum.at[2, part] if step == 1 else ybuf.at[way, part],
            dst_ref=yin.at[way, step - 1, part],
            send_sem=ysend.at[way, step - 1, part],
            recv_sem=yrecv.at[way, step - 1, part],
            device_id=ydev[way],
            device_id_type=MESH,
        )

    for offset in (2, 1, 3, 0):
        for part in (0, 1):
            ccopy(offset, part).start()
    for way in (0, 1):
        zcopy(way, 1, way).start()
        zcopy(way, 2, 1 - way).start()

    def zround(step):
        for part in (0, 1):
            for way in (0, 1):
                if part in zparts(way, step):
                    zcopy(way, step, part).wait_recv()
                    rows = pl.ds(part * half, half)
                    mine = dq_in[ztarget(way, step + 1), rows, :].astype(F32)
                    zbuf[way, step, rows, :] = (mine + zin[way, step - 1, rows, :].astype(F32)).astype(BF16)
                    zcopy(way, step + 1, part).start()

    def cadd(offset, part):
        ccopy(offset, part).wait_recv()
        row = lax.rem(y + offset, NY)
        mine = dkv_in[row * NC + c, part].astype(F32)
        return mine + cin[offset, part].astype(F32)

    for part in (0, 1):
        csum[2, part] = cadd(2, part).astype(BF16)
        ycopy(part, 1, part).start()
    zround(1)
    for way in (0, 1):
        offset = 1 if way == 0 else NY - 1
        for part in (1 - way, way):
            total = cadd(offset, part)
            if part == way:
                ycopy(way, 1, part).wait_recv()
                total = total + yin[way, 0, part].astype(F32)
            ybuf[way, part] = total.astype(BF16)
            ycopy(way, 2, part).start()
    zround(2)
    zround(3)
    for part, out in ((0, dk_out), (1, dv_out)):
        total = cadd(0, part)
        for way in (0, 1):
            ycopy(way, 2, part).wait_recv()
            total = total + yin[way, 1, part].astype(F32)
        out[...] = total.astype(BF16)
    for part in (0, 1):
        rows = pl.ds(part * half, half)
        total = dq_in[z, rows, :].astype(F32)
        for way in (0, 1):
            zcopy(way, 4, part).wait_recv()
            total = total + zin[way, 3, rows, :].astype(F32)
        dq_out[rows, :] = total.astype(BF16)
    for way in (0, 1):
        for step in range(1, 5):
            for part in zparts(way, step):
                zcopy(way, step, part).wait_send()
        ycopy(way, 1, way).wait_send()
        for part in (0, 1):
            ycopy(way, 2, part).wait_send()
    for offset in range(NY):
        for part in (0, 1):
            ccopy(offset, part).wait_send()


def shards(queries, keys, values, outputs, d_outputs, log_norm, rand_owner, rand_local, glob_blocks):
    tokens, features = queries.shape
    blocks = tokens // BLOCK
    factor = 1.0 / math.sqrt(features // log_norm.shape[0])
    vmem = pl.BlockSpec(memory_space=pltpu.VMEM)
    smem = pl.BlockSpec(memory_space=pltpu.SMEM)
    anywhere = pl.BlockSpec(memory_space=pl.ANY)
    dma = pltpu.SemaphoreType.DMA

    side, refs = pl.pallas_call(
        side_kernel,
        out_shape=(
            jax.ShapeDtypeStruct((blocks, 8, BLOCK), F32),
            jax.ShapeDtypeStruct((blocks, BLOCK), jnp.int32),
        ),
        in_specs=[vmem] * 5,
        out_specs=(vmem, vmem),
        name="side",
    )(outputs, d_outputs, log_norm, rand_owner, rand_local)

    qd, kv, nd, rf = pl.pallas_call(
        gather_kernel,
        out_shape=(
            jax.ShapeDtypeStruct((NZ, 2, tokens, features), BF16),
            jax.ShapeDtypeStruct((NY * NC, 2, tokens, features), BF16),
            jax.ShapeDtypeStruct((NZ, blocks, 8, BLOCK), F32),
            jax.ShapeDtypeStruct((NZ, blocks, BLOCK), jnp.int32),
        ),
        in_specs=[vmem] * 6,
        out_specs=(anywhere,) * 4,
        scratch_shapes=[
            dma((2, 4, 4)), dma((2, 4, 4)), dma((2, 2, 2)), dma((2, 2, 2)),
            dma((NY, 2)), dma((NY, 2)), dma((6,)),
        ],
        compiler_params=pltpu.CompilerParams(collective_id=0, has_side_effects=True),
        name="gather",
    )(queries, d_outputs, keys, values, side, refs)

    dq_part, dkv_part = pl.pallas_call(
        functools.partial(pair_kernel, factor=factor),
        out_shape=(
            jax.ShapeDtypeStruct((NZ, tokens, features), BF16),
            jax.ShapeDtypeStruct((NY * NC, 2, tokens, features), BF16),
        ),
        in_specs=[smem, smem, vmem, vmem, vmem],
        out_specs=(vmem, vmem),
        scratch_shapes=[
            pltpu.VMEM((NZ * blocks, BLOCK, features), F32),
            pltpu.VMEM((NY * NC * blocks, BLOCK, features), F32),
            pltpu.VMEM((NY * NC * blocks, BLOCK, features), F32),
            pltpu.SMEM((NZ * blocks * 8 + 8,), jnp.int32),
        ],
        compiler_params=pltpu.CompilerParams(vmem_limit_bytes=50 * 1024 * 1024),
        name="pairs",
    )(glob_blocks, rf, qd, kv, nd)

    return tuple(pl.pallas_call(
        reduce_kernel,
        out_shape=(jax.ShapeDtypeStruct((tokens, features), BF16),) * 3,
        in_specs=[vmem] * 2,
        out_specs=(vmem,) * 3,
        scratch_shapes=[
            pltpu.VMEM((2, 4, tokens, features), BF16),
            pltpu.VMEM((2, 4, tokens, features), BF16),
            pltpu.VMEM((NY, 2, tokens, features), BF16),
            pltpu.VMEM((NY, 2, tokens, features), BF16),
            pltpu.VMEM((2, 2, tokens, features), BF16),
            pltpu.VMEM((2, 2, 2, tokens, features), BF16),
            dma((2, 4, 2)), dma((2, 4, 2)), dma((2, 2, 2)), dma((2, 2, 2)), dma((NY, 2)), dma((NY, 2)),
        ],
        compiler_params=pltpu.CompilerParams(
            collective_id=1, has_side_effects=True, vmem_limit_bytes=50 * 1024 * 1024
        ),
        name="reduce",
    )(dq_part, dkv_part))


def solution(mesh):
    placed = (
        P("seq", "head"), P("seq", "head"), P("seq", "head"), P("seq", "head"), P("seq", "head"),
        P("head", "seq"), P("seq", None), P("seq", None), P(),
    )
    return jax.shard_map(
        shards,
        mesh=mesh,
        in_specs=placed,
        out_specs=(P("seq", "head"), P("seq", "head"), P("seq", "head")),
        check_vma=False,
    )
```

```python
import functools
import math

import jax
import jax.numpy as jnp
from jax import lax
from jax.experimental import pallas as pl
from jax.experimental.pallas import tpu as pltpu
from jax.sharding import PartitionSpec as P

BLOCK = 128
NY, NZ, NC = 4, 8, 2
MESH = pl.DeviceIdType.MESH
F32 = jnp.float32
BF16 = jnp.bfloat16
MIB = 1024 * 1024


def place():
    seq = lax.axis_index("seq")
    core = lax.rem(seq, NC)
    z = lax.rem(seq // NC, NZ)
    y = seq // (NC * NZ)
    return y, z, core


def device(y, z, core):
    return {"seq": (y * NZ + z) * NC + core}


def side_kernel(
    out_ref, grad_ref, norm_ref, owner_ref, local_ref, key_ref, value_ref, glob_ref, nd_ref, refs_ref, cand_ref
):
    blocks = out_ref.shape[0] // BLOCK
    for b in range(blocks):
        rows = pl.ds(b * BLOCK, BLOCK)
        product = out_ref[rows, :].astype(F32) * grad_ref[rows, :].astype(F32)
        turned = product.T
        half = turned.shape[0] // 2
        first = 4 * (b % 2)
        nd_ref[b // 2, first : first + 2, :] = norm_ref[:, rows]
        nd_ref[b // 2, first + 2 : first + 3, :] = jnp.sum(turned[:half], axis=0, keepdims=True)
        nd_ref[b // 2, first + 3 : first + 4, :] = jnp.sum(turned[half:], axis=0, keepdims=True)
    owner = owner_ref[...]
    column = jnp.bitwise_and(owner >> 1, NZ - 1)
    member = (owner >> 4) * NC + jnp.bitwise_and(owner, 1)
    refs_ref[...] = jnp.zeros(refs_ref.shape, jnp.int32)
    refs_ref[0:3, 0:blocks] = (column * (NY * NC) + member) * blocks + local_ref[...]
    seq = lax.axis_index("seq")
    half = BLOCK // 2
    for g in range(2):
        where = glob_ref[g]
        mine = (where // blocks) == seq
        start = pl.multiple_of(lax.rem(where, blocks) * BLOCK, BLOCK)
        for i, ref in enumerate((key_ref, value_ref)):
            block = ref[pl.ds(start, BLOCK), :]
            block = jnp.where(mine, block, jnp.zeros_like(block))
            cand_ref[4 * g + 2 * i] = block[:half]
            cand_ref[4 * g + 2 * i + 1] = block[half:]


def pair_terms(q, d, nd, k, v, factor):
    lane = lax.broadcasted_iota(jnp.int32, k.shape, 1)
    half = k.shape[1] // 2
    rows = k.shape[0]
    zero = jnp.zeros_like(k)
    k = k * factor
    k2 = jnp.concatenate([jnp.where(lane < half, k, zero), jnp.where(lane < half, zero, k)], axis=0)
    v2 = jnp.concatenate([jnp.where(lane < half, v, zero), jnp.where(lane < half, zero, v)], axis=0)
    across = (((1,), (1,)), ((), ()))
    scores = lax.dot_general(k2, q, across, preferred_element_type=F32)
    grads = lax.dot_general(v2, d, across, preferred_element_type=F32)

    def per_head(first):
        return jnp.concatenate(
            [jnp.broadcast_to(nd[i : i + 1, :], (rows, BLOCK)) for i in (first, first + 1)], axis=0
        )

    weights = jnp.exp(scores - per_head(0))
    grad_scores = weights * (grads - per_head(2))
    weights_low = weights.astype(BF16)
    scores_low = grad_scores.astype(BF16)
    dv2 = jnp.dot(weights_low, d, preferred_element_type=F32)
    dk2 = jnp.dot(scores_low, q, preferred_element_type=F32)
    dq = lax.dot_general(scores_low, k2, (((0,), (0,)), ((), ())), preferred_element_type=F32)
    dv = jnp.where(lane < half, dv2[:rows], dv2[rows:])
    dk = jnp.where(lane < half, dk2[:rows], dk2[rows:])
    return dq, dk, dv


def query_rows(nd_tile, b):
    return jnp.where(lax.rem(b, 2) == 0, nd_tile[0:4], nd_tile[4:8])


def gather_kernel(
    q_ref, d_ref, k_ref, v_ref, nd_ref, rf_ref, cand_ref,
    qd_out, kv_out, nd_out, rf_out, dq_out, dk_out, dv_out, total_out,
    g1in, s1, g2in, s2, g3in, s3, gkv, gacc, r1in, t1, r2in, t2, r3in,
    zsend, zrecv, ysend, yrecv, csend, crecv, gsend, grecv, lsem,
    *, factor,
):
    y, z, c = place()
    blocks = q_ref.shape[0] // BLOCK
    half = BLOCK // 2
    zdev = [device(y, lax.rem(z + 1, NZ), c), device(y, lax.rem(z + NZ - 1, NZ), c)]
    ydev = [device(lax.rem(y + 1, NY), z, c), device(lax.rem(y + NY - 1, NY), z, c)]
    cdev = device(y, z, 1 - c)
    me = y * NC + c

    def member(offset):
        return lax.rem(me + offset, NY * NC)

    def member_device(offset):
        other = member(offset)
        return device(other // NC, z, lax.rem(other, NC))

    def row_device(offset):
        return device(y, lax.rem(z + offset, NZ), c)

    barrier = pltpu.get_barrier_semaphore()
    for offset in range(1, 8):
        for target in (member_device(offset), row_device(offset)):
            pl.semaphore_signal(barrier, inc=1, device_id=target, device_id_type=MESH)
    pl.semaphore_wait(barrier, 14)

    own = [q_ref, d_ref, nd_ref, rf_ref]

    def zslot(part, slot):
        if part < 2:
            return qd_out.at[slot, part]
        return (nd_out, rf_out)[part - 2].at[slot]

    def zcopy(way, step, part):
        slot = lax.rem(z + (NZ - step + 1 if way == 0 else step - 1), NZ)
        return pltpu.make_async_remote_copy(
            src_ref=own[part] if step == 1 else zslot(part, slot),
            dst_ref=zslot(part, slot),
            send_sem=zsend.at[way, step - 1, part],
            recv_sem=zrecv.at[way, step - 1, part],
            device_id=zdev[way],
            device_id_type=MESH,
        )

    def zparts(way, step):
        if step < 4:
            return (0, 2, 3, 1)
        return (0, 2, 3) if way == 0 else (1,)

    def ycopy(way, step, part):
        row = lax.rem(y + ((NY if step == 1 else NY - 1) if way == 0 else step - 1), NY)
        slot = row * NC + c
        return pltpu.make_async_remote_copy(
            src_ref=(k_ref, v_ref)[part] if step == 1 else kv_out.at[slot, part],
            dst_ref=kv_out.at[slot, part],
            send_sem=ysend.at[way, step - 1, part],
            recv_sem=yrecv.at[way, step - 1, part],
            device_id=ydev[way],
            device_id_type=MESH,
        )

    def ccopy(offset, part):
        slot = lax.rem(y + offset, NY) * NC + c
        return pltpu.make_async_remote_copy(
            src_ref=(k_ref, v_ref)[part] if offset == 0 else kv_out.at[slot, part],
            dst_ref=kv_out.at[slot, part],
            send_sem=csend.at[offset, part],
            recv_sem=crecv.at[offset, part],
            device_id=cdev,
            device_id_type=MESH,
        )

    def small(phase, offset):
        over_column = phase in (0, 3, 4)
        other = member(offset) if over_column else lax.rem(z + offset, NZ)
        source, target = (
            (cand_ref.at[other], g1in.at[offset]),
            (s1.at[other], g2in.at[offset]),
            (s2, g3in.at[offset]),
            (gkv.at[me], gkv.at[me]),
            (gacc.at[other], r1in.at[offset]),
            (t1.at[other], r2in.at[offset]),
            (t2, r3in.at[offset]),
        )[phase]
        return pltpu.make_async_remote_copy(
            src_ref=source,
            dst_ref=target,
            send_sem=gsend.at[phase, offset],
            recv_sem=grecv.at[phase, offset],
            device_id=member_device(offset) if over_column else row_device(offset),
            device_id_type=MESH,
        )

    def small_start(phase):
        for offset in range(1, 8):
            small(phase, offset).start()

    def small_wait(phase):
        for offset in range(1, 8):
            small(phase, offset).wait_recv()

    def zstart(step, parts):
        for part in parts:
            for way in (0, 1):
                if part in zparts(way, step):
                    zcopy(way, step, part).start()

    def zpass(step, parts):
        for part in parts:
            for way in (0, 1):
                if part in zparts(way, step):
                    zcopy(way, step, part).wait_recv()
                    if step < 4 and part in zparts(way, step + 1):
                        zcopy(way, step + 1, part).start()

    def block_rows(b):
        return pl.ds(pl.multiple_of(b * BLOCK, BLOCK), BLOCK)

    def window(first, end):
        @pl.loop(first, end)
        def _(i):
            up = (i >= blocks).astype(jnp.int32)
            down = (i >= 2 * blocks - 1).astype(jnp.int32)
            low = i - up * blocks - down * (blocks - 1)
            qb = low + down
            kb = low + up - down
            rows, krows = block_rows(qb), block_rows(kb)
            dq, dk, dv = pair_terms(
                q_ref[rows, :], d_ref[rows, :], query_rows(nd_ref[qb // 2], qb), k_ref[krows, :], v_ref[krows, :], factor
            )
            dq_out[rows, :] += dq
            dk_out[krows, :] += dk
            dv_out[krows, :] += dv

    def whole(g):
        gk = jnp.concatenate([gkv[4 * g], gkv[4 * g + 1]], axis=0)
        gv = jnp.concatenate([gkv[4 * g + 2], gkv[4 * g + 3]], axis=0)

        @pl.loop(0, blocks)
        def _(b):
            rows = block_rows(b)
            dq, dk, dv = pair_terms(
                q_ref[rows, :], d_ref[rows, :], query_rows(nd_ref[b // 2], b), gk, gv, factor
            )
            dq_out[rows, :] += dq
            gacc[4 * g] += dk[:half]
            gacc[4 * g + 1] += dk[half:]
            gacc[4 * g + 2] += dv[:half]
            gacc[4 * g + 3] += dv[half:]

    zstart(1, (0,))
    small_start(0)
    local = [
        pltpu.make_async_copy(q_ref, qd_out.at[z, 0], lsem.at[0]),
        pltpu.make_async_copy(d_ref, qd_out.at[z, 1], lsem.at[1]),
        pltpu.make_async_copy(nd_ref, nd_out.at[z], lsem.at[2]),
        pltpu.make_async_copy(rf_ref, rf_out.at[z], lsem.at[3]),
        pltpu.make_async_copy(k_ref, kv_out.at[me, 0], lsem.at[4]),
        pltpu.make_async_copy(v_ref, kv_out.at[me, 1], lsem.at[5]),
    ]
    for copy in local:
        copy.start()

    @pl.loop(0, blocks)
    def _(b):
        zero = jnp.zeros((BLOCK, q_ref.shape[1]), F32)
        dq_out[block_rows(b), :] = zero
        dk_out[block_rows(b), :] = zero
        dv_out[block_rows(b), :] = zero
        gacc[b] = zero[:half]

    window(0, 2)
    small_wait(0)
    slice_sum = cand_ref[me].astype(F32)
    for offset in range(1, 8):
        slice_sum = slice_sum + g1in[offset].astype(F32)
    s1[...] = slice_sum.astype(BF16).reshape(s1.shape)
    zstart(1, (2, 3, 1))
    window(2, 4)
    small_start(1)
    window(4, 7)
    small_wait(1)
    part_sum = s1[z].astype(F32)
    for offset in range(1, 8):
        part_sum = part_sum + g2in[offset].astype(F32)
    s2[...] = part_sum.astype(BF16)
    window(7, 8)
    small_start(2)
    zpass(1, (0,))
    window(8, 11)
    small_wait(2)
    s3[z] = s2[...]
    for offset in range(1, 8):
        s3[lax.rem(z + NZ - offset, NZ)] = g3in[offset]
    gkv[me] = s3[...].reshape(gkv.shape[1:])
    window(11, 13)
    small_start(3)
    for part in (0, 1):
        for way in (0, 1):
            ycopy(way, 1, part).start()
        ccopy(0, part).start()
    zpass(1, (2, 3, 1))
    window(13, 16)
    small_wait(3)
    whole(0)
    zpass(2, (0,))
    whole(1)
    for part in (0, 1):
        for way in (0, 1):
            ycopy(way, 1, part).wait_recv()
            if part == way:
                ycopy(way, 2, part).start()
            ccopy(NY - 1 if way == 0 else 1, part).start()
    small_start(4)
    zpass(2, (2, 3, 1))
    window(16, 19)
    small_wait(4)
    slice_sum = gacc[me]
    for offset in range(1, 8):
        slice_sum = slice_sum + r1in[offset]
    t1[...] = slice_sum.reshape(t1.shape)
    window(19, 21)
    small_start(5)
    for way in (0, 1):
        ycopy(way, 2, way).wait_recv()
        ccopy(2, way).start()
    zpass(3, (0,))
    window(21, 22)
    small_wait(5)
    part_sum = t1[z]
    for offset in range(1, 8):
        part_sum = part_sum + r2in[offset]
    t2[...] = part_sum
    zpass(3, (2, 3, 1))
    small_start(6)
    small_wait(6)
    total_out[z] = t2[...]
    for offset in range(1, 8):
        total_out[lax.rem(z + NZ - offset, NZ)] = r3in[offset]
    zpass(4, (0, 2, 3, 1))
    for offset in range(NY):
        for part in (0, 1):
            ccopy(offset, part).wait()
    for way in (0, 1):
        for step in range(1, 5):
            for part in zparts(way, step):
                zcopy(way, step, part).wait_send()
        for part in (0, 1):
            ycopy(way, 1, part).wait_send()
        ycopy(way, 2, way).wait_send()
    for phase in range(7):
        for offset in range(1, 8):
            small(phase, offset).wait_send()
    for copy in local:
        copy.wait()


def pair_kernel(
    glob_ref, rf_hbm, qd_hbm, kv_hbm, nd_hbm, total_ref, dq_out, dkv_out,
    dq_acc, dk_acc, dv_acc, qd_ref, kv_ref, nd_ref, rf_ref, list_ref, sem,
    *, factor,
):
    y, z, c = place()
    blocks = qd_ref.shape[2] // BLOCK
    grid = NZ * blocks
    copies = [
        pltpu.make_async_copy(rf_hbm, rf_ref, sem.at[0]),
        pltpu.make_async_copy(nd_hbm, nd_ref, sem.at[1]),
        pltpu.make_async_copy(qd_hbm, qd_ref, sem.at[2]),
        pltpu.make_async_copy(kv_hbm, kv_ref, sem.at[3]),
    ]
    for copy in copies:
        copy.start()

    @pl.loop(0, grid)
    def _(i):
        zero = jnp.zeros((BLOCK, qd_ref.shape[3]), F32)
        dq_acc[i] = zero
        dk_acc[i] = zero
        dv_acc[i] = zero

    half = BLOCK // 2
    for g in range(2):
        owner = glob_ref[g] // blocks
        column = lax.rem(owner // NC, NZ)
        member = (owner // (NC * NZ)) * NC + lax.rem(owner, NC)
        slot = member * blocks + lax.rem(glob_ref[g], blocks)
        mine = jnp.logical_and(column == z, (y * NC + c) // 4 == g)
        total = total_ref[...].reshape(half, total_ref.shape[2])
        rows = pl.ds(pl.multiple_of(c * half, half), half)

        @pl.when(jnp.logical_and(mine, lax.rem(y, 2) == 0))
        def _():
            dk_acc[slot, rows, :] += total

        @pl.when(jnp.logical_and(mine, lax.rem(y, 2) == 1))
        def _():
            dv_acc[slot, rows, :] += total

    def window_item(n, slot, b, seq, key_block, wanted):
        member = (seq // (NC * NZ)) * NC + lax.rem(seq, NC)
        list_ref[n] = ((slot * blocks + b) << 8) | ((member * blocks + key_block) << 1)
        return n + wanted.astype(jnp.int32)

    seq = (y * NZ + z) * NC + c
    nearby = jnp.where(c == 0, seq + 1, seq - 1)
    count = window_item(
        jnp.int32(0), z, jnp.where(c == 0, blocks - 1, 0), nearby, jnp.where(c == 0, 0, blocks - 1), seq >= 0
    )
    far_slot = jnp.where(c == 0, lax.rem(z + 1, NZ), lax.rem(z + NZ - 1, NZ))
    far_seq = (y * NZ + far_slot) * NC + c
    far_key = jnp.where(c == 0, far_seq - 1, far_seq + 1)
    inside = jnp.logical_and(far_key >= 0, far_key < NY * NZ * NC)
    count = window_item(
        count, far_slot, jnp.where(c == 0, 0, blocks - 1),
        jnp.clip(far_key, 0, NY * NZ * NC - 1), jnp.where(c == 0, blocks - 1, 0), inside,
    )

    copies[0].wait()

    def per_slot(slot, n):
        for b in range(blocks):
            for r in range(3):
                code = rf_ref[slot, r, b]
                list_ref[n] = ((slot * blocks + b) << 8) | ((code & (grid - 1)) << 1)
                n = n + ((code >> 6) == z).astype(jnp.int32)
        return n

    count = lax.fori_loop(0, NZ, per_slot, count)
    list_ref[count] = jnp.int32(1)
    for copy in copies[1:]:
        copy.wait()

    def terms(item):
        query, key = item >> 8, (item >> 1) & (grid - 1)
        qs, qb = query >> 3, query & (blocks - 1)
        ks, kb = key >> 3, key & (blocks - 1)
        qrows = pl.ds(pl.multiple_of(qb * BLOCK, BLOCK), BLOCK)
        krows = pl.ds(pl.multiple_of(kb * BLOCK, BLOCK), BLOCK)
        return pair_terms(
            qd_ref[qs, 0, qrows, :],
            qd_ref[qs, 1, qrows, :],
            query_rows(nd_ref[qs, qb >> 1], qb),
            kv_ref[ks, 0, krows, :],
            kv_ref[ks, 1, krows, :],
            factor,
        )

    @pl.loop(0, (count + 1) // 2)
    def _(i):
        items = [list_ref[2 * i], list_ref[2 * i + 1]]
        sums = [terms(item) for item in items]
        for item, (dq, dk, dv) in zip(items, sums):
            spare = (item & 1) * grid
            dq_acc[(item >> 8) + spare] += dq
            dk_acc[((item >> 1) & (grid - 1)) + spare] += dk
            dv_acc[((item >> 1) & (grid - 1)) + spare] += dv

    @pl.loop(0, grid)
    def _(i):
        slot = i >> 3
        rows = pl.ds(pl.multiple_of((i & (blocks - 1)) * BLOCK, BLOCK), BLOCK)
        dq_out[slot, rows, :] = dq_acc[i].astype(BF16)
        dkv_out[slot, 0, rows, :] = (dk_acc[i] * factor).astype(BF16)
        dkv_out[slot, 1, rows, :] = dv_acc[i].astype(BF16)


def reduce_kernel(
    dq_in, dkv_in, dq_own, dk_own, dv_own, dq_out, dk_out, dv_out,
    zbuf, zin, cin, csum, ybuf, yin,
    zsend, zrecv, ysend, yrecv, csend, crecv,
    *, factor,
):
    y, z, c = place()
    half = dq_out.shape[0] // 2
    zdev = [device(y, lax.rem(z + 1, NZ), c), device(y, lax.rem(z + NZ - 1, NZ), c)]
    ydev = [device(lax.rem(y + 1, NY), z, c), device(lax.rem(y + NY - 1, NY), z, c)]
    cdev = device(y, z, 1 - c)

    barrier = pltpu.get_barrier_semaphore()
    for target in zdev + ydev + [cdev]:
        pl.semaphore_signal(barrier, inc=1, device_id=target, device_id_type=MESH)
    pl.semaphore_wait(barrier, 5)

    def zparts(way, step):
        return (way,) if step == 1 else (0, 1)

    def zplain(way, step, part):
        return step == 1 or (step == 2 and part != way)

    def ztarget(way, step):
        return lax.rem(z + (5 - step if way == 0 else NZ - 5 + step), NZ)

    def zcopy(way, step, part):
        rows = pl.ds(part * half, half)
        if zplain(way, step, part):
            source = dq_in.at[ztarget(way, step), rows]
        else:
            source = zbuf.at[way, step - 1, rows]
        return pltpu.make_async_remote_copy(
            src_ref=source,
            dst_ref=zin.at[way, step - 1, rows],
            send_sem=zsend.at[way, step - 1, part],
            recv_sem=zrecv.at[way, step - 1, part],
            device_id=zdev[way],
            device_id_type=MESH,
        )

    def ccopy(offset, part):
        row = lax.rem(y + offset, NY)
        return pltpu.make_async_remote_copy(
            src_ref=dkv_in.at[row * NC + 1 - c, part],
            dst_ref=cin.at[offset, part],
            send_sem=csend.at[offset, part],
            recv_sem=crecv.at[offset, part],
            device_id=cdev,
            device_id_type=MESH,
        )

    def ycopy(way, step, part):
        return pltpu.make_async_remote_copy(
            src_ref=csum.at[2, part] if step == 1 else ybuf.at[way, part],
            dst_ref=yin.at[way, step - 1, part],
            send_sem=ysend.at[way, step - 1, part],
            recv_sem=yrecv.at[way, step - 1, part],
            device_id=ydev[way],
            device_id_type=MESH,
        )

    for offset in (2, 1, 3, 0):
        for part in (0, 1):
            ccopy(offset, part).start()
    for way in (0, 1):
        zcopy(way, 1, way).start()
        zcopy(way, 2, 1 - way).start()

    def zround(step):
        for part in (0, 1):
            for way in (0, 1):
                if part in zparts(way, step):
                    zcopy(way, step, part).wait_recv()
                    rows = pl.ds(part * half, half)
                    mine = dq_in[ztarget(way, step + 1), rows, :].astype(F32)
                    zbuf[way, step, rows, :] = (mine + zin[way, step - 1, rows, :].astype(F32)).astype(BF16)
                    zcopy(way, step + 1, part).start()

    def cadd(offset, part):
        ccopy(offset, part).wait_recv()
        row = lax.rem(y + offset, NY)
        mine = dkv_in[row * NC + c, part].astype(F32)
        return mine + cin[offset, part].astype(F32)

    for part in (0, 1):
        csum[2, part] = cadd(2, part).astype(BF16)
        ycopy(part, 1, part).start()
    zround(1)
    for way in (0, 1):
        offset = 1 if way == 0 else NY - 1
        for part in (1 - way, way):
            total = cadd(offset, part)
            if part == way:
                ycopy(way, 1, part).wait_recv()
                total = total + yin[way, 0, part].astype(F32)
            ybuf[way, part] = total.astype(BF16)
            ycopy(way, 2, part).start()
    zround(2)
    zround(3)
    for part, out in ((0, dk_out), (1, dv_out)):
        total = cadd(0, part) + (dk_own[...] * factor if part == 0 else dv_own[...])
        for way in (0, 1):
            ycopy(way, 2, part).wait_recv()
            total = total + yin[way, 1, part].astype(F32)
        out[...] = total.astype(BF16)
    for part in (0, 1):
        rows = pl.ds(part * half, half)
        total = dq_in[z, rows, :].astype(F32) + dq_own[rows, :]
        for way in (0, 1):
            zcopy(way, 4, part).wait_recv()
            total = total + zin[way, 3, rows, :].astype(F32)
        dq_out[rows, :] = total.astype(BF16)
    for way in (0, 1):
        for step in range(1, 5):
            for part in zparts(way, step):
                zcopy(way, step, part).wait_send()
        ycopy(way, 1, way).wait_send()
        for part in (0, 1):
            ycopy(way, 2, part).wait_send()
    for offset in range(NY):
        for part in (0, 1):
            ccopy(offset, part).wait_send()


def shards(queries, keys, values, outputs, d_outputs, log_norm, rand_owner, rand_local, glob_blocks):
    tokens, features = queries.shape
    blocks = tokens // BLOCK
    factor = 1.0 / math.sqrt(features // log_norm.shape[0])
    vmem = pl.BlockSpec(memory_space=pltpu.VMEM)
    smem = pl.BlockSpec(memory_space=pltpu.SMEM)
    anywhere = pl.BlockSpec(memory_space=pl.ANY)
    dma = pltpu.SemaphoreType.DMA

    side, refs, cand = pl.pallas_call(
        side_kernel,
        out_shape=(
            jax.ShapeDtypeStruct((blocks // 2, 8, BLOCK), F32),
            jax.ShapeDtypeStruct((8, BLOCK), jnp.int32),
            jax.ShapeDtypeStruct((8, BLOCK // 2, features), BF16),
        ),
        in_specs=[vmem] * 7 + [smem],
        out_specs=(vmem,) * 3,
        name="side",
    )(outputs, d_outputs, log_norm, rand_owner.T, rand_local.T, keys, values, glob_blocks)

    slices = (8, BLOCK // 2, features)
    eighths = (8, BLOCK // 16, features)
    qd, kv, nd, rf, dq_own, dk_own, dv_own, total = pl.pallas_call(
        functools.partial(gather_kernel, factor=factor),
        out_shape=(
            jax.ShapeDtypeStruct((NZ, 2, tokens, features), BF16),
            jax.ShapeDtypeStruct((NY * NC, 2, tokens, features), BF16),
            jax.ShapeDtypeStruct((NZ, blocks // 2, 8, BLOCK), F32),
            jax.ShapeDtypeStruct((NZ, 8, BLOCK), jnp.int32),
            jax.ShapeDtypeStruct((tokens, features), F32),
            jax.ShapeDtypeStruct((tokens, features), F32),
            jax.ShapeDtypeStruct((tokens, features), F32),
            jax.ShapeDtypeStruct(eighths, F32),
        ),
        in_specs=[vmem] * 7,
        out_specs=(anywhere,) * 4 + (vmem,) * 4,
        scratch_shapes=[
            pltpu.VMEM(slices, BF16), pltpu.VMEM(eighths, BF16), pltpu.VMEM(eighths, BF16),
            pltpu.VMEM(eighths[1:], BF16), pltpu.VMEM(eighths, BF16), pltpu.VMEM(eighths, BF16),
            pltpu.VMEM(slices, BF16), pltpu.VMEM(slices, F32), pltpu.VMEM(slices, F32),
            pltpu.VMEM(eighths, F32), pltpu.VMEM(eighths, F32), pltpu.VMEM(eighths[1:], F32),
            pltpu.VMEM(eighths, F32),
            dma((2, 4, 4)), dma((2, 4, 4)), dma((2, 2, 2)), dma((2, 2, 2)),
            dma((NY, 2)), dma((NY, 2)), dma((7, 8)), dma((7, 8)), dma((6,)),
        ],
        compiler_params=pltpu.CompilerParams(collective_id=0, has_side_effects=True, vmem_limit_bytes=12 * MIB),
        name="gather",
    )(queries, d_outputs, keys, values, side, refs, cand)

    dq_part, dkv_part = pl.pallas_call(
        functools.partial(pair_kernel, factor=factor),
        out_shape=(
            jax.ShapeDtypeStruct((NZ, tokens, features), BF16),
            jax.ShapeDtypeStruct((NY * NC, 2, tokens, features), BF16),
        ),
        in_specs=[smem, anywhere, anywhere, anywhere, anywhere, vmem],
        out_specs=(vmem, vmem),
        scratch_shapes=[
            pltpu.VMEM((NZ * blocks + 1, BLOCK, features), F32),
            pltpu.VMEM((NY * NC * blocks + 1, BLOCK, features), F32),
            pltpu.VMEM((NY * NC * blocks + 1, BLOCK, features), F32),
            pltpu.VMEM((NZ, 2, tokens, features), BF16),
            pltpu.VMEM((NY * NC, 2, tokens, features), BF16),
            pltpu.VMEM((NZ, blocks // 2, 8, BLOCK), F32),
            pltpu.SMEM((NZ, 8, BLOCK), jnp.int32),
            pltpu.SMEM((256,), jnp.int32),
            dma((4,)),
        ],
        compiler_params=pltpu.CompilerParams(vmem_limit_bytes=32 * MIB),
        name="pairs",
    )(glob_blocks, rf, qd, kv, nd, total)

    return tuple(pl.pallas_call(
        functools.partial(reduce_kernel, factor=factor),
        out_shape=(jax.ShapeDtypeStruct((tokens, features), BF16),) * 3,
        in_specs=[vmem] * 5,
        out_specs=(vmem,) * 3,
        scratch_shapes=[
            pltpu.VMEM((2, 4, tokens, features), BF16),
            pltpu.VMEM((2, 4, tokens, features), BF16),
            pltpu.VMEM((NY, 2, tokens, features), BF16),
            pltpu.VMEM((NY, 2, tokens, features), BF16),
            pltpu.VMEM((2, 2, tokens, features), BF16),
            pltpu.VMEM((2, 2, 2, tokens, features), BF16),
            dma((2, 4, 2)), dma((2, 4, 2)), dma((2, 2, 2)), dma((2, 2, 2)), dma((NY, 2)), dma((NY, 2)),
        ],
        compiler_params=pltpu.CompilerParams(collective_id=1, has_side_effects=True, vmem_limit_bytes=24 * MIB),
        name="reduce",
    )(dq_part, dkv_part, dq_own, dk_own, dv_own))


def solution(mesh):
    placed = (
        P("seq", "head"), P("seq", "head"), P("seq", "head"), P("seq", "head"), P("seq", "head"),
        P("head", "seq"), P("seq", None), P("seq", None), P(),
    )
    return jax.shard_map(
        shards,
        mesh=mesh,
        in_specs=placed,
        out_specs=(P("seq", "head"), P("seq", "head"), P("seq", "head")),
        check_vma=False,
    )
```

```python
import functools
import math

import jax
import jax.numpy as jnp
from jax import lax
from jax.experimental import pallas as pl
from jax.experimental.pallas import tpu as pltpu
from jax.sharding import PartitionSpec as P

BLOCK = 128
NY, NZ, NC = 4, 8, 2
MESH = pl.DeviceIdType.MESH
F32 = jnp.float32
BF16 = jnp.bfloat16
MIB = 1024 * 1024


def place():
    seq = lax.axis_index("seq")
    core = lax.rem(seq, NC)
    z = lax.rem(seq // NC, NZ)
    y = seq // (NC * NZ)
    return y, z, core


def device(y, z, core):
    return {"seq": (y * NZ + z) * NC + core}


def per_head(x):
    lane = lax.broadcasted_iota(jnp.int32, x.shape, 1)
    zero = jnp.zeros_like(x)
    low = lane < x.shape[1] // 2
    return jnp.concatenate([jnp.where(low, x, zero), jnp.where(low, zero, x)], axis=0)


def pair_terms(q2, d2, nd, k, v, factor):
    k = k * factor
    rows = k.shape[0]
    across = (((1,), (1,)), ((), ()))
    scores = lax.dot_general(k, q2, across, preferred_element_type=F32)
    grads = lax.dot_general(v, d2, across, preferred_element_type=F32)
    norm = jnp.concatenate([nd[0:1], nd[1:2]], axis=1)
    delta = jnp.concatenate([nd[2:3], nd[3:4]], axis=1)
    weights = jnp.exp(scores - norm)
    grad_scores = weights * (grads - delta)
    weights_low = weights.astype(BF16)
    scores_low = grad_scores.astype(BF16)
    dv = jnp.dot(weights_low, d2, preferred_element_type=F32)
    dk = jnp.dot(scores_low, q2, preferred_element_type=F32)
    both = jnp.concatenate([scores_low[:, :BLOCK], scores_low[:, BLOCK:]], axis=0)
    dq = lax.dot_general(both, per_head(k), (((0,), (0,)), ((), ())), preferred_element_type=F32)
    return dq, dk, dv


def query_rows(nd_tile, b):
    return jnp.where(lax.rem(b, 2) == 0, nd_tile[0:4], nd_tile[4:8])


def gather_kernel(
    q_hbm, d_hbm, k_hbm, v_hbm, o_hbm, norm_ref, owner_ref, local_ref, glob_ref,
    qd_out, kv_out, nd_out, rf_out, dq_out, dk_out, dv_out, total_out,
    q_ref, d_ref, k_ref, v_ref, o_ref, nd_ref, rf_ref, cand_ref,
    g1in, s1, g2in, s2, g3in, s3, gkv, gacc, r1in, t1, r2in, t2, r3in,
    zsend, zrecv, ysend, yrecv, csend, crecv, gsend, grecv, lsem,
    *, factor,
):
    y, z, c = place()
    tokens = q_ref.shape[0]
    blocks = tokens // BLOCK
    half = BLOCK // 2
    loads = [
        pltpu.make_async_copy(source, target, lsem.at[i])
        for i, (source, target) in enumerate(
            ((k_hbm, k_ref), (v_hbm, v_ref), (o_hbm, o_ref), (d_hbm, d_ref), (q_hbm, q_ref))
        )
    ]
    for copy in loads:
        copy.start()
    zdev = [device(y, lax.rem(z + 1, NZ), c), device(y, lax.rem(z + NZ - 1, NZ), c)]
    ydev = [device(lax.rem(y + 1, NY), z, c), device(lax.rem(y + NY - 1, NY), z, c)]
    cdev = device(y, z, 1 - c)
    me = y * NC + c

    def member(offset):
        return lax.rem(me + offset, NY * NC)

    def member_device(offset):
        other = member(offset)
        return device(other // NC, z, lax.rem(other, NC))

    def row_device(offset):
        return device(y, lax.rem(z + offset, NZ), c)

    barrier = pltpu.get_barrier_semaphore()
    for offset in range(1, 8):
        for target in (member_device(offset), row_device(offset)):
            pl.semaphore_signal(barrier, inc=1, device_id=target, device_id_type=MESH)
    pl.semaphore_wait(barrier, 14)

    def zwhere(part, slot):
        if part < 4:
            return qd_out.at[slot, part // 2, pl.ds((part % 2) * tokens // 2, tokens // 2)]
        return (nd_out, rf_out)[part - 4].at[slot]

    def zown(part):
        if part < 4:
            return (q_hbm, d_hbm)[part // 2].at[pl.ds((part % 2) * tokens // 2, tokens // 2)]
        return (nd_ref, rf_ref)[part - 4]

    def zcopy(way, step, part):
        slot = lax.rem(z + (NZ - step + 1 if way == 0 else step - 1), NZ)
        return pltpu.make_async_remote_copy(
            src_ref=zown(part) if step == 1 else zwhere(part, slot),
            dst_ref=zwhere(part, slot),
            send_sem=zsend.at[way, step - 1, part],
            recv_sem=zrecv.at[way, step - 1, part],
            device_id=zdev[way],
            device_id_type=MESH,
        )

    def zparts(way, step):
        if step < 4:
            return (0, 1, 2, 3, 4, 5)
        return (0, 1, 4, 5) if way == 0 else (2, 3)

    def ycopy(way, step, part):
        row = lax.rem(y + ((NY if step == 1 else NY - 1) if way == 0 else step - 1), NY)
        slot = row * NC + c
        return pltpu.make_async_remote_copy(
            src_ref=(k_hbm, v_hbm)[part] if step == 1 else kv_out.at[slot, part],
            dst_ref=kv_out.at[slot, part],
            send_sem=ysend.at[way, step - 1, part],
            recv_sem=yrecv.at[way, step - 1, part],
            device_id=ydev[way],
            device_id_type=MESH,
        )

    def ccopy(offset, part):
        slot = lax.rem(y + offset, NY) * NC + c
        return pltpu.make_async_remote_copy(
            src_ref=(k_hbm, v_hbm)[part] if offset == 0 else kv_out.at[slot, part],
            dst_ref=kv_out.at[slot, part],
            send_sem=csend.at[offset, part],
            recv_sem=crecv.at[offset, part],
            device_id=cdev,
            device_id_type=MESH,
        )

    def small(phase, offset):
        over_column = phase in (0, 3, 4)
        other = member(offset) if over_column else lax.rem(z + offset, NZ)
        source, target = (
            (cand_ref.at[other], g1in.at[offset]),
            (s1.at[other], g2in.at[offset]),
            (s2, g3in.at[offset]),
            (gkv.at[me], gkv.at[me]),
            (gacc.at[other], r1in.at[offset]),
            (t1.at[other], r2in.at[offset]),
            (t2, r3in.at[offset]),
        )[phase]
        return pltpu.make_async_remote_copy(
            src_ref=source,
            dst_ref=target,
            send_sem=gsend.at[phase, offset],
            recv_sem=grecv.at[phase, offset],
            device_id=member_device(offset) if over_column else row_device(offset),
            device_id_type=MESH,
        )

    def small_start(phase):
        for offset in range(1, 8):
            small(phase, offset).start()

    def small_wait(phase):
        for offset in range(1, 8):
            small(phase, offset).wait_recv()

    def zstart(step, parts):
        for part in parts:
            for way in (0, 1):
                if part in zparts(way, step):
                    zcopy(way, step, part).start()

    def zpass(step, parts):
        for part in parts:
            for way in (0, 1):
                if part in zparts(way, step):
                    zcopy(way, step, part).wait_recv()
                    if step < 4 and part in zparts(way, step + 1):
                        zcopy(way, step + 1, part).start()

    def block_rows(b):
        return pl.ds(pl.multiple_of(b * BLOCK, BLOCK), BLOCK)

    def window(first, end):
        @pl.loop(first, end)
        def _(i):
            up = (i >= blocks).astype(jnp.int32)
            down = (i >= 2 * blocks - 1).astype(jnp.int32)
            low = i - up * blocks - down * (blocks - 1)
            qb = low + down
            kb = low + up - down
            rows, krows = block_rows(qb), block_rows(kb)
            dq, dk, dv = pair_terms(
                per_head(q_ref[rows, :]), per_head(d_ref[rows, :]), query_rows(nd_ref[qb // 2], qb),
                k_ref[krows, :], v_ref[krows, :], factor,
            )
            dq_out[rows, :] += dq
            dk_out[krows, :] += dk
            dv_out[krows, :] += dv

    def whole(first, end):
        @pl.loop(first, end)
        def _(i):
            b, g = i // 2, lax.rem(i, 2)
            rows = block_rows(b)
            part = 4 * g
            dq, dk, dv = pair_terms(
                per_head(q_ref[rows, :]), per_head(d_ref[rows, :]), query_rows(nd_ref[b // 2], b),
                jnp.concatenate([gkv[part], gkv[part + 1]], axis=0),
                jnp.concatenate([gkv[part + 2], gkv[part + 3]], axis=0),
                factor,
            )
            dq_out[rows, :] += dq
            gacc[part] += dk[:half]
            gacc[part + 1] += dk[half:]
            gacc[part + 2] += dv[:half]
            gacc[part + 3] += dv[half:]

    def ystep1(part):
        for way in (0, 1):
            ycopy(way, 1, part).wait_recv()
            if part == way:
                ycopy(way, 2, part).start()
            ccopy(NY - 1 if way == 0 else 1, part).start()

    zstart(1, (0,))
    loads[0].wait()
    loads[1].wait()
    seq = lax.axis_index("seq")
    for g in range(2):
        local_block = glob_ref[g] - seq * blocks
        for i, ref in enumerate((k_ref, v_ref)):
            block = jnp.zeros((BLOCK, k_ref.shape[1]), BF16)
            for b in range(blocks):
                block = jnp.where(local_block == b, ref[pl.ds(b * BLOCK, BLOCK), :], block)
            cand_ref[4 * g + 2 * i] = block[:half]
            cand_ref[4 * g + 2 * i + 1] = block[half:]
    owner = owner_ref[...]
    column = jnp.bitwise_and(owner >> 1, NZ - 1)
    other = (owner >> 4) * NC + jnp.bitwise_and(owner, 1)
    rf_ref[...] = jnp.zeros(rf_ref.shape, jnp.int32)
    rf_ref[0:3, 0:blocks] = (column * (NY * NC) + other) * blocks + local_ref[...]
    loads[2].wait()
    loads[3].wait()

    def row_values(b):
        rows = pl.ds(b * BLOCK, BLOCK)
        turned = (o_ref[rows, :].astype(F32) * d_ref[rows, :].astype(F32)).T
        nd_ref[b // 2, 4 * (b % 2) : 4 * (b % 2) + 4, :] = jnp.concatenate(
            [
                norm_ref[:, rows],
                jnp.sum(turned[: turned.shape[0] // 2], axis=0, keepdims=True),
                jnp.sum(turned[turned.shape[0] // 2 :], axis=0, keepdims=True),
            ],
            axis=0,
        )

    row_values(0)
    small_start(0)
    zstart(1, (1,))
    for b in range(1, blocks):
        row_values(b)
    loads[4].wait()
    local = [
        pltpu.make_async_copy(q_ref, qd_out.at[z, 0], lsem.at[5]),
        pltpu.make_async_copy(d_ref, qd_out.at[z, 1], lsem.at[6]),
        pltpu.make_async_copy(nd_ref, nd_out.at[z], lsem.at[7]),
        pltpu.make_async_copy(rf_ref, rf_out.at[z], lsem.at[8]),
        pltpu.make_async_copy(k_ref, kv_out.at[me, 0], lsem.at[9]),
        pltpu.make_async_copy(v_ref, kv_out.at[me, 1], lsem.at[10]),
    ]
    for copy in local:
        copy.start()

    @pl.loop(0, blocks)
    def _(b):
        zero = jnp.zeros((BLOCK, q_ref.shape[1]), F32)
        dq_out[block_rows(b), :] = zero
        dk_out[block_rows(b), :] = zero
        dv_out[block_rows(b), :] = zero
        gacc[b] = zero[:half]

    small_wait(0)
    slice_sum = cand_ref[me].astype(F32)
    for offset in range(1, 8):
        slice_sum = slice_sum + g1in[offset].astype(F32)
    s1[...] = slice_sum.astype(BF16).reshape(s1.shape)
    window(0, 2)
    small_start(1)
    zstart(1, (4, 5, 2, 3))
    window(2, 4)
    zpass(1, (0,))
    window(4, 5)
    small_wait(1)
    part_sum = s1[z].astype(F32)
    for offset in range(1, 8):
        part_sum = part_sum + g2in[offset].astype(F32)
    s2[...] = part_sum.astype(BF16)
    window(5, 6)
    small_start(2)
    zpass(1, (1, 4, 5))
    window(6, 9)
    zpass(1, (2,))
    small_wait(2)
    s3[z] = s2[...]
    for offset in range(1, 8):
        s3[lax.rem(z + NZ - offset, NZ)] = g3in[offset]
    gkv[me] = s3[...].reshape(gkv.shape[1:])
    window(9, 11)
    small_start(3)
    for part in (0, 1):
        for way in (0, 1):
            ycopy(way, 1, part).start()
        ccopy(0, part).start()
    zpass(1, (3,))
    window(11, 14)
    zpass(2, (0,))
    small_wait(3)
    whole(0, 4)
    zpass(2, (1, 4, 5))
    whole(4, 8)
    zpass(2, (2,))
    whole(8, 12)
    zpass(2, (3,))
    whole(12, 16)
    window(14, 15)
    ystep1(0)
    small_start(4)
    zpass(3, (0,))
    window(15, 17)
    ystep1(1)
    small_wait(4)
    slice_sum = gacc[me]
    for offset in range(1, 8):
        slice_sum = slice_sum + r1in[offset]
    t1[...] = slice_sum.reshape(t1.shape)
    window(17, 19)
    small_start(5)
    zpass(3, (1, 4, 5))
    window(19, 22)
    zpass(3, (2,))
    small_wait(5)
    part_sum = t1[z]
    for offset in range(1, 8):
        part_sum = part_sum + r2in[offset]
    t2[...] = part_sum
    for way in (0, 1):
        ycopy(way, 2, way).wait_recv()
        ccopy(2, way).start()
    small_start(6)
    zpass(3, (3,))
    small_wait(6)
    total_out[z] = t2[...]
    for offset in range(1, 8):
        total_out[lax.rem(z + NZ - offset, NZ)] = r3in[offset]
    zpass(4, (0, 1, 4, 5, 2, 3))
    for offset in range(NY):
        for part in (0, 1):
            ccopy(offset, part).wait()
    for way in (0, 1):
        for step in range(1, 5):
            for part in zparts(way, step):
                zcopy(way, step, part).wait_send()
        for part in (0, 1):
            ycopy(way, 1, part).wait_send()
        ycopy(way, 2, way).wait_send()
    for phase in range(7):
        for offset in range(1, 8):
            small(phase, offset).wait_send()
    for copy in local:
        copy.wait()


def pair_kernel(
    glob_hbm, rf_any, qd_ref, kv_ref, nd_ref, total_ref, dq_out, dkv_out,
    dq_acc, dk_acc, dv_acc, glob_ref, rf_ref, list_ref, sem,
    *, factor,
):
    y, z, c = place()
    blocks = qd_ref.shape[2] // BLOCK
    grid = NZ * blocks
    copies = [
        pltpu.make_async_copy(rf_any, rf_ref, sem.at[0]),
        pltpu.make_async_copy(glob_hbm, glob_ref, sem.at[1]),
    ]
    for copy in copies:
        copy.start()

    @pl.loop(0, grid)
    def _(i):
        zero = jnp.zeros((BLOCK, qd_ref.shape[3]), F32)
        dq_acc[i] = zero
        dk_acc[i] = zero
        dv_acc[i] = zero

    copies[1].wait()
    half = BLOCK // 2
    for g in range(2):
        owner = glob_ref[g] // blocks
        column = lax.rem(owner // NC, NZ)
        member = (owner // (NC * NZ)) * NC + lax.rem(owner, NC)
        slot = member * blocks + lax.rem(glob_ref[g], blocks)
        mine = jnp.logical_and(column == z, (y * NC + c) // 4 == g)
        total = total_ref[...].reshape(half, total_ref.shape[2])
        rows = pl.ds(pl.multiple_of(c * half, half), half)

        @pl.when(jnp.logical_and(mine, lax.rem(y, 2) == 0))
        def _():
            dk_acc[slot, rows, :] += total

        @pl.when(jnp.logical_and(mine, lax.rem(y, 2) == 1))
        def _():
            dv_acc[slot, rows, :] += total

    def window_item(n, slot, b, seq, key_block, wanted):
        member = (seq // (NC * NZ)) * NC + lax.rem(seq, NC)
        list_ref[n] = ((slot * blocks + b) << 8) | ((member * blocks + key_block) << 1)
        return n + wanted.astype(jnp.int32)

    seq = (y * NZ + z) * NC + c
    nearby = jnp.where(c == 0, seq + 1, seq - 1)
    count = window_item(
        jnp.int32(0), z, jnp.where(c == 0, blocks - 1, 0), nearby, jnp.where(c == 0, 0, blocks - 1), seq >= 0
    )
    far_slot = jnp.where(c == 0, lax.rem(z + 1, NZ), lax.rem(z + NZ - 1, NZ))
    far_seq = (y * NZ + far_slot) * NC + c
    far_key = jnp.where(c == 0, far_seq - 1, far_seq + 1)
    inside = jnp.logical_and(far_key >= 0, far_key < NY * NZ * NC)
    count = window_item(
        count, far_slot, jnp.where(c == 0, 0, blocks - 1),
        jnp.clip(far_key, 0, NY * NZ * NC - 1), jnp.where(c == 0, blocks - 1, 0), inside,
    )

    copies[0].wait()

    def per_slot(slot, n):
        for b in range(blocks):
            for r in range(3):
                code = rf_ref[slot, r, b]
                list_ref[n] = ((slot * blocks + b) << 8) | ((code & (grid - 1)) << 1)
                n = n + ((code >> 6) == z).astype(jnp.int32)
        return n

    count = lax.fori_loop(0, NZ, per_slot, count)
    list_ref[count] = jnp.int32(1)

    def terms(item):
        query, key = item >> 8, (item >> 1) & (grid - 1)
        qs, qb = query >> 3, query & (blocks - 1)
        ks, kb = key >> 3, key & (blocks - 1)
        qrows = pl.ds(pl.multiple_of(qb * BLOCK, BLOCK), BLOCK)
        krows = pl.ds(pl.multiple_of(kb * BLOCK, BLOCK), BLOCK)
        return pair_terms(
            per_head(qd_ref[qs, 0, qrows, :]),
            per_head(qd_ref[qs, 1, qrows, :]),
            query_rows(nd_ref[qs, qb >> 1], qb),
            kv_ref[ks, 0, krows, :],
            kv_ref[ks, 1, krows, :],
            factor,
        )

    @pl.loop(0, (count + 1) // 2)
    def _(i):
        items = [list_ref[2 * i], list_ref[2 * i + 1]]
        sums = [terms(item) for item in items]
        for item, (dq, dk, dv) in zip(items, sums):
            spare = (item & 1) * grid
            dq_acc[(item >> 8) + spare] += dq
            dk_acc[((item >> 1) & (grid - 1)) + spare] += dk
            dv_acc[((item >> 1) & (grid - 1)) + spare] += dv

    @pl.loop(0, grid)
    def _(i):
        slot = i >> 3
        rows = pl.ds(pl.multiple_of((i & (blocks - 1)) * BLOCK, BLOCK), BLOCK)
        dq_out[slot, rows, :] = dq_acc[i].astype(BF16)
        dkv_out[slot, 0, rows, :] = (dk_acc[i] * factor).astype(BF16)
        dkv_out[slot, 1, rows, :] = dv_acc[i].astype(BF16)


def reduce_kernel(
    dq_in, dkv_in, dq_own, dk_own, dv_own, dq_out, dk_out, dv_out,
    zbuf, zin, cin, csum, ybuf, yin,
    zsend, zrecv, ysend, yrecv, csend, crecv,
    *, factor,
):
    y, z, c = place()
    half = dq_out.shape[0] // 2
    zdev = [device(y, lax.rem(z + 1, NZ), c), device(y, lax.rem(z + NZ - 1, NZ), c)]
    ydev = [device(lax.rem(y + 1, NY), z, c), device(lax.rem(y + NY - 1, NY), z, c)]
    cdev = device(y, z, 1 - c)

    barrier = pltpu.get_barrier_semaphore()
    for target in zdev + ydev + [cdev]:
        pl.semaphore_signal(barrier, inc=1, device_id=target, device_id_type=MESH)
    pl.semaphore_wait(barrier, 5)

    def zparts(way, step):
        return (way,) if step == 1 else (0, 1)

    def zplain(way, step, part):
        return step == 1 or (step == 2 and part != way)

    def ztarget(way, step):
        return lax.rem(z + (5 - step if way == 0 else NZ - 5 + step), NZ)

    def zcopy(way, step, part):
        rows = pl.ds(part * half, half)
        if zplain(way, step, part):
            source = dq_in.at[ztarget(way, step), rows]
        else:
            source = zbuf.at[way, step - 1, rows]
        return pltpu.make_async_remote_copy(
            src_ref=source,
            dst_ref=zin.at[way, step - 1, rows],
            send_sem=zsend.at[way, step - 1, part],
            recv_sem=zrecv.at[way, step - 1, part],
            device_id=zdev[way],
            device_id_type=MESH,
        )

    def ccopy(offset, part):
        row = lax.rem(y + offset, NY)
        return pltpu.make_async_remote_copy(
            src_ref=dkv_in.at[row * NC + 1 - c, part],
            dst_ref=cin.at[offset, part],
            send_sem=csend.at[offset, part],
            recv_sem=crecv.at[offset, part],
            device_id=cdev,
            device_id_type=MESH,
        )

    def ycopy(way, step, part):
        return pltpu.make_async_remote_copy(
            src_ref=csum.at[2, part] if step == 1 else ybuf.at[way, part],
            dst_ref=yin.at[way, step - 1, part],
            send_sem=ysend.at[way, step - 1, part],
            recv_sem=yrecv.at[way, step - 1, part],
            device_id=ydev[way],
            device_id_type=MESH,
        )

    for offset in (2, 1, 3, 0):
        for part in (0, 1):
            ccopy(offset, part).start()
    for way in (0, 1):
        zcopy(way, 1, way).start()
        zcopy(way, 2, 1 - way).start()

    def zround(step):
        for part in (0, 1):
            for way in (0, 1):
                if part in zparts(way, step):
                    zcopy(way, step, part).wait_recv()
                    rows = pl.ds(part * half, half)
                    mine = dq_in[ztarget(way, step + 1), rows, :].astype(F32)
                    zbuf[way, step, rows, :] = (mine + zin[way, step - 1, rows, :].astype(F32)).astype(BF16)
                    zcopy(way, step + 1, part).start()

    def cadd(offset, part):
        ccopy(offset, part).wait_recv()
        row = lax.rem(y + offset, NY)
        mine = dkv_in[row * NC + c, part].astype(F32)
        return mine + cin[offset, part].astype(F32)

    for part in (0, 1):
        csum[2, part] = cadd(2, part).astype(BF16)
        ycopy(part, 1, part).start()
    zround(1)
    for way in (0, 1):
        offset = 1 if way == 0 else NY - 1
        for part in (1 - way, way):
            total = cadd(offset, part)
            if part == way:
                ycopy(way, 1, part).wait_recv()
                total = total + yin[way, 0, part].astype(F32)
            ybuf[way, part] = total.astype(BF16)
            ycopy(way, 2, part).start()
    zround(2)
    zround(3)
    for part, out in ((0, dk_out), (1, dv_out)):
        total = cadd(0, part) + (dk_own[...] * factor if part == 0 else dv_own[...])
        for way in (0, 1):
            ycopy(way, 2, part).wait_recv()
            total = total + yin[way, 1, part].astype(F32)
        out[...] = total.astype(BF16)
    for part in (0, 1):
        rows = pl.ds(part * half, half)
        total = dq_in[z, rows, :].astype(F32) + dq_own[rows, :]
        for way in (0, 1):
            zcopy(way, 4, part).wait_recv()
            total = total + zin[way, 3, rows, :].astype(F32)
        dq_out[rows, :] = total.astype(BF16)
    for way in (0, 1):
        for step in range(1, 5):
            for part in zparts(way, step):
                zcopy(way, step, part).wait_send()
        ycopy(way, 1, way).wait_send()
        for part in (0, 1):
            ycopy(way, 2, part).wait_send()
    for offset in range(NY):
        for part in (0, 1):
            ccopy(offset, part).wait_send()


def shards(queries, keys, values, outputs, d_outputs, log_norm, rand_owner, rand_local, glob_blocks):
    tokens, features = queries.shape
    blocks = tokens // BLOCK
    factor = 1.0 / math.sqrt(features // log_norm.shape[0])
    queries, keys, values, outputs, d_outputs, log_norm, owner, local, glob_blocks = (
        pltpu.with_memory_space_constraint(array, pltpu.HBM)
        for array in (
            queries, keys, values, outputs, d_outputs, log_norm, rand_owner.T, rand_local.T, glob_blocks
        )
    )
    vmem = pl.BlockSpec(memory_space=pltpu.VMEM)
    smem = pl.BlockSpec(memory_space=pltpu.SMEM)
    anywhere = pl.BlockSpec(memory_space=pl.ANY)
    hbm = pl.BlockSpec(memory_space=pltpu.HBM)
    dma = pltpu.SemaphoreType.DMA

    slices = (8, BLOCK // 2, features)
    eighths = (8, BLOCK // 16, features)
    qd, kv, nd, rf, dq_own, dk_own, dv_own, total = pl.pallas_call(
        functools.partial(gather_kernel, factor=factor),
        out_shape=(
            jax.ShapeDtypeStruct((NZ, 2, tokens, features), BF16),
            jax.ShapeDtypeStruct((NY * NC, 2, tokens, features), BF16),
            jax.ShapeDtypeStruct((NZ, blocks // 2, 8, BLOCK), F32),
            jax.ShapeDtypeStruct((NZ, 8, BLOCK), jnp.int32),
            jax.ShapeDtypeStruct((tokens, features), F32),
            jax.ShapeDtypeStruct((tokens, features), F32),
            jax.ShapeDtypeStruct((tokens, features), F32),
            jax.ShapeDtypeStruct(eighths, F32),
        ),
        in_specs=[hbm] * 5 + [vmem] * 3 + [smem],
        out_specs=(anywhere,) * 4 + (vmem,) * 4,
        scratch_shapes=[
            pltpu.VMEM((tokens, features), BF16), pltpu.VMEM((tokens, features), BF16),
            pltpu.VMEM((tokens, features), BF16), pltpu.VMEM((tokens, features), BF16),
            pltpu.VMEM((tokens, features), BF16),
            pltpu.VMEM((blocks // 2, 8, BLOCK), F32), pltpu.VMEM((8, BLOCK), jnp.int32), pltpu.VMEM(slices, BF16),
            pltpu.VMEM(slices, BF16), pltpu.VMEM(eighths, BF16), pltpu.VMEM(eighths, BF16),
            pltpu.VMEM(eighths[1:], BF16), pltpu.VMEM(eighths, BF16), pltpu.VMEM(eighths, BF16),
            pltpu.VMEM(slices, BF16), pltpu.VMEM(slices, F32), pltpu.VMEM(slices, F32),
            pltpu.VMEM(eighths, F32), pltpu.VMEM(eighths, F32), pltpu.VMEM(eighths[1:], F32),
            pltpu.VMEM(eighths, F32),
            dma((2, 4, 6)), dma((2, 4, 6)), dma((2, 2, 2)), dma((2, 2, 2)),
            dma((NY, 2)), dma((NY, 2)), dma((7, 8)), dma((7, 8)), dma((11,)),
        ],
        compiler_params=pltpu.CompilerParams(collective_id=0, has_side_effects=True, vmem_limit_bytes=12 * MIB),
        name="gather",
    )(queries, d_outputs, keys, values, outputs, log_norm, owner, local, glob_blocks)

    dq_part, dkv_part = pl.pallas_call(
        functools.partial(pair_kernel, factor=factor),
        out_shape=(
            jax.ShapeDtypeStruct((NZ, tokens, features), BF16),
            jax.ShapeDtypeStruct((NY * NC, 2, tokens, features), BF16),
        ),
        in_specs=[hbm, anywhere, vmem, vmem, vmem, vmem],
        out_specs=(vmem, vmem),
        scratch_shapes=[
            pltpu.VMEM((NZ * blocks + 1, BLOCK, features), F32),
            pltpu.VMEM((NY * NC * blocks + 1, BLOCK, features), F32),
            pltpu.VMEM((NY * NC * blocks + 1, BLOCK, features), F32),
            pltpu.SMEM((2,), jnp.int32),
            pltpu.SMEM((NZ, 8, BLOCK), jnp.int32),
            pltpu.SMEM((256,), jnp.int32),
            dma((2,)),
        ],
        compiler_params=pltpu.CompilerParams(vmem_limit_bytes=16 * MIB),
        name="pairs",
    )(glob_blocks, rf, qd, kv, nd, total)

    return tuple(pl.pallas_call(
        functools.partial(reduce_kernel, factor=factor),
        out_shape=(jax.ShapeDtypeStruct((tokens, features), BF16),) * 3,
        in_specs=[vmem] * 5,
        out_specs=(vmem,) * 3,
        scratch_shapes=[
            pltpu.VMEM((2, 4, tokens, features), BF16),
            pltpu.VMEM((2, 4, tokens, features), BF16),
            pltpu.VMEM((NY, 2, tokens, features), BF16),
            pltpu.VMEM((NY, 2, tokens, features), BF16),
            pltpu.VMEM((2, 2, tokens, features), BF16),
            pltpu.VMEM((2, 2, 2, tokens, features), BF16),
            dma((2, 4, 2)), dma((2, 4, 2)), dma((2, 2, 2)), dma((2, 2, 2)), dma((NY, 2)), dma((NY, 2)),
        ],
        compiler_params=pltpu.CompilerParams(collective_id=1, has_side_effects=True, vmem_limit_bytes=24 * MIB),
        name="reduce",
    )(dq_part, dkv_part, dq_own, dk_own, dv_own))


def solution(mesh):
    placed = (
        P("seq", "head"), P("seq", "head"), P("seq", "head"), P("seq", "head"), P("seq", "head"),
        P("head", "seq"), P("seq", None), P("seq", None), P(),
    )
    return jax.shard_map(
        shards,
        mesh=mesh,
        in_specs=placed,
        out_specs=(P("seq", "head"), P("seq", "head"), P("seq", "head")),
        check_vma=False,
    )
```

```python
import functools
import math

import jax
import jax.numpy as jnp
from jax import lax
from jax.experimental import pallas as pl
from jax.experimental.pallas import tpu as pltpu
from jax.sharding import PartitionSpec as P

BLOCK = 128
NY, NZ, NC = 4, 8, 2
MESH = pl.DeviceIdType.MESH
F32 = jnp.float32
BF16 = jnp.bfloat16
MIB = 1024 * 1024


def place():
    seq = lax.axis_index("seq")
    core = lax.rem(seq, NC)
    z = lax.rem(seq // NC, NZ)
    y = seq // (NC * NZ)
    return y, z, core


def device(y, z, core):
    return {"seq": (y * NZ + z) * NC + core}


def per_head(x):
    lane = lax.broadcasted_iota(jnp.int32, x.shape, 1)
    zero = jnp.zeros_like(x)
    low = lane < x.shape[1] // 2
    return jnp.concatenate([jnp.where(low, x, zero), jnp.where(low, zero, x)], axis=0)


def pair_terms(q2, d2, nd, k, v, factor):
    k = k * factor
    rows = k.shape[0]
    across = (((1,), (1,)), ((), ()))
    scores = lax.dot_general(k, q2, across, preferred_element_type=F32)
    grads = lax.dot_general(v, d2, across, preferred_element_type=F32)
    norm = jnp.concatenate([nd[0:1], nd[1:2]], axis=1)
    delta = jnp.concatenate([nd[2:3], nd[3:4]], axis=1)
    weights = jnp.exp(scores - norm)
    grad_scores = weights * (grads - delta)
    weights_low = weights.astype(BF16)
    scores_low = grad_scores.astype(BF16)
    dv = jnp.dot(weights_low, d2, preferred_element_type=F32)
    dk = jnp.dot(scores_low, q2, preferred_element_type=F32)
    both = jnp.concatenate([scores_low[:, :BLOCK], scores_low[:, BLOCK:]], axis=0)
    dq = lax.dot_general(both, per_head(k), (((0,), (0,)), ((), ())), preferred_element_type=F32)
    return dq, dk, dv


def query_rows(nd_tile, b):
    return jnp.where(lax.rem(b, 2) == 0, nd_tile[0:4], nd_tile[4:8])


def gather_kernel(
    q_hbm, d_hbm, k_hbm, v_hbm, o_hbm, norm_ref, owner_ref, local_ref, glob_ref,
    qd_out, kv_out, nd_out, rf_out, dq_out, dk_out, dv_out, part_out,
    q_ref, d_ref, k_ref, v_ref, o_ref, nd_ref, rf_ref, cand_ref,
    g1in, s1, g2in, s2, g3in, s3, gkv, gacc, r1in, t1, r2in,
    zsend, zrecv, ysend, yrecv, csend, crecv, gsend, grecv, lsem,
    *, factor,
):
    y, z, c = place()
    tokens = q_ref.shape[0]
    blocks = tokens // BLOCK
    half = BLOCK // 2
    loads = [
        pltpu.make_async_copy(source, target, lsem.at[i])
        for i, (source, target) in enumerate(
            ((k_hbm, k_ref), (v_hbm, v_ref), (o_hbm, o_ref), (d_hbm, d_ref), (q_hbm, q_ref))
        )
    ]
    for copy in loads:
        copy.start()
    zdev = [device(y, lax.rem(z + 1, NZ), c), device(y, lax.rem(z + NZ - 1, NZ), c)]
    ydev = [device(lax.rem(y + 1, NY), z, c), device(lax.rem(y + NY - 1, NY), z, c)]
    cdev = device(y, z, 1 - c)
    me = y * NC + c

    def member(offset):
        return lax.rem(me + offset, NY * NC)

    def member_device(offset):
        other = member(offset)
        return device(other // NC, z, lax.rem(other, NC))

    def row_device(offset):
        return device(y, lax.rem(z + offset, NZ), c)

    barrier = pltpu.get_barrier_semaphore()
    for offset in range(1, 8):
        for target in (member_device(offset), row_device(offset)):
            pl.semaphore_signal(barrier, inc=1, device_id=target, device_id_type=MESH)
    pl.semaphore_wait(barrier, 14)

    def zwhere(part, slot):
        if part < 4:
            return qd_out.at[slot, part // 2, pl.ds((part % 2) * tokens // 2, tokens // 2)]
        return (nd_out, rf_out)[part - 4].at[slot]

    def zown(part):
        if part < 4:
            return (q_hbm, d_hbm)[part // 2].at[pl.ds((part % 2) * tokens // 2, tokens // 2)]
        return (nd_ref, rf_ref)[part - 4]

    def zcopy(way, step, part):
        slot = lax.rem(z + (NZ - step + 1 if way == 0 else step - 1), NZ)
        return pltpu.make_async_remote_copy(
            src_ref=zown(part) if step == 1 else zwhere(part, slot),
            dst_ref=zwhere(part, slot),
            send_sem=zsend.at[way, step - 1, part],
            recv_sem=zrecv.at[way, step - 1, part],
            device_id=zdev[way],
            device_id_type=MESH,
        )

    def zparts(way, step):
        if step < 4:
            return (0, 1, 2, 3, 4, 5)
        return (0, 1, 4, 5) if way == 0 else (2, 3)

    def ycopy(way, step, part):
        row = lax.rem(y + ((NY if step == 1 else NY - 1) if way == 0 else step - 1), NY)
        slot = row * NC + c
        return pltpu.make_async_remote_copy(
            src_ref=(k_hbm, v_hbm)[part] if step == 1 else kv_out.at[slot, part],
            dst_ref=kv_out.at[slot, part],
            send_sem=ysend.at[way, step - 1, part],
            recv_sem=yrecv.at[way, step - 1, part],
            device_id=ydev[way],
            device_id_type=MESH,
        )

    def ccopy(offset, part):
        slot = lax.rem(y + offset, NY) * NC + c
        return pltpu.make_async_remote_copy(
            src_ref=(k_hbm, v_hbm)[part] if offset == 0 else kv_out.at[slot, part],
            dst_ref=kv_out.at[slot, part],
            send_sem=csend.at[offset, part],
            recv_sem=crecv.at[offset, part],
            device_id=cdev,
            device_id_type=MESH,
        )

    def small(phase, offset):
        over_column = phase in (0, 3, 4)
        other = member(offset) if over_column else lax.rem(z + offset, NZ)
        source, target = (
            (cand_ref.at[other], g1in.at[offset]),
            (s1.at[other], g2in.at[offset]),
            (s2, g3in.at[offset]),
            (gkv.at[me], gkv.at[me]),
            (gacc.at[other], r1in.at[offset]),
            (t1.at[other], r2in.at[offset]),
        )[phase]
        return pltpu.make_async_remote_copy(
            src_ref=source,
            dst_ref=target,
            send_sem=gsend.at[phase, offset],
            recv_sem=grecv.at[phase, offset],
            device_id=member_device(offset) if over_column else row_device(offset),
            device_id_type=MESH,
        )

    def small_start(phase):
        for offset in range(1, 8):
            small(phase, offset).start()

    def small_wait(phase):
        for offset in range(1, 8):
            small(phase, offset).wait_recv()

    def zstart(step, parts):
        for part in parts:
            for way in (0, 1):
                if part in zparts(way, step):
                    zcopy(way, step, part).start()

    def zpass(step, parts):
        for part in parts:
            for way in (0, 1):
                if part in zparts(way, step):
                    zcopy(way, step, part).wait_recv()
                    if step < 4 and part in zparts(way, step + 1):
                        zcopy(way, step + 1, part).start()

    def block_rows(b):
        return pl.ds(pl.multiple_of(b * BLOCK, BLOCK), BLOCK)

    def window(first, end):
        @pl.loop(first, end)
        def _(i):
            up = (i >= blocks).astype(jnp.int32)
            down = (i >= 2 * blocks - 1).astype(jnp.int32)
            low = i - up * blocks - down * (blocks - 1)
            qb = low + down
            kb = low + up - down
            rows, krows = block_rows(qb), block_rows(kb)
            dq, dk, dv = pair_terms(
                per_head(q_ref[rows, :]), per_head(d_ref[rows, :]), query_rows(nd_ref[qb // 2], qb),
                k_ref[krows, :], v_ref[krows, :], factor,
            )
            dq_out[rows, :] += dq
            dk_out[krows, :] += dk
            dv_out[krows, :] += dv

    def whole(first, end):
        @pl.loop(first, end)
        def _(i):
            b, g = i // 2, lax.rem(i, 2)
            rows = block_rows(b)
            part = 4 * g
            dq, dk, dv = pair_terms(
                per_head(q_ref[rows, :]), per_head(d_ref[rows, :]), query_rows(nd_ref[b // 2], b),
                jnp.concatenate([gkv[part], gkv[part + 1]], axis=0),
                jnp.concatenate([gkv[part + 2], gkv[part + 3]], axis=0),
                factor,
            )
            dq_out[rows, :] += dq
            gacc[part] += dk[:half]
            gacc[part + 1] += dk[half:]
            gacc[part + 2] += dv[:half]
            gacc[part + 3] += dv[half:]

    def ystep1(part):
        for way in (0, 1):
            ycopy(way, 1, part).wait_recv()
            if part == way:
                ycopy(way, 2, part).start()
            ccopy(NY - 1 if way == 0 else 1, part).start()

    zstart(1, (0,))
    loads[0].wait()
    loads[1].wait()
    seq = lax.axis_index("seq")
    for g in range(2):
        local_block = glob_ref[g] - seq * blocks
        for i, ref in enumerate((k_ref, v_ref)):
            block = jnp.zeros((BLOCK, k_ref.shape[1]), BF16)
            for b in range(blocks):
                block = jnp.where(local_block == b, ref[pl.ds(b * BLOCK, BLOCK), :], block)
            cand_ref[4 * g + 2 * i] = block[:half]
            cand_ref[4 * g + 2 * i + 1] = block[half:]
    owner = owner_ref[...]
    column = jnp.bitwise_and(owner >> 1, NZ - 1)
    other = (owner >> 4) * NC + jnp.bitwise_and(owner, 1)
    rf_ref[...] = jnp.zeros(rf_ref.shape, jnp.int32)
    rf_ref[0:3, 0:blocks] = (column * (NY * NC) + other) * blocks + local_ref[...]
    loads[2].wait()
    loads[3].wait()

    def row_values(b):
        rows = pl.ds(b * BLOCK, BLOCK)
        turned = (o_ref[rows, :].astype(F32) * d_ref[rows, :].astype(F32)).T
        nd_ref[b // 2, 4 * (b % 2) : 4 * (b % 2) + 4, :] = jnp.concatenate(
            [
                norm_ref[:, rows],
                jnp.sum(turned[: turned.shape[0] // 2], axis=0, keepdims=True),
                jnp.sum(turned[turned.shape[0] // 2 :], axis=0, keepdims=True),
            ],
            axis=0,
        )

    row_values(0)
    small_start(0)
    zstart(1, (1,))
    for part in (0, 1):
        for way in (0, 1):
            ycopy(way, 1, part).start()
        ccopy(0, part).start()
    for b in range(1, blocks):
        row_values(b)
    loads[4].wait()
    local = [
        pltpu.make_async_copy(q_ref, qd_out.at[z, 0], lsem.at[5]),
        pltpu.make_async_copy(d_ref, qd_out.at[z, 1], lsem.at[6]),
        pltpu.make_async_copy(nd_ref, nd_out.at[z], lsem.at[7]),
        pltpu.make_async_copy(rf_ref, rf_out.at[z], lsem.at[8]),
        pltpu.make_async_copy(k_ref, kv_out.at[me, 0], lsem.at[9]),
        pltpu.make_async_copy(v_ref, kv_out.at[me, 1], lsem.at[10]),
    ]
    for copy in local:
        copy.start()

    @pl.loop(0, blocks)
    def _(b):
        zero = jnp.zeros((BLOCK, q_ref.shape[1]), F32)
        dq_out[block_rows(b), :] = zero
        dk_out[block_rows(b), :] = zero
        dv_out[block_rows(b), :] = zero
        gacc[b] = zero[:half]

    small_wait(0)
    slice_sum = cand_ref[me].astype(F32)
    for offset in range(1, 8):
        slice_sum = slice_sum + g1in[offset].astype(F32)
    s1[...] = slice_sum.astype(BF16).reshape(s1.shape)
    window(0, 2)
    small_start(1)
    zstart(1, (4, 5, 2, 3))
    window(2, 4)
    zpass(1, (0,))
    window(4, 5)
    small_wait(1)
    part_sum = s1[z].astype(F32)
    for offset in range(1, 8):
        part_sum = part_sum + g2in[offset].astype(F32)
    s2[...] = part_sum.astype(BF16)
    window(5, 6)
    small_start(2)
    zpass(1, (1, 4, 5))
    ystep1(0)
    window(6, 9)
    zpass(1, (2,))
    window(9, 10)
    zpass(1, (3,))
    ystep1(1)
    window(10, 11)
    zpass(2, (0,))
    small_wait(2)
    s3[z] = s2[...]
    for offset in range(1, 8):
        s3[lax.rem(z + NZ - offset, NZ)] = g3in[offset]
    gkv[me] = s3[...].reshape(gkv.shape[1:])
    window(11, 12)
    small_start(3)
    zpass(2, (1, 4, 5))
    window(12, 16)
    zpass(2, (2,))
    for way in (0, 1):
        ycopy(way, 2, way).wait_recv()
        ccopy(2, way).start()
    small_wait(3)
    whole(0, 4)
    zpass(2, (3,))
    whole(4, 10)
    zpass(3, (0,))
    whole(10, 16)
    window(16, 17)
    small_start(4)
    zpass(3, (1, 4, 5))
    window(17, 20)
    small_wait(4)
    slice_sum = gacc[me]
    for offset in range(1, 8):
        slice_sum = slice_sum + r1in[offset]
    t1[...] = slice_sum.reshape(t1.shape)
    window(20, 21)
    small_start(5)
    zpass(3, (2,))
    window(21, 22)
    zpass(3, (3,))
    zpass(4, (0, 2, 1, 4, 5, 3))
    small_wait(5)
    part_sum = t1[z]
    for offset in range(1, 8):
        part_sum = part_sum + r2in[offset]
    part_out[...] = part_sum
    for offset in range(NY):
        for part in (0, 1):
            ccopy(offset, part).wait()
    for way in (0, 1):
        for step in range(1, 5):
            for part in zparts(way, step):
                zcopy(way, step, part).wait_send()
        for part in (0, 1):
            ycopy(way, 1, part).wait_send()
        ycopy(way, 2, way).wait_send()
    for phase in range(6):
        for offset in range(1, 8):
            small(phase, offset).wait_send()
    for copy in local:
        copy.wait()


def pair_kernel(
    rf_any, qd_ref, kv_ref, nd_ref, dq_out, dkv_out, dq_acc, dk_acc, dv_acc, rf_ref, list_ref, sem,
    *, factor,
):
    y, z, c = place()
    blocks = qd_ref.shape[2] // BLOCK
    grid = NZ * blocks
    refs = pltpu.make_async_copy(rf_any, rf_ref, sem)
    refs.start()

    @pl.loop(0, grid)
    def _(i):
        zero = jnp.zeros((BLOCK, qd_ref.shape[3]), F32)
        dq_acc[i] = zero
        dk_acc[i] = zero
        dv_acc[i] = zero

    def window_item(n, slot, b, seq, key_block, wanted):
        member = (seq // (NC * NZ)) * NC + lax.rem(seq, NC)
        list_ref[n] = ((slot * blocks + b) << 8) | ((member * blocks + key_block) << 1)
        return n + wanted.astype(jnp.int32)

    seq = (y * NZ + z) * NC + c
    nearby = jnp.where(c == 0, seq + 1, seq - 1)
    count = window_item(
        jnp.int32(0), z, jnp.where(c == 0, blocks - 1, 0), nearby, jnp.where(c == 0, 0, blocks - 1), seq >= 0
    )
    far_slot = jnp.where(c == 0, lax.rem(z + 1, NZ), lax.rem(z + NZ - 1, NZ))
    far_seq = (y * NZ + far_slot) * NC + c
    far_key = jnp.where(c == 0, far_seq - 1, far_seq + 1)
    inside = jnp.logical_and(far_key >= 0, far_key < NY * NZ * NC)
    count = window_item(
        count, far_slot, jnp.where(c == 0, 0, blocks - 1),
        jnp.clip(far_key, 0, NY * NZ * NC - 1), jnp.where(c == 0, blocks - 1, 0), inside,
    )

    refs.wait()

    def per_slot(slot, n):
        for b in range(blocks):
            for r in range(3):
                code = rf_ref[slot, r, b]
                list_ref[n] = ((slot * blocks + b) << 8) | ((code & (grid - 1)) << 1)
                n = n + ((code >> 6) == z).astype(jnp.int32)
        return n

    count = lax.fori_loop(0, NZ, per_slot, count)
    list_ref[count] = jnp.int32(1)

    def terms(item):
        query, key = item >> 8, (item >> 1) & (grid - 1)
        qs, qb = query >> 3, query & (blocks - 1)
        ks, kb = key >> 3, key & (blocks - 1)
        qrows = pl.ds(pl.multiple_of(qb * BLOCK, BLOCK), BLOCK)
        krows = pl.ds(pl.multiple_of(kb * BLOCK, BLOCK), BLOCK)
        return pair_terms(
            per_head(qd_ref[qs, 0, qrows, :]),
            per_head(qd_ref[qs, 1, qrows, :]),
            query_rows(nd_ref[qs, qb >> 1], qb),
            kv_ref[ks, 0, krows, :],
            kv_ref[ks, 1, krows, :],
            factor,
        )

    @pl.loop(0, (count + 1) // 2)
    def _(i):
        items = [list_ref[2 * i], list_ref[2 * i + 1]]
        sums = [terms(item) for item in items]
        for item, (dq, dk, dv) in zip(items, sums):
            spare = (item & 1) * grid
            dq_acc[(item >> 8) + spare] += dq
            dk_acc[((item >> 1) & (grid - 1)) + spare] += dk
            dv_acc[((item >> 1) & (grid - 1)) + spare] += dv

    @pl.loop(0, grid)
    def _(i):
        slot = i >> 3
        rows = pl.ds(pl.multiple_of((i & (blocks - 1)) * BLOCK, BLOCK), BLOCK)
        dq_out[slot, rows, :] = dq_acc[i].astype(BF16)
        dkv_out[slot, 0, rows, :] = (dk_acc[i] * factor).astype(BF16)
        dkv_out[slot, 1, rows, :] = dv_acc[i].astype(BF16)


def reduce_kernel(
    dq_in, dkv_in, dq_own, dk_own, dv_own, part_in, glob_ref, dq_out, dk_out, dv_out,
    zbuf, zin, cin, ysum, ybuf, yin, rin, totals,
    zsend, zrecv, ysend, yrecv, csend, crecv, gsend, grecv,
    *, factor,
):
    y, z, c = place()
    half = dq_out.shape[0] // 2
    me = y * NC + c
    zdev = [device(y, lax.rem(z + 1, NZ), c), device(y, lax.rem(z + NZ - 1, NZ), c)]
    ydev = [device(lax.rem(y + 1, NY), z, c), device(lax.rem(y + NY - 1, NY), z, c)]
    cdev = device(y, z, 1 - c)

    def member_device(offset):
        other = lax.rem(me + offset, NY * NC)
        return device(other // NC, z, lax.rem(other, NC))

    def row_device(offset):
        return device(y, lax.rem(z + offset, NZ), c)

    barrier = pltpu.get_barrier_semaphore()
    for offset in range(1, 8):
        for target in (member_device(offset), row_device(offset)):
            pl.semaphore_signal(barrier, inc=1, device_id=target, device_id_type=MESH)
    pl.semaphore_wait(barrier, 14)

    def halves(part):
        return pl.ds(part * half, half)

    def zparts(way, step):
        return (way,) if step == 1 else (1 - way, way)

    def zplain(way, step, part):
        return step == 1 or (step == 2 and part != way)

    def ztarget(way, step):
        return lax.rem(z + (5 - step if way == 0 else NZ - 5 + step), NZ)

    def zcopy(way, step, part):
        if zplain(way, step, part):
            source = dq_in.at[ztarget(way, step), halves(part)]
        else:
            source = zbuf.at[way, step - 1, halves(part)]
        return pltpu.make_async_remote_copy(
            src_ref=source,
            dst_ref=zin.at[way, step - 1, halves(part)],
            send_sem=zsend.at[way, step - 1, part],
            recv_sem=zrecv.at[way, step - 1, part],
            device_id=zdev[way],
            device_id_type=MESH,
        )

    def ccopy(offset, part, h):
        row = lax.rem(y + offset, NY)
        return pltpu.make_async_remote_copy(
            src_ref=dkv_in.at[row * NC + 1 - c, part, halves(h)],
            dst_ref=cin.at[offset, part, halves(h)],
            send_sem=csend.at[offset, part, h],
            recv_sem=crecv.at[offset, part, h],
            device_id=cdev,
            device_id_type=MESH,
        )

    def ycopy(way, step, part, h):
        return pltpu.make_async_remote_copy(
            src_ref=ysum.at[part, halves(h)] if step == 1 else ybuf.at[way, part, halves(h)],
            dst_ref=yin.at[way, step - 1, part, halves(h)],
            send_sem=ysend.at[way, step - 1, part, h],
            recv_sem=yrecv.at[way, step - 1, part, h],
            device_id=ydev[way],
            device_id_type=MESH,
        )

    def small(phase, offset):
        return pltpu.make_async_remote_copy(
            src_ref=part_in if phase == 0 else totals.at[me],
            dst_ref=rin.at[offset] if phase == 0 else totals.at[me],
            send_sem=gsend.at[phase, offset],
            recv_sem=grecv.at[phase, offset],
            device_id=row_device(offset) if phase == 0 else member_device(offset),
            device_id_type=MESH,
        )

    for h in (0, 1):
        for part in (0, 1):
            ccopy(2, part, h).start()
    for offset in range(1, 8):
        small(0, offset).start()
    for way in (0, 1):
        zcopy(way, 1, way).start()
        zcopy(way, 2, 1 - way).start()
    for h in (0, 1):
        for way in (0, 1):
            ccopy(1 if way == 0 else 3, 1 - way, h).start()
    for h in (0, 1):
        for way in (0, 1):
            ccopy(1 if way == 0 else 3, way, h).start()
    for h in (0, 1):
        for part in (0, 1):
            ccopy(0, part, h).start()

    def zround(step, late):
        for way in (0, 1):
            part = way if late else 1 - way
            zcopy(way, step, part).wait_recv()
            rows = halves(part)
            mine = dq_in[ztarget(way, step + 1), rows, :].astype(F32)
            zbuf[way, step, rows, :] = (mine + zin[way, step - 1, rows, :].astype(F32)).astype(BF16)
            zcopy(way, step + 1, part).start()

    def cadd(offset, part, h):
        ccopy(offset, part, h).wait_recv()
        row = lax.rem(y + offset, NY)
        return dkv_in[row * NC + c, part, halves(h), :].astype(F32) + cin[offset, part, halves(h), :].astype(F32)

    def ypass(way, part, h):
        total = cadd(1 if way == 0 else 3, part, h)
        if part == way:
            ycopy(way, 1, part, h).wait_recv()
            total = total + yin[way, 0, part, halves(h), :].astype(F32)
        ybuf[way, part, halves(h), :] = total.astype(BF16)
        ycopy(way, 2, part, h).start()

    for h in (0, 1):
        for part in (0, 1):
            ysum[part, halves(h), :] = cadd(2, part, h).astype(BF16)
            ycopy(part, 1, part, h).start()
    ypass(0, 1, 0)
    ypass(1, 0, 0)
    zround(1, True)
    ypass(0, 1, 1)
    ypass(1, 0, 1)
    for offset in range(1, 8):
        small(0, offset).wait_recv()
    totals[me, z] = part_in[...]
    for offset in range(1, 8):
        totals[me, lax.rem(z + NZ - offset, NZ)] = rin[offset]
    ypass(0, 0, 0)
    ypass(1, 1, 0)
    zround(2, False)
    for offset in range(1, 8):
        small(1, offset).start()
    zround(2, True)
    ypass(0, 0, 1)
    ypass(1, 1, 1)
    zround(3, False)
    zround(3, True)
    for offset in range(1, 8):
        small(1, offset).wait_recv()
    seq = lax.axis_index("seq")
    per_half = half // BLOCK
    for part, out, own in ((1, dv_out, dv_own), (0, dk_out, dk_own)):
        for h in (0, 1):
            total = cadd(0, part, h)
            for way in (0, 1):
                ycopy(way, 2, part, h).wait_recv()
                total = total + yin[way, 1, part, halves(h), :].astype(F32)
            for i in range(per_half):
                b = h * per_half + i
                rows = pl.ds(b * BLOCK, BLOCK)
                more = own[rows, :]
                for g in range(2):
                    whole = totals[pl.ds(4 * g + 2 * part, 2)].reshape(more.shape)
                    more = more + jnp.where(glob_ref[g] == seq * 2 * per_half + b, whole, jnp.zeros_like(whole))
                if part == 0:
                    more = more * factor
                out[rows, :] = (total[i * BLOCK : (i + 1) * BLOCK] + more).astype(BF16)
    for part in (0, 1):
        rows = halves(part)
        total = dq_in[z, rows, :].astype(F32) + dq_own[rows, :]
        for way in (0, 1):
            zcopy(way, 4, part).wait_recv()
            total = total + zin[way, 3, rows, :].astype(F32)
        dq_out[rows, :] = total.astype(BF16)
    for way in (0, 1):
        for step in range(1, 5):
            for part in zparts(way, step):
                zcopy(way, step, part).wait_send()
        for h in (0, 1):
            ycopy(way, 1, way, h).wait_send()
            for part in (0, 1):
                ycopy(way, 2, part, h).wait_send()
    for offset in range(NY):
        for part in (0, 1):
            for h in (0, 1):
                ccopy(offset, part, h).wait_send()
    for phase in range(2):
        for offset in range(1, 8):
            small(phase, offset).wait_send()


def shards(queries, keys, values, outputs, d_outputs, log_norm, rand_owner, rand_local, glob_blocks):
    tokens, features = queries.shape
    blocks = tokens // BLOCK
    factor = 1.0 / math.sqrt(features // log_norm.shape[0])
    queries, keys, values, outputs, d_outputs, log_norm, owner, local, glob_blocks = (
        pltpu.with_memory_space_constraint(array, pltpu.HBM)
        for array in (
            queries, keys, values, outputs, d_outputs, log_norm, rand_owner.T, rand_local.T, glob_blocks
        )
    )
    vmem = pl.BlockSpec(memory_space=pltpu.VMEM)
    smem = pl.BlockSpec(memory_space=pltpu.SMEM)
    anywhere = pl.BlockSpec(memory_space=pl.ANY)
    hbm = pl.BlockSpec(memory_space=pltpu.HBM)
    dma = pltpu.SemaphoreType.DMA

    slices = (8, BLOCK // 2, features)
    eighths = (8, BLOCK // 16, features)
    qd, kv, nd, rf, dq_own, dk_own, dv_own, part = pl.pallas_call(
        functools.partial(gather_kernel, factor=factor),
        out_shape=(
            jax.ShapeDtypeStruct((NZ, 2, tokens, features), BF16),
            jax.ShapeDtypeStruct((NY * NC, 2, tokens, features), BF16),
            jax.ShapeDtypeStruct((NZ, blocks // 2, 8, BLOCK), F32),
            jax.ShapeDtypeStruct((NZ, 8, BLOCK), jnp.int32),
            jax.ShapeDtypeStruct((tokens, features), F32),
            jax.ShapeDtypeStruct((tokens, features), F32),
            jax.ShapeDtypeStruct((tokens, features), F32),
            jax.ShapeDtypeStruct(eighths[1:], F32),
        ),
        in_specs=[hbm] * 5 + [vmem] * 3 + [smem],
        out_specs=(anywhere,) * 4 + (vmem,) * 4,
        scratch_shapes=[
            pltpu.VMEM((tokens, features), BF16), pltpu.VMEM((tokens, features), BF16),
            pltpu.VMEM((tokens, features), BF16), pltpu.VMEM((tokens, features), BF16),
            pltpu.VMEM((tokens, features), BF16),
            pltpu.VMEM((blocks // 2, 8, BLOCK), F32), pltpu.VMEM((8, BLOCK), jnp.int32), pltpu.VMEM(slices, BF16),
            pltpu.VMEM(slices, BF16), pltpu.VMEM(eighths, BF16), pltpu.VMEM(eighths, BF16),
            pltpu.VMEM(eighths[1:], BF16), pltpu.VMEM(eighths, BF16), pltpu.VMEM(eighths, BF16),
            pltpu.VMEM(slices, BF16), pltpu.VMEM(slices, F32), pltpu.VMEM(slices, F32),
            pltpu.VMEM(eighths, F32), pltpu.VMEM(eighths, F32),
            dma((2, 4, 6)), dma((2, 4, 6)), dma((2, 2, 2)), dma((2, 2, 2)),
            dma((NY, 2)), dma((NY, 2)), dma((6, 8)), dma((6, 8)), dma((11,)),
        ],
        compiler_params=pltpu.CompilerParams(collective_id=0, has_side_effects=True, vmem_limit_bytes=12 * MIB),
        name="gather",
    )(queries, d_outputs, keys, values, outputs, log_norm, owner, local, glob_blocks)

    dq_part, dkv_part = pl.pallas_call(
        functools.partial(pair_kernel, factor=factor),
        out_shape=(
            jax.ShapeDtypeStruct((NZ, tokens, features), BF16),
            jax.ShapeDtypeStruct((NY * NC, 2, tokens, features), BF16),
        ),
        in_specs=[anywhere, vmem, vmem, vmem],
        out_specs=(vmem, vmem),
        scratch_shapes=[
            pltpu.VMEM((NZ * blocks + 1, BLOCK, features), F32),
            pltpu.VMEM((NY * NC * blocks + 1, BLOCK, features), F32),
            pltpu.VMEM((NY * NC * blocks + 1, BLOCK, features), F32),
            pltpu.SMEM((NZ, 8, BLOCK), jnp.int32),
            pltpu.SMEM((256,), jnp.int32),
            dma,
        ],
        compiler_params=pltpu.CompilerParams(vmem_limit_bytes=16 * MIB),
        name="pairs",
    )(rf, qd, kv, nd)

    return tuple(pl.pallas_call(
        functools.partial(reduce_kernel, factor=factor),
        out_shape=(jax.ShapeDtypeStruct((tokens, features), BF16),) * 3,
        in_specs=[vmem] * 6 + [smem],
        out_specs=(vmem,) * 3,
        scratch_shapes=[
            pltpu.VMEM((2, 4, tokens, features), BF16),
            pltpu.VMEM((2, 4, tokens, features), BF16),
            pltpu.VMEM((NY, 2, tokens, features), BF16),
            pltpu.VMEM((2, tokens, features), BF16),
            pltpu.VMEM((2, 2, tokens, features), BF16),
            pltpu.VMEM((2, 2, 2, tokens, features), BF16),
            pltpu.VMEM(eighths, F32),
            pltpu.VMEM((8,) + eighths, F32),
            dma((2, 4, 2)), dma((2, 4, 2)), dma((2, 2, 2, 2)), dma((2, 2, 2, 2)),
            dma((NY, 2, 2)), dma((NY, 2, 2)), dma((2, 8)), dma((2, 8)),
        ],
        compiler_params=pltpu.CompilerParams(collective_id=1, has_side_effects=True, vmem_limit_bytes=24 * MIB),
        name="reduce",
    )(dq_part, dkv_part, dq_own, dk_own, dv_own, part, glob_blocks))


def solution(mesh):
    placed = (
        P("seq", "head"), P("seq", "head"), P("seq", "head"), P("seq", "head"), P("seq", "head"),
        P("head", "seq"), P("seq", None), P("seq", None), P(),
    )
    return jax.shard_map(
        shards,
        mesh=mesh,
        in_specs=placed,
        out_specs=(P("seq", "head"), P("seq", "head"), P("seq", "head")),
        check_vma=False,
    )
```

```python
import functools
import math

import jax
import jax.numpy as jnp
from jax import lax
from jax.experimental import pallas as pl
from jax.experimental.pallas import tpu as pltpu
from jax.sharding import PartitionSpec as P

BLOCK = 128
NY, NZ, NC = 4, 8, 2
MESH = pl.DeviceIdType.MESH
F32 = jnp.float32
BF16 = jnp.bfloat16
MIB = 1024 * 1024


def place():
    seq = lax.axis_index("seq")
    core = lax.rem(seq, NC)
    z = lax.rem(seq // NC, NZ)
    y = seq // (NC * NZ)
    return y, z, core


def device(y, z, core):
    return {"seq": (y * NZ + z) * NC + core}


def per_head(x):
    lane = lax.broadcasted_iota(jnp.int32, x.shape, 1)
    zero = jnp.zeros_like(x)
    low = lane < x.shape[1] // 2
    return jnp.concatenate([jnp.where(low, x, zero), jnp.where(low, zero, x)], axis=0)


def pair_terms(q2, d2, nd, k, v, factor):
    k = k * factor
    across = (((1,), (1,)), ((), ()))
    scores = lax.dot_general(k, q2, across, preferred_element_type=F32)
    grads = lax.dot_general(v, d2, across, preferred_element_type=F32)
    norm = jnp.concatenate([nd[0:1], nd[1:2]], axis=1)
    delta = jnp.concatenate([nd[2:3], nd[3:4]], axis=1)
    weights = jnp.exp(scores - norm)
    grad_scores = weights * (grads - delta)
    weights_low = weights.astype(BF16)
    scores_low = grad_scores.astype(BF16)
    dv = jnp.dot(weights_low, d2, preferred_element_type=F32)
    dk = jnp.dot(scores_low, q2, preferred_element_type=F32)
    turned = k.T
    half = turned.shape[0] // 2
    dq = jnp.concatenate(
        [
            jnp.dot(turned[:half], scores_low[:, :BLOCK], preferred_element_type=F32),
            jnp.dot(turned[half:], scores_low[:, BLOCK:], preferred_element_type=F32),
        ],
        axis=0,
    )
    return dq, dk, dv


def query_rows(nd_tile, b):
    return jnp.where(lax.rem(b, 2) == 0, nd_tile[0:4], nd_tile[4:8])


def gather_kernel(
    q_hbm, d_hbm, k_hbm, v_hbm, o_hbm, norm_ref, owner_ref, local_ref, glob_ref,
    qd_out, kv_out, nd_out, rf_out, dq_out, dk_out, dv_out, part_out,
    q_ref, d_ref, k_ref, v_ref, o_ref, nd_ref, cand_ref,
    g1in, s1, g2in, s2, g3in, s3, gkv, gacc, r1in, t1, r2in,
    zsend, zrecv, ysend, yrecv, csend, crecv, gsend, grecv, lsem,
    *, factor,
):
    y, z, c = place()
    tokens = q_ref.shape[0]
    blocks = tokens // BLOCK
    half = BLOCK // 2
    loads = [
        pltpu.make_async_copy(source, target, lsem.at[i])
        for i, (source, target) in enumerate(
            ((k_hbm, k_ref), (v_hbm, v_ref), (o_hbm, o_ref), (d_hbm, d_ref), (q_hbm, q_ref))
        )
    ]
    for copy in loads:
        copy.start()
    zdev = [device(y, lax.rem(z + 1, NZ), c), device(y, lax.rem(z + NZ - 1, NZ), c)]
    ydev = [device(lax.rem(y + 1, NY), z, c), device(lax.rem(y + NY - 1, NY), z, c)]
    cdev = device(y, z, 1 - c)
    me = y * NC + c

    def member(offset):
        return lax.rem(me + offset, NY * NC)

    def member_device(offset):
        other = member(offset)
        return device(other // NC, z, lax.rem(other, NC))

    def row_device(offset):
        return device(y, lax.rem(z + offset, NZ), c)

    barrier = pltpu.get_barrier_semaphore()
    for offset in range(1, 8):
        for target in (member_device(offset), row_device(offset)):
            pl.semaphore_signal(barrier, inc=1, device_id=target, device_id_type=MESH)
    pl.semaphore_wait(barrier, 14)

    def zwhere(part, slot):
        if part < 4:
            return qd_out.at[slot, part // 2, pl.ds((part % 2) * tokens // 2, tokens // 2)]
        return nd_out.at[slot]

    def zown(part):
        if part < 4:
            return (q_hbm, d_hbm)[part // 2].at[pl.ds((part % 2) * tokens // 2, tokens // 2)]
        return nd_ref

    def zcopy(way, step, part):
        slot = lax.rem(z + (NZ - step + 1 if way == 0 else step - 1), NZ)
        return pltpu.make_async_remote_copy(
            src_ref=zown(part) if step == 1 else zwhere(part, slot),
            dst_ref=zwhere(part, slot),
            send_sem=zsend.at[way, step - 1, part],
            recv_sem=zrecv.at[way, step - 1, part],
            device_id=zdev[way],
            device_id_type=MESH,
        )

    def zparts(way, step):
        if step < 4:
            return (0, 1, 2, 3, 4)
        return (0, 1, 4) if way == 0 else (2, 3)

    def ycopy(way, step, part):
        row = lax.rem(y + ((NY if step == 1 else NY - 1) if way == 0 else step - 1), NY)
        slot = row * NC + c
        return pltpu.make_async_remote_copy(
            src_ref=(k_hbm, v_hbm)[part] if step == 1 else kv_out.at[slot, part],
            dst_ref=kv_out.at[slot, part],
            send_sem=ysend.at[way, step - 1, part],
            recv_sem=yrecv.at[way, step - 1, part],
            device_id=ydev[way],
            device_id_type=MESH,
        )

    def ccopy(offset, part):
        slot = lax.rem(y + offset, NY) * NC + c
        return pltpu.make_async_remote_copy(
            src_ref=(k_hbm, v_hbm)[part] if offset == 0 else kv_out.at[slot, part],
            dst_ref=kv_out.at[slot, part],
            send_sem=csend.at[offset, part],
            recv_sem=crecv.at[offset, part],
            device_id=cdev,
            device_id_type=MESH,
        )

    def small(phase, offset):
        over_column = phase in (0, 3, 4)
        other = member(offset) if over_column else lax.rem(z + offset, NZ)
        source, target = (
            (cand_ref.at[other], g1in.at[offset]),
            (s1.at[other], g2in.at[offset]),
            (s2, g3in.at[offset]),
            (gkv.at[me], gkv.at[me]),
            (gacc.at[other], r1in.at[offset]),
            (t1.at[other], r2in.at[offset]),
        )[phase]
        return pltpu.make_async_remote_copy(
            src_ref=source,
            dst_ref=target,
            send_sem=gsend.at[phase, offset],
            recv_sem=grecv.at[phase, offset],
            device_id=member_device(offset) if over_column else row_device(offset),
            device_id_type=MESH,
        )

    def small_start(phase):
        for offset in range(1, 8):
            small(phase, offset).start()

    def small_wait(phase):
        for offset in range(1, 8):
            small(phase, offset).wait_recv()

    def zstart(step, parts):
        for part in parts:
            for way in (0, 1):
                if part in zparts(way, step):
                    zcopy(way, step, part).start()

    def zpass(step, parts):
        for part in parts:
            for way in (0, 1):
                if part in zparts(way, step):
                    zcopy(way, step, part).wait_recv()
                    if step < 4 and part in zparts(way, step + 1):
                        zcopy(way, step + 1, part).start()

    def block_rows(b):
        return pl.ds(pl.multiple_of(b * BLOCK, BLOCK), BLOCK)

    def window(first, end):
        @pl.loop(first, end)
        def _(i):
            up = (i >= blocks).astype(jnp.int32)
            down = (i >= 2 * blocks - 1).astype(jnp.int32)
            low = i - up * blocks - down * (blocks - 1)
            qb = low + down
            kb = low + up - down
            rows, krows = block_rows(qb), block_rows(kb)
            dq, dk, dv = pair_terms(
                per_head(q_ref[rows, :]), per_head(d_ref[rows, :]), query_rows(nd_ref[qb // 2], qb),
                k_ref[krows, :], v_ref[krows, :], factor,
            )
            dq_out[rows, :] += dq
            dk_out[krows, :] += dk
            dv_out[krows, :] += dv

    def whole(first, end):
        @pl.loop(first, end)
        def _(i):
            b, g = i // 2, lax.rem(i, 2)
            rows = block_rows(b)
            part = 4 * g
            dq, dk, dv = pair_terms(
                per_head(q_ref[rows, :]), per_head(d_ref[rows, :]), query_rows(nd_ref[b // 2], b),
                jnp.concatenate([gkv[part], gkv[part + 1]], axis=0),
                jnp.concatenate([gkv[part + 2], gkv[part + 3]], axis=0),
                factor,
            )
            dq_out[rows, :] += dq
            gacc[part] += dk[:half]
            gacc[part + 1] += dk[half:]
            gacc[part + 2] += dv[:half]
            gacc[part + 3] += dv[half:]

    def ystep1(part):
        for way in (0, 1):
            ycopy(way, 1, part).wait_recv()
            if part == way:
                ycopy(way, 2, part).start()
            ccopy(NY - 1 if way == 0 else 1, part).start()

    zstart(1, (0,))
    loads[0].wait()
    loads[1].wait()
    seq = lax.axis_index("seq")
    for g in range(2):
        local_block = glob_ref[g] - seq * blocks
        for i, ref in enumerate((k_ref, v_ref)):
            block = jnp.zeros((BLOCK, k_ref.shape[1]), BF16)
            for b in range(blocks):
                block = jnp.where(local_block == b, ref[pl.ds(b * BLOCK, BLOCK), :], block)
            cand_ref[4 * g + 2 * i] = block[:half]
            cand_ref[4 * g + 2 * i + 1] = block[half:]
    owner = owner_ref[...]
    column = jnp.bitwise_and(owner >> 1, NZ - 1)
    other = (owner >> 4) * NC + jnp.bitwise_and(owner, 1)
    nd_ref[blocks // 2] = jnp.zeros(nd_ref.shape[1:], F32)
    nd_ref[blocks // 2, 0:3, 0:blocks] = ((column * (NY * NC) + other) * blocks + local_ref[...]).astype(F32)
    loads[2].wait()
    loads[3].wait()

    def row_values(b):
        rows = pl.ds(b * BLOCK, BLOCK)
        turned = (o_ref[rows, :].astype(F32) * d_ref[rows, :].astype(F32)).T
        nd_ref[b // 2, 4 * (b % 2) : 4 * (b % 2) + 4, :] = jnp.concatenate(
            [
                norm_ref[:, rows],
                jnp.sum(turned[: turned.shape[0] // 2], axis=0, keepdims=True),
                jnp.sum(turned[turned.shape[0] // 2 :], axis=0, keepdims=True),
            ],
            axis=0,
        )

    row_values(0)
    small_start(0)
    zstart(1, (1,))
    for part in (0, 1):
        for way in (0, 1):
            ycopy(way, 1, part).start()
        ccopy(0, part).start()
    for b in range(1, blocks):
        row_values(b)
    loads[4].wait()
    local = [
        pltpu.make_async_copy(q_ref, qd_out.at[z, 0], lsem.at[5]),
        pltpu.make_async_copy(d_ref, qd_out.at[z, 1], lsem.at[6]),
        pltpu.make_async_copy(nd_ref, nd_out.at[z], lsem.at[7]),
        pltpu.make_async_copy(k_ref, kv_out.at[me, 0], lsem.at[8]),
        pltpu.make_async_copy(v_ref, kv_out.at[me, 1], lsem.at[9]),
    ]
    for copy in local:
        copy.start()

    @pl.loop(0, blocks)
    def _(b):
        zero = jnp.zeros((BLOCK, q_ref.shape[1]), F32)
        dq_out[block_rows(b), :] = zero
        dk_out[block_rows(b), :] = zero
        dv_out[block_rows(b), :] = zero
        gacc[b] = zero[:half]

    small_wait(0)
    slice_sum = cand_ref[me].astype(F32)
    for offset in range(1, 8):
        slice_sum = slice_sum + g1in[offset].astype(F32)
    s1[...] = slice_sum.astype(BF16).reshape(s1.shape)
    window(0, 2)
    small_start(1)
    zstart(1, (4, 2, 3))
    window(2, 4)
    zpass(1, (0,))
    window(4, 5)
    small_wait(1)
    part_sum = s1[z].astype(F32)
    for offset in range(1, 8):
        part_sum = part_sum + g2in[offset].astype(F32)
    s2[...] = part_sum.astype(BF16)
    window(5, 6)
    small_start(2)
    zpass(1, (1, 4))
    ystep1(0)
    window(6, 9)
    zpass(1, (2,))
    window(9, 10)
    zpass(1, (3,))
    ystep1(1)
    window(10, 11)
    zpass(2, (0,))
    small_wait(2)
    s3[z] = s2[...]
    for offset in range(1, 8):
        s3[lax.rem(z + NZ - offset, NZ)] = g3in[offset]
    gkv[me] = s3[...].reshape(gkv.shape[1:])
    window(11, 12)
    small_start(3)
    zpass(2, (1, 4))
    window(12, 16)
    zpass(2, (2,))
    for way in (0, 1):
        ycopy(way, 2, way).wait_recv()
        ccopy(2, way).start()
    small_wait(3)
    whole(0, 4)
    zpass(2, (3,))
    whole(4, 10)
    zpass(3, (0,))
    whole(10, 16)
    window(16, 17)
    small_start(4)
    zpass(3, (1, 4))
    window(17, 20)
    small_wait(4)
    slice_sum = gacc[me]
    for offset in range(1, 8):
        slice_sum = slice_sum + r1in[offset]
    t1[...] = slice_sum.reshape(t1.shape)
    window(20, 21)
    small_start(5)
    zpass(3, (2,))
    window(21, 22)
    zpass(3, (3,))
    zpass(4, (0, 2, 1, 4, 3))
    small_wait(5)
    part_sum = t1[z]
    for offset in range(1, 8):
        part_sum = part_sum + r2in[offset]
    part_out[...] = part_sum
    for offset in range(NY):
        for part in (0, 1):
            ccopy(offset, part).wait()
    for way in (0, 1):
        for step in range(1, 5):
            for part in zparts(way, step):
                zcopy(way, step, part).wait_send()
        for part in (0, 1):
            ycopy(way, 1, part).wait_send()
        ycopy(way, 2, way).wait_send()
    for phase in range(6):
        for offset in range(1, 8):
            small(phase, offset).wait_send()
    for copy in local:
        copy.wait()
    for slot in range(NZ):
        rf_out[slot] = nd_out[slot, blocks // 2].astype(jnp.int32)


def pair_kernel(
    rf_any, qd_ref, kv_ref, nd_ref, dq_out, dkv_out, dq_acc, dk_acc, dv_acc, rf_ref, list_ref, sem,
    *, factor,
):
    y, z, c = place()
    blocks = qd_ref.shape[2] // BLOCK
    grid = NZ * blocks
    refs = pltpu.make_async_copy(rf_any, rf_ref, sem)
    refs.start()

    def window_item(n, slot, b, seq, key_block, wanted):
        member = (seq // (NC * NZ)) * NC + lax.rem(seq, NC)
        list_ref[n] = ((slot * blocks + b) << 8) | ((member * blocks + key_block) << 1)
        return n + wanted.astype(jnp.int32)

    seq = (y * NZ + z) * NC + c
    nearby = jnp.where(c == 0, seq + 1, seq - 1)
    count = window_item(
        jnp.int32(0), z, jnp.where(c == 0, blocks - 1, 0), nearby, jnp.where(c == 0, 0, blocks - 1), seq >= 0
    )
    far_slot = jnp.where(c == 0, lax.rem(z + 1, NZ), lax.rem(z + NZ - 1, NZ))
    far_seq = (y * NZ + far_slot) * NC + c
    far_key = jnp.where(c == 0, far_seq - 1, far_seq + 1)
    inside = jnp.logical_and(far_key >= 0, far_key < NY * NZ * NC)
    count = window_item(
        count, far_slot, jnp.where(c == 0, 0, blocks - 1),
        jnp.clip(far_key, 0, NY * NZ * NC - 1), jnp.where(c == 0, blocks - 1, 0), inside,
    )

    refs.wait()

    def per_slot(slot, n):
        zero = jnp.zeros((BLOCK, qd_ref.shape[3]), F32)
        for b in range(blocks):
            dq_acc[slot * blocks + b] = zero
            dk_acc[slot * blocks + b] = zero
            dv_acc[slot * blocks + b] = zero
            for r in range(3):
                code = rf_ref[slot, r, b]
                list_ref[n] = ((slot * blocks + b) << 8) | ((code & (grid - 1)) << 1)
                n = n + ((code >> 6) == z).astype(jnp.int32)
        return n

    count = lax.fori_loop(0, NZ, per_slot, count)
    list_ref[count] = jnp.int32(1)

    def terms(item):
        query, key = item >> 8, (item >> 1) & (grid - 1)
        qs, qb = query >> 3, query & (blocks - 1)
        ks, kb = key >> 3, key & (blocks - 1)
        qrows = pl.ds(pl.multiple_of(qb * BLOCK, BLOCK), BLOCK)
        krows = pl.ds(pl.multiple_of(kb * BLOCK, BLOCK), BLOCK)
        return pair_terms(
            per_head(qd_ref[qs, 0, qrows, :]),
            per_head(qd_ref[qs, 1, qrows, :]),
            query_rows(nd_ref[qs, qb >> 1], qb),
            kv_ref[ks, 0, krows, :],
            kv_ref[ks, 1, krows, :],
            factor,
        )

    @pl.loop(0, (count + 1) // 2)
    def _(i):
        items = [list_ref[2 * i], list_ref[2 * i + 1]]
        sums = [terms(item) for item in items]
        for item, (dq, dk, dv) in zip(items, sums):
            spare = (item & 1) * grid
            dq_acc[(item >> 8) + spare] += dq
            dk_acc[((item >> 1) & (grid - 1)) + spare] += dk
            dv_acc[((item >> 1) & (grid - 1)) + spare] += dv

    @pl.loop(0, grid)
    def _(i):
        slot = i >> 3
        rows = pl.ds(pl.multiple_of((i & (blocks - 1)) * BLOCK, BLOCK), BLOCK)
        dq_out[slot, rows, :] = dq_acc[i].astype(BF16)
        dkv_out[slot, 0, rows, :] = (dk_acc[i] * factor).astype(BF16)
        dkv_out[slot, 1, rows, :] = dv_acc[i].astype(BF16)


def reduce_kernel(
    dq_in, dkv_in, dk_own, dv_own, part_in, glob_ref, dq_out, dk_out, dv_out,
    zbuf, zin, cin, ysum, ybuf, yin, rin, totals,
    zsend, zrecv, ysend, yrecv, csend, crecv, gsend, grecv,
    *, factor,
):
    y, z, c = place()
    half = dk_out.shape[0] // 2
    me = y * NC + c
    zdev = [device(y, lax.rem(z + 1, NZ), c), device(y, lax.rem(z + NZ - 1, NZ), c)]
    ydev = [device(lax.rem(y + 1, NY), z, c), device(lax.rem(y + NY - 1, NY), z, c)]
    cdev = device(y, z, 1 - c)

    def member_device(offset):
        other = lax.rem(me + offset, NY * NC)
        return device(other // NC, z, lax.rem(other, NC))

    def row_device(offset):
        return device(y, lax.rem(z + offset, NZ), c)

    barrier = pltpu.get_barrier_semaphore()
    for offset in range(1, 8):
        for target in (member_device(offset), row_device(offset)):
            pl.semaphore_signal(barrier, inc=1, device_id=target, device_id_type=MESH)
    pl.semaphore_wait(barrier, 14)

    def halves(part):
        return pl.ds(part * half, half)

    def zparts(way, step):
        return (way,) if step == 1 else (1 - way, way)

    def zplain(way, step, part):
        return step == 1 or (step == 2 and part != way)

    def ztarget(way, step):
        return lax.rem(z + (5 - step if way == 0 else NZ - 5 + step), NZ)

    def zcopy(way, step, part):
        if zplain(way, step, part):
            source = dq_in.at[ztarget(way, step), halves(part)]
        else:
            source = zbuf.at[way, step - 1, halves(part)]
        return pltpu.make_async_remote_copy(
            src_ref=source,
            dst_ref=dq_out.at[way, halves(part)] if step == 4 else zin.at[way, step - 1, halves(part)],
            send_sem=zsend.at[way, step - 1, part],
            recv_sem=zrecv.at[way, step - 1, part],
            device_id=zdev[way],
            device_id_type=MESH,
        )

    def ccopy(offset, part, h):
        row = lax.rem(y + offset, NY)
        return pltpu.make_async_remote_copy(
            src_ref=dkv_in.at[row * NC + 1 - c, part, halves(h)],
            dst_ref=cin.at[offset, part, halves(h)],
            send_sem=csend.at[offset, part, h],
            recv_sem=crecv.at[offset, part, h],
            device_id=cdev,
            device_id_type=MESH,
        )

    def ycopy(way, step, part, h):
        return pltpu.make_async_remote_copy(
            src_ref=ysum.at[part, halves(h)] if step == 1 else ybuf.at[way, part, halves(h)],
            dst_ref=yin.at[way, step - 1, part, halves(h)],
            send_sem=ysend.at[way, step - 1, part, h],
            recv_sem=yrecv.at[way, step - 1, part, h],
            device_id=ydev[way],
            device_id_type=MESH,
        )

    def small(phase, offset):
        return pltpu.make_async_remote_copy(
            src_ref=part_in if phase == 0 else totals.at[me],
            dst_ref=rin.at[offset] if phase == 0 else totals.at[me],
            send_sem=gsend.at[phase, offset],
            recv_sem=grecv.at[phase, offset],
            device_id=row_device(offset) if phase == 0 else member_device(offset),
            device_id_type=MESH,
        )

    for h in (0, 1):
        for part in (0, 1):
            ccopy(2, part, h).start()
    for offset in range(1, 8):
        small(0, offset).start()
    for way in (0, 1):
        zcopy(way, 1, way).start()
        zcopy(way, 2, 1 - way).start()
    for h in (0, 1):
        for way in (0, 1):
            ccopy(1 if way == 0 else 3, 1 - way, h).start()
    for h in (0, 1):
        for way in (0, 1):
            ccopy(1 if way == 0 else 3, way, h).start()
    for h in (0, 1):
        for part in (0, 1):
            ccopy(0, part, h).start()

    def zround(step, late):
        for way in (0, 1):
            part = way if late else 1 - way
            zcopy(way, step, part).wait_recv()
            rows = halves(part)
            mine = dq_in[ztarget(way, step + 1), rows, :].astype(F32)
            zbuf[way, step, rows, :] = (mine + zin[way, step - 1, rows, :].astype(F32)).astype(BF16)
            zcopy(way, step + 1, part).start()

    def cadd(offset, part, h):
        ccopy(offset, part, h).wait_recv()
        row = lax.rem(y + offset, NY)
        return dkv_in[row * NC + c, part, halves(h), :].astype(F32) + cin[offset, part, halves(h), :].astype(F32)

    def ypass(way, part, h):
        total = cadd(1 if way == 0 else 3, part, h)
        if part == way:
            ycopy(way, 1, part, h).wait_recv()
            total = total + yin[way, 0, part, halves(h), :].astype(F32)
        ybuf[way, part, halves(h), :] = total.astype(BF16)
        ycopy(way, 2, part, h).start()

    for h in (0, 1):
        for part in (0, 1):
            ysum[part, halves(h), :] = cadd(2, part, h).astype(BF16)
            ycopy(part, 1, part, h).start()
    ypass(0, 1, 0)
    ypass(1, 0, 0)
    zround(1, True)
    ypass(0, 1, 1)
    ypass(1, 0, 1)
    for offset in range(1, 8):
        small(0, offset).wait_recv()
    totals[me, z] = part_in[...]
    for offset in range(1, 8):
        totals[me, lax.rem(z + NZ - offset, NZ)] = rin[offset]
    ypass(0, 0, 0)
    ypass(1, 1, 0)
    zround(2, False)
    for offset in range(1, 8):
        small(1, offset).start()
    zround(2, True)
    ypass(0, 0, 1)
    ypass(1, 1, 1)
    zround(3, False)
    zround(3, True)
    for offset in range(1, 8):
        small(1, offset).wait_recv()
    seq = lax.axis_index("seq")
    per_half = half // BLOCK
    for part, out, own in ((1, dv_out, dv_own), (0, dk_out, dk_own)):
        for h in (0, 1):
            total = cadd(0, part, h)
            for way in (0, 1):
                ycopy(way, 2, part, h).wait_recv()
                total = total + yin[way, 1, part, halves(h), :].astype(F32)
            for i in range(per_half):
                b = h * per_half + i
                rows = pl.ds(b * BLOCK, BLOCK)
                more = own[rows, :]
                for g in range(2):
                    whole = totals[pl.ds(4 * g + 2 * part, 2)].reshape(more.shape)
                    more = more + jnp.where(glob_ref[g] == seq * 2 * per_half + b, whole, jnp.zeros_like(whole))
                if part == 0:
                    more = more * factor
                out[rows, :] = (total[i * BLOCK : (i + 1) * BLOCK] + more).astype(BF16)
    for part in (0, 1):
        for way in (0, 1):
            zcopy(way, 4, part).wait_recv()
    for way in (0, 1):
        for step in range(1, 5):
            for part in zparts(way, step):
                zcopy(way, step, part).wait_send()
        for h in (0, 1):
            ycopy(way, 1, way, h).wait_send()
            for part in (0, 1):
                ycopy(way, 2, part, h).wait_send()
    for offset in range(NY):
        for part in (0, 1):
            for h in (0, 1):
                ccopy(offset, part, h).wait_send()
    for phase in range(2):
        for offset in range(1, 8):
            small(phase, offset).wait_send()


def last_kernel(part_ref, own_ref, arrived_ref, dk_in, dv_in, dq_out, dk_out, dv_out):
    y, z, c = place()
    for b in range(own_ref.shape[0] // BLOCK):
        rows = pl.ds(b * BLOCK, BLOCK)
        total = part_ref[z, rows, :].astype(F32) + own_ref[rows, :]
        total = total + arrived_ref[0, rows, :].astype(F32) + arrived_ref[1, rows, :].astype(F32)
        dq_out[rows, :] = total.T.astype(BF16)
    dk_out[...] = dk_in[...]
    dv_out[...] = dv_in[...]


def shards(queries, keys, values, outputs, d_outputs, log_norm, rand_owner, rand_local, glob_blocks):
    tokens, features = queries.shape
    blocks = tokens // BLOCK
    factor = 1.0 / math.sqrt(features // log_norm.shape[0])
    queries, keys, values, outputs, d_outputs, log_norm, owner, local, glob_blocks = (
        pltpu.with_memory_space_constraint(array, pltpu.HBM)
        for array in (
            queries, keys, values, outputs, d_outputs, log_norm, rand_owner.T, rand_local.T, glob_blocks
        )
    )
    vmem = pl.BlockSpec(memory_space=pltpu.VMEM)
    smem = pl.BlockSpec(memory_space=pltpu.SMEM)
    anywhere = pl.BlockSpec(memory_space=pl.ANY)
    hbm = pl.BlockSpec(memory_space=pltpu.HBM)
    dma = pltpu.SemaphoreType.DMA

    slices = (8, BLOCK // 2, features)
    eighths = (8, BLOCK // 16, features)
    qd, kv, nd, rf, dq_own, dk_own, dv_own, part = pl.pallas_call(
        functools.partial(gather_kernel, factor=factor),
        out_shape=(
            jax.ShapeDtypeStruct((NZ, 2, tokens, features), BF16),
            jax.ShapeDtypeStruct((NY * NC, 2, tokens, features), BF16),
            jax.ShapeDtypeStruct((NZ, blocks // 2 + 1, 8, BLOCK), F32),
            jax.ShapeDtypeStruct((NZ, 8, BLOCK), jnp.int32),
            jax.ShapeDtypeStruct((tokens, features), F32),
            jax.ShapeDtypeStruct((tokens, features), F32),
            jax.ShapeDtypeStruct((tokens, features), F32),
            jax.ShapeDtypeStruct(eighths[1:], F32),
        ),
        in_specs=[hbm] * 5 + [vmem] * 3 + [smem],
        out_specs=(anywhere,) * 2 + (vmem,) * 6,
        scratch_shapes=[
            pltpu.VMEM((tokens, features), BF16), pltpu.VMEM((tokens, features), BF16),
            pltpu.VMEM((tokens, features), BF16), pltpu.VMEM((tokens, features), BF16),
            pltpu.VMEM((tokens, features), BF16),
            pltpu.VMEM((blocks // 2 + 1, 8, BLOCK), F32), pltpu.VMEM(slices, BF16),
            pltpu.VMEM(slices, BF16), pltpu.VMEM(eighths, BF16), pltpu.VMEM(eighths, BF16),
            pltpu.VMEM(eighths[1:], BF16), pltpu.VMEM(eighths, BF16), pltpu.VMEM(eighths, BF16),
            pltpu.VMEM(slices, BF16), pltpu.VMEM(slices, F32), pltpu.VMEM(slices, F32),
            pltpu.VMEM(eighths, F32), pltpu.VMEM(eighths, F32),
            dma((2, 4, 5)), dma((2, 4, 5)), dma((2, 2, 2)), dma((2, 2, 2)),
            dma((NY, 2)), dma((NY, 2)), dma((6, 8)), dma((6, 8)), dma((10,)),
        ],
        compiler_params=pltpu.CompilerParams(collective_id=0, has_side_effects=True, vmem_limit_bytes=12 * MIB),
        name="gather",
    )(queries, d_outputs, keys, values, outputs, log_norm, owner, local, glob_blocks)

    dq_part, dkv_part = pl.pallas_call(
        functools.partial(pair_kernel, factor=factor),
        out_shape=(
            jax.ShapeDtypeStruct((NZ, tokens, features), BF16),
            jax.ShapeDtypeStruct((NY * NC, 2, tokens, features), BF16),
        ),
        in_specs=[anywhere, vmem, vmem, vmem],
        out_specs=(vmem, vmem),
        scratch_shapes=[
            pltpu.VMEM((NZ * blocks + 1, BLOCK, features), F32),
            pltpu.VMEM((NY * NC * blocks + 1, BLOCK, features), F32),
            pltpu.VMEM((NY * NC * blocks + 1, BLOCK, features), F32),
            pltpu.SMEM((NZ, 8, BLOCK), jnp.int32),
            pltpu.SMEM((256,), jnp.int32),
            dma,
        ],
        compiler_params=pltpu.CompilerParams(vmem_limit_bytes=16 * MIB),
        name="pairs",
    )(rf, qd, kv, nd)

    result = jax.ShapeDtypeStruct((tokens, features), BF16)
    arrived, dk, dv = pl.pallas_call(
        functools.partial(reduce_kernel, factor=factor),
        out_shape=(jax.ShapeDtypeStruct((2, tokens, features), BF16), result, result),
        in_specs=[vmem] * 5 + [smem],
        out_specs=(vmem,) * 3,
        scratch_shapes=[
            pltpu.VMEM((2, 4, tokens, features), BF16),
            pltpu.VMEM((2, 3, tokens, features), BF16),
            pltpu.VMEM((NY, 2, tokens, features), BF16),
            pltpu.VMEM((2, tokens, features), BF16),
            pltpu.VMEM((2, 2, tokens, features), BF16),
            pltpu.VMEM((2, 2, 2, tokens, features), BF16),
            pltpu.VMEM(eighths, F32),
            pltpu.VMEM((8,) + eighths, F32),
            dma((2, 4, 2)), dma((2, 4, 2)), dma((2, 2, 2, 2)), dma((2, 2, 2, 2)),
            dma((NY, 2, 2)), dma((NY, 2, 2)), dma((2, 8)), dma((2, 8)),
        ],
        compiler_params=pltpu.CompilerParams(collective_id=1, has_side_effects=True, vmem_limit_bytes=24 * MIB),
        name="reduce",
    )(dq_part, dkv_part, dk_own, dv_own, part, glob_blocks)

    return tuple(pl.pallas_call(
        last_kernel,
        out_shape=(result,) * 3,
        in_specs=[vmem] * 5,
        out_specs=(vmem,) * 3,
        compiler_params=pltpu.CompilerParams(vmem_limit_bytes=8 * MIB),
        name="last",
    )(dq_part, dq_own, arrived, dk, dv))


def solution(mesh):
    placed = (
        P("seq", "head"), P("seq", "head"), P("seq", "head"), P("seq", "head"), P("seq", "head"),
        P("head", "seq"), P("seq", None), P("seq", None), P(),
    )
    return jax.shard_map(
        shards,
        mesh=mesh,
        in_specs=placed,
        out_specs=(P("seq", "head"), P("seq", "head"), P("seq", "head")),
        check_vma=False,
    )
```

```python
import functools
import math

import jax
import jax.numpy as jnp
from jax import lax
from jax.experimental import pallas as pl
from jax.experimental.pallas import tpu as pltpu
from jax.sharding import PartitionSpec as P

BLOCK = 128
NY, NZ, NC = 4, 8, 2
MESH = pl.DeviceIdType.MESH
F32 = jnp.float32
BF16 = jnp.bfloat16
MIB = 1024 * 1024
STEP = 4


def place():
    seq = lax.axis_index("seq")
    core = lax.rem(seq, NC)
    z = lax.rem(seq // NC, NZ)
    y = seq // (NC * NZ)
    return y, z, core


def device(y, z, core):
    return {"seq": (y * NZ + z) * NC + core}


def per_head(x):
    lane = lax.broadcasted_iota(jnp.int32, x.shape, 1)
    zero = jnp.zeros_like(x)
    low = lane < x.shape[1] // 2
    return jnp.concatenate([jnp.where(low, x, zero), jnp.where(low, zero, x)], axis=0)


def pair_terms(q2, d2, nd, k, v, factor):
    k = k * factor
    across = (((1,), (1,)), ((), ()))
    scores = lax.dot_general(k, q2, across, preferred_element_type=F32)
    grads = lax.dot_general(v, d2, across, preferred_element_type=F32)
    norm = jnp.concatenate([nd[0:1], nd[1:2]], axis=1)
    delta = jnp.concatenate([nd[2:3], nd[3:4]], axis=1)
    weights = jnp.exp(scores - norm)
    grad_scores = weights * (grads - delta)
    weights_low = weights.astype(BF16)
    scores_low = grad_scores.astype(BF16)
    dv = jnp.dot(weights_low, d2, preferred_element_type=F32)
    dk = jnp.dot(scores_low, q2, preferred_element_type=F32)
    turned = k.T
    half = turned.shape[0] // 2
    dq = jnp.concatenate(
        [
            jnp.dot(turned[:half], scores_low[:, :BLOCK], preferred_element_type=F32),
            jnp.dot(turned[half:], scores_low[:, BLOCK:], preferred_element_type=F32),
        ],
        axis=0,
    )
    return dq, dk, dv


def query_rows(nd_tile, b):
    return jnp.where(lax.rem(b, 2) == 0, nd_tile[0:4], nd_tile[4:8])


def gather_kernel(
    q_hbm, d_hbm, k_hbm, v_hbm, o_hbm, norm_ref, owner_ref, local_ref, glob_ref,
    qd_out, kv_out, nd_out, rf_out, dq_out, dk_out, dv_out, t1,
    q_ref, d_ref, k_ref, v_ref, o_ref, nd_ref, cand_ref,
    g1in, s1, g2in, s2, g3in, s3, gkv, gacc, r1in,
    zsend, zrecv, ysend, yrecv, csend, crecv, gsend, grecv, lsem,
    *, factor,
):
    y, z, c = place()
    tokens = q_ref.shape[0]
    blocks = tokens // BLOCK
    half = BLOCK // 2
    loads = [
        pltpu.make_async_copy(source, target, lsem.at[i])
        for i, (source, target) in enumerate(
            ((k_hbm, k_ref), (v_hbm, v_ref), (o_hbm, o_ref), (d_hbm, d_ref), (q_hbm, q_ref))
        )
    ]
    for copy in loads:
        copy.start()
    zdev = [device(y, lax.rem(z + 1, NZ), c), device(y, lax.rem(z + NZ - 1, NZ), c)]
    ydev = [device(lax.rem(y + 1, NY), z, c), device(lax.rem(y + NY - 1, NY), z, c)]
    cdev = device(y, z, 1 - c)
    me = y * NC + c

    def member(offset):
        return lax.rem(me + offset, NY * NC)

    def member_device(offset):
        other = member(offset)
        return device(other // NC, z, lax.rem(other, NC))

    def row_device(offset):
        return device(y, lax.rem(z + offset, NZ), c)

    barrier = pltpu.get_barrier_semaphore()
    for offset in range(1, 8):
        for target in (member_device(offset), row_device(offset)):
            pl.semaphore_signal(barrier, inc=1, device_id=target, device_id_type=MESH)
    pl.semaphore_wait(barrier, 14)

    def zwhere(part, slot):
        if part < 4:
            return qd_out.at[slot, part // 2, pl.ds((part % 2) * tokens // 2, tokens // 2)]
        return nd_out.at[slot]

    def zown(part):
        if part < 4:
            return (q_hbm, d_hbm)[part // 2].at[pl.ds((part % 2) * tokens // 2, tokens // 2)]
        return nd_ref

    def zcopy(way, step, part):
        slot = lax.rem(z + (NZ - step + 1 if way == 0 else step - 1), NZ)
        return pltpu.make_async_remote_copy(
            src_ref=zown(part) if step == 1 else zwhere(part, slot),
            dst_ref=zwhere(part, slot),
            send_sem=zsend.at[way, step - 1, part],
            recv_sem=zrecv.at[way, step - 1, part],
            device_id=zdev[way],
            device_id_type=MESH,
        )

    def zparts(way, step):
        if step < 4:
            return (0, 1, 2, 3, 4)
        return (0, 1, 4) if way == 0 else (2, 3)

    def ycopy(way, step, part):
        row = lax.rem(y + ((NY if step == 1 else NY - 1) if way == 0 else step - 1), NY)
        slot = row * NC + c
        return pltpu.make_async_remote_copy(
            src_ref=(k_hbm, v_hbm)[part] if step == 1 else kv_out.at[slot, part],
            dst_ref=kv_out.at[slot, part],
            send_sem=ysend.at[way, step - 1, part],
            recv_sem=yrecv.at[way, step - 1, part],
            device_id=ydev[way],
            device_id_type=MESH,
        )

    def ccopy(offset, part):
        slot = lax.rem(y + offset, NY) * NC + c
        return pltpu.make_async_remote_copy(
            src_ref=(k_hbm, v_hbm)[part] if offset == 0 else kv_out.at[slot, part],
            dst_ref=kv_out.at[slot, part],
            send_sem=csend.at[offset, part],
            recv_sem=crecv.at[offset, part],
            device_id=cdev,
            device_id_type=MESH,
        )

    def small(phase, offset):
        over_column = phase in (0, 3, 4)
        other = member(offset) if over_column else lax.rem(z + offset, NZ)
        source, target = (
            (cand_ref.at[other], g1in.at[offset]),
            (s1.at[other], g2in.at[offset]),
            (s2, g3in.at[offset]),
            (gkv.at[me], gkv.at[me]),
            (gacc.at[other], r1in.at[offset]),
        )[phase]
        return pltpu.make_async_remote_copy(
            src_ref=source,
            dst_ref=target,
            send_sem=gsend.at[phase, offset],
            recv_sem=grecv.at[phase, offset],
            device_id=member_device(offset) if over_column else row_device(offset),
            device_id_type=MESH,
        )

    def small_start(phase):
        for offset in range(1, 8):
            small(phase, offset).start()

    def small_wait(phase):
        for offset in range(1, 8):
            small(phase, offset).wait_recv()

    def zstart(step, parts):
        for part in parts:
            for way in (0, 1):
                if part in zparts(way, step):
                    zcopy(way, step, part).start()

    def zpass(step, parts):
        for part in parts:
            for way in (0, 1):
                if part in zparts(way, step):
                    zcopy(way, step, part).wait_recv()
                    if step < 4 and part in zparts(way, step + 1):
                        zcopy(way, step + 1, part).start()

    def block_rows(b):
        return pl.ds(pl.multiple_of(b * BLOCK, BLOCK), BLOCK)

    def window(first, end):
        @pl.loop(first, end)
        def _(i):
            up = (i >= blocks).astype(jnp.int32)
            down = (i >= 2 * blocks - 1).astype(jnp.int32)
            low = i - up * blocks - down * (blocks - 1)
            qb = low + down
            kb = low + up - down
            rows, krows = block_rows(qb), block_rows(kb)
            dq, dk, dv = pair_terms(
                per_head(q_ref[rows, :]), per_head(d_ref[rows, :]), query_rows(nd_ref[qb // 2], qb),
                k_ref[krows, :], v_ref[krows, :], factor,
            )
            dq_out[rows, :] += dq
            dk_out[krows, :] += dk
            dv_out[krows, :] += dv

    def whole(first, end):
        @pl.loop(first, end)
        def _(i):
            b, g = i // 2, lax.rem(i, 2)
            rows = block_rows(b)
            part = 4 * g
            dq, dk, dv = pair_terms(
                per_head(q_ref[rows, :]), per_head(d_ref[rows, :]), query_rows(nd_ref[b // 2], b),
                jnp.concatenate([gkv[part], gkv[part + 1]], axis=0),
                jnp.concatenate([gkv[part + 2], gkv[part + 3]], axis=0),
                factor,
            )
            dq_out[rows, :] += dq
            gacc[part] += dk[:half]
            gacc[part + 1] += dk[half:]
            gacc[part + 2] += dv[:half]
            gacc[part + 3] += dv[half:]

    def ystep1(part):
        for way in (0, 1):
            ycopy(way, 1, part).wait_recv()
            if part == way:
                ycopy(way, 2, part).start()
            ccopy(NY - 1 if way == 0 else 1, part).start()

    zstart(1, (0,))
    loads[0].wait()
    loads[1].wait()
    seq = lax.axis_index("seq")
    for g in range(2):
        local_block = glob_ref[g] - seq * blocks
        for i, ref in enumerate((k_ref, v_ref)):
            block = jnp.zeros((BLOCK, k_ref.shape[1]), BF16)
            for b in range(blocks):
                block = jnp.where(local_block == b, ref[pl.ds(b * BLOCK, BLOCK), :], block)
            cand_ref[4 * g + 2 * i] = block[:half]
            cand_ref[4 * g + 2 * i + 1] = block[half:]
    owner = owner_ref[...]
    column = jnp.bitwise_and(owner >> 1, NZ - 1)
    other = (owner >> 4) * NC + jnp.bitwise_and(owner, 1)
    nd_ref[blocks // 2] = jnp.zeros(nd_ref.shape[1:], F32)
    nd_ref[blocks // 2, 0:3, 0:blocks] = ((column * (NY * NC) + other) * blocks + local_ref[...]).astype(F32)
    loads[2].wait()
    loads[3].wait()

    def row_values(b):
        rows = pl.ds(b * BLOCK, BLOCK)
        turned = (o_ref[rows, :].astype(F32) * d_ref[rows, :].astype(F32)).T
        nd_ref[b // 2, 4 * (b % 2) : 4 * (b % 2) + 4, :] = jnp.concatenate(
            [
                norm_ref[:, rows],
                jnp.sum(turned[: turned.shape[0] // 2], axis=0, keepdims=True),
                jnp.sum(turned[turned.shape[0] // 2 :], axis=0, keepdims=True),
            ],
            axis=0,
        )

    row_values(0)
    small_start(0)
    zstart(1, (1,))
    for part in (0, 1):
        for way in (0, 1):
            ycopy(way, 1, part).start()
        ccopy(0, part).start()
    for b in range(1, blocks):
        row_values(b)
    loads[4].wait()
    local = [
        pltpu.make_async_copy(q_ref, qd_out.at[z, 0], lsem.at[5]),
        pltpu.make_async_copy(d_ref, qd_out.at[z, 1], lsem.at[6]),
        pltpu.make_async_copy(nd_ref, nd_out.at[z], lsem.at[7]),
        pltpu.make_async_copy(k_ref, kv_out.at[me, 0], lsem.at[8]),
        pltpu.make_async_copy(v_ref, kv_out.at[me, 1], lsem.at[9]),
    ]
    for copy in local:
        copy.start()

    @pl.loop(0, blocks)
    def _(b):
        zero = jnp.zeros((BLOCK, q_ref.shape[1]), F32)
        dq_out[block_rows(b), :] = zero
        dk_out[block_rows(b), :] = zero
        dv_out[block_rows(b), :] = zero
        gacc[b] = zero[:half]

    small_wait(0)
    slice_sum = cand_ref[me].astype(F32)
    for offset in range(1, 8):
        slice_sum = slice_sum + g1in[offset].astype(F32)
    s1[...] = slice_sum.astype(BF16).reshape(s1.shape)
    window(0, 2)
    small_start(1)
    zstart(1, (4, 2, 3))
    window(2, 4)
    zpass(1, (0,))
    window(4, 5)
    small_wait(1)
    part_sum = s1[z].astype(F32)
    for offset in range(1, 8):
        part_sum = part_sum + g2in[offset].astype(F32)
    s2[...] = part_sum.astype(BF16)
    window(5, 6)
    small_start(2)
    zpass(1, (1, 4))
    ystep1(0)
    window(6, 9)
    zpass(1, (2,))
    window(9, 10)
    zpass(1, (3,))
    ystep1(1)
    window(10, 11)
    zpass(2, (0,))
    small_wait(2)
    s3[z] = s2[...]
    for offset in range(1, 8):
        s3[lax.rem(z + NZ - offset, NZ)] = g3in[offset]
    gkv[me] = s3[...].reshape(gkv.shape[1:])
    window(11, 12)
    small_start(3)
    zpass(2, (1, 4))
    window(12, 16)
    zpass(2, (2,))
    for way in (0, 1):
        ycopy(way, 2, way).wait_recv()
        ccopy(2, way).start()
    small_wait(3)
    whole(0, 4)
    zpass(2, (3,))
    whole(4, 10)
    zpass(3, (0,))
    whole(10, 16)
    window(16, 17)
    small_start(4)
    zpass(3, (1, 4))
    window(17, 20)
    small_wait(4)
    slice_sum = gacc[me]
    for offset in range(1, 8):
        slice_sum = slice_sum + r1in[offset]
    t1[...] = slice_sum.reshape(t1.shape)
    zpass(3, (2,))
    window(20, 22)
    zpass(3, (3,))
    zpass(4, (0, 2, 1, 4, 3))
    for offset in range(NY):
        for part in (0, 1):
            ccopy(offset, part).wait()
    for way in (0, 1):
        for step in range(1, 5):
            for part in zparts(way, step):
                zcopy(way, step, part).wait_send()
        for part in (0, 1):
            ycopy(way, 1, part).wait_send()
        ycopy(way, 2, way).wait_send()
    for phase in range(5):
        for offset in range(1, 8):
            small(phase, offset).wait_send()
    for copy in local:
        copy.wait()
    for slot in range(NZ):
        rf_out[slot] = nd_out[slot, blocks // 2].astype(jnp.int32)


def pair_kernel(
    rf_any, qd_ref, kv_ref, nd_ref, dq_out, dkv_out, dq_acc, dk_acc, dv_acc, rf_ref, list_ref, sem,
    *, factor,
):
    y, z, c = place()
    blocks = qd_ref.shape[2] // BLOCK
    grid = NZ * blocks
    refs = pltpu.make_async_copy(rf_any, rf_ref, sem)
    refs.start()

    def window_item(n, slot, b, seq, key_block, wanted):
        member = (seq // (NC * NZ)) * NC + lax.rem(seq, NC)
        list_ref[n] = ((slot * blocks + b) << 8) | ((member * blocks + key_block) << 1)
        return n + wanted.astype(jnp.int32)

    seq = (y * NZ + z) * NC + c
    nearby = jnp.where(c == 0, seq + 1, seq - 1)
    count = window_item(
        jnp.int32(0), z, jnp.where(c == 0, blocks - 1, 0), nearby, jnp.where(c == 0, 0, blocks - 1), seq >= 0
    )
    far_slot = jnp.where(c == 0, lax.rem(z + 1, NZ), lax.rem(z + NZ - 1, NZ))
    far_seq = (y * NZ + far_slot) * NC + c
    far_key = jnp.where(c == 0, far_seq - 1, far_seq + 1)
    inside = jnp.logical_and(far_key >= 0, far_key < NY * NZ * NC)
    count = window_item(
        count, far_slot, jnp.where(c == 0, 0, blocks - 1),
        jnp.clip(far_key, 0, NY * NZ * NC - 1), jnp.where(c == 0, blocks - 1, 0), inside,
    )

    refs.wait()

    def per_slot(slot, n):
        zero = jnp.zeros((BLOCK, qd_ref.shape[3]), F32)
        for b in range(blocks):
            dq_acc[slot * blocks + b] = zero
            dk_acc[slot * blocks + b] = zero
            dv_acc[slot * blocks + b] = zero
            for r in range(3):
                code = rf_ref[slot, r, b]
                list_ref[n] = ((slot * blocks + b) << 8) | ((code & (grid - 1)) << 1)
                n = n + ((code >> 6) == z).astype(jnp.int32)
        return n

    count = lax.fori_loop(0, NZ, per_slot, count)
    for i in range(STEP - 1):
        list_ref[count + i] = jnp.int32(1)

    def terms(item):
        query, key = item >> 8, (item >> 1) & (grid - 1)
        qs, qb = query >> 3, query & (blocks - 1)
        ks, kb = key >> 3, key & (blocks - 1)
        qrows = pl.ds(pl.multiple_of(qb * BLOCK, BLOCK), BLOCK)
        krows = pl.ds(pl.multiple_of(kb * BLOCK, BLOCK), BLOCK)
        return pair_terms(
            per_head(qd_ref[qs, 0, qrows, :]),
            per_head(qd_ref[qs, 1, qrows, :]),
            query_rows(nd_ref[qs, qb >> 1], qb),
            kv_ref[ks, 0, krows, :],
            kv_ref[ks, 1, krows, :],
            factor,
        )

    @pl.loop(0, (count + STEP - 1) // STEP)
    def _(i):
        items = [list_ref[STEP * i + j] for j in range(STEP)]
        sums = [terms(item) for item in items]
        for item, (dq, dk, dv) in zip(items, sums):
            spare = (item & 1) * grid
            dq_acc[(item >> 8) + spare] += dq
            dk_acc[((item >> 1) & (grid - 1)) + spare] += dk
            dv_acc[((item >> 1) & (grid - 1)) + spare] += dv

    @pl.loop(0, grid)
    def _(i):
        slot = i >> 3
        rows = pl.ds(pl.multiple_of((i & (blocks - 1)) * BLOCK, BLOCK), BLOCK)
        dq_out[slot, rows, :] = dq_acc[i].astype(BF16)
        dkv_out[slot, 0, rows, :] = (dk_acc[i] * factor).astype(BF16)
        dkv_out[slot, 1, rows, :] = dv_acc[i].astype(BF16)


def reduce_kernel(
    dq_in, dkv_in, dk_own, dv_own, part_in, glob_ref, dq_out, dk_out, dv_out,
    zbuf, zin, cin, ysum, ybuf, yin, r2in, t2, rin, totals,
    zsend, zrecv, ysend, yrecv, csend, crecv, gsend, grecv,
    *, factor,
):
    y, z, c = place()
    half = dk_out.shape[0] // 2
    me = y * NC + c
    zdev = [device(y, lax.rem(z + 1, NZ), c), device(y, lax.rem(z + NZ - 1, NZ), c)]
    ydev = [device(lax.rem(y + 1, NY), z, c), device(lax.rem(y + NY - 1, NY), z, c)]
    cdev = device(y, z, 1 - c)

    def member_device(offset):
        other = lax.rem(me + offset, NY * NC)
        return device(other // NC, z, lax.rem(other, NC))

    def row_device(offset):
        return device(y, lax.rem(z + offset, NZ), c)

    barrier = pltpu.get_barrier_semaphore()
    for offset in range(1, 8):
        for target in (member_device(offset), row_device(offset)):
            pl.semaphore_signal(barrier, inc=1, device_id=target, device_id_type=MESH)
    pl.semaphore_wait(barrier, 14)

    def halves(part):
        return pl.ds(part * half, half)

    def zparts(way, step):
        return (way,) if step == 1 else (1 - way, way)

    def zplain(way, step, part):
        return step == 1 or (step == 2 and part != way)

    def ztarget(way, step):
        return lax.rem(z + (5 - step if way == 0 else NZ - 5 + step), NZ)

    def zcopy(way, step, part):
        if zplain(way, step, part):
            source = dq_in.at[ztarget(way, step), halves(part)]
        else:
            source = zbuf.at[way, step - 1, halves(part)]
        return pltpu.make_async_remote_copy(
            src_ref=source,
            dst_ref=dq_out.at[way, halves(part)] if step == 4 else zin.at[way, step - 1, halves(part)],
            send_sem=zsend.at[way, step - 1, part],
            recv_sem=zrecv.at[way, step - 1, part],
            device_id=zdev[way],
            device_id_type=MESH,
        )

    def ccopy(offset, part, h):
        row = lax.rem(y + offset, NY)
        return pltpu.make_async_remote_copy(
            src_ref=dkv_in.at[row * NC + 1 - c, part, halves(h)],
            dst_ref=cin.at[offset, part, halves(h)],
            send_sem=csend.at[offset, part, h],
            recv_sem=crecv.at[offset, part, h],
            device_id=cdev,
            device_id_type=MESH,
        )

    def ycopy(way, step, part, h):
        return pltpu.make_async_remote_copy(
            src_ref=ysum.at[part, halves(h)] if step == 1 else ybuf.at[way, part, halves(h)],
            dst_ref=yin.at[way, step - 1, part, halves(h)],
            send_sem=ysend.at[way, step - 1, part, h],
            recv_sem=yrecv.at[way, step - 1, part, h],
            device_id=ydev[way],
            device_id_type=MESH,
        )

    def small(phase, offset):
        source, target = (
            (part_in.at[lax.rem(z + offset, NZ)], r2in.at[offset]),
            (t2, rin.at[offset]),
            (totals.at[me], totals.at[me]),
        )[phase]
        return pltpu.make_async_remote_copy(
            src_ref=source,
            dst_ref=target,
            send_sem=gsend.at[phase, offset],
            recv_sem=grecv.at[phase, offset],
            device_id=row_device(offset) if phase < 2 else member_device(offset),
            device_id_type=MESH,
        )

    for h in (0, 1):
        for part in (0, 1):
            ccopy(2, part, h).start()
    for way in (0, 1):
        zcopy(way, 1, way).start()
    for offset in range(1, 8):
        small(0, offset).start()
    for way in (0, 1):
        zcopy(way, 2, 1 - way).start()
    for h in (0, 1):
        for way in (0, 1):
            ccopy(1 if way == 0 else 3, 1 - way, h).start()
    for h in (0, 1):
        for way in (0, 1):
            ccopy(1 if way == 0 else 3, way, h).start()
    for h in (0, 1):
        for part in (0, 1):
            ccopy(0, part, h).start()

    def zround(step, late):
        for way in (0, 1):
            part = way if late else 1 - way
            zcopy(way, step, part).wait_recv()
            rows = halves(part)
            mine = dq_in[ztarget(way, step + 1), rows, :].astype(F32)
            zbuf[way, step, rows, :] = (mine + zin[way, step - 1, rows, :].astype(F32)).astype(BF16)
            zcopy(way, step + 1, part).start()

    def cadd(offset, part, h):
        ccopy(offset, part, h).wait_recv()
        row = lax.rem(y + offset, NY)
        return dkv_in[row * NC + c, part, halves(h), :].astype(F32) + cin[offset, part, halves(h), :].astype(F32)

    def ypass(way, part, h):
        total = cadd(1 if way == 0 else 3, part, h)
        if part == way:
            ycopy(way, 1, part, h).wait_recv()
            total = total + yin[way, 0, part, halves(h), :].astype(F32)
        ybuf[way, part, halves(h), :] = total.astype(BF16)
        ycopy(way, 2, part, h).start()

    for h in (0, 1):
        for part in (0, 1):
            ysum[part, halves(h), :] = cadd(2, part, h).astype(BF16)
            ycopy(part, 1, part, h).start()
    ypass(0, 1, 0)
    ypass(1, 0, 0)
    zround(1, True)
    for offset in range(1, 8):
        small(0, offset).wait_recv()
    total = part_in[z]
    for offset in range(1, 8):
        total = total + r2in[offset]
    t2[...] = total
    ypass(0, 1, 1)
    ypass(1, 0, 1)
    for offset in range(1, 8):
        small(1, offset).start()
    ypass(0, 0, 0)
    ypass(1, 1, 0)
    zround(2, False)
    zround(2, True)
    ypass(0, 0, 1)
    ypass(1, 1, 1)
    for offset in range(1, 8):
        small(1, offset).wait_recv()
    totals[me, z] = t2[...]
    for offset in range(1, 8):
        totals[me, lax.rem(z + NZ - offset, NZ)] = rin[offset]
    zround(3, False)
    for offset in range(1, 8):
        small(2, offset).start()
    zround(3, True)
    for offset in range(1, 8):
        small(2, offset).wait_recv()
    seq = lax.axis_index("seq")
    per_half = half // BLOCK
    for part, out, own in ((1, dv_out, dv_own), (0, dk_out, dk_own)):
        for h in (0, 1):
            total = cadd(0, part, h)
            for way in (0, 1):
                ycopy(way, 2, part, h).wait_recv()
                total = total + yin[way, 1, part, halves(h), :].astype(F32)
            for i in range(per_half):
                b = h * per_half + i
                rows = pl.ds(b * BLOCK, BLOCK)
                more = own[rows, :]
                for g in range(2):
                    whole = totals[pl.ds(4 * g + 2 * part, 2)].reshape(more.shape)
                    more = more + jnp.where(glob_ref[g] == seq * 2 * per_half + b, whole, jnp.zeros_like(whole))
                if part == 0:
                    more = more * factor
                out[rows, :] = (total[i * BLOCK : (i + 1) * BLOCK] + more).astype(BF16)
    for part in (0, 1):
        for way in (0, 1):
            zcopy(way, 4, part).wait_recv()
    for way in (0, 1):
        for step in range(1, 5):
            for part in zparts(way, step):
                zcopy(way, step, part).wait_send()
        for h in (0, 1):
            ycopy(way, 1, way, h).wait_send()
            for part in (0, 1):
                ycopy(way, 2, part, h).wait_send()
    for offset in range(NY):
        for part in (0, 1):
            for h in (0, 1):
                ccopy(offset, part, h).wait_send()
    for phase in range(3):
        for offset in range(1, 8):
            small(phase, offset).wait_send()


def last_kernel(part_ref, own_ref, arrived_ref, dk_in, dv_in, dq_out, dk_out, dv_out):
    y, z, c = place()
    for b in range(own_ref.shape[0] // BLOCK):
        rows = pl.ds(b * BLOCK, BLOCK)
        total = part_ref[z, rows, :].astype(F32) + own_ref[rows, :]
        total = total + arrived_ref[0, rows, :].astype(F32) + arrived_ref[1, rows, :].astype(F32)
        dq_out[rows, :] = total.T.astype(BF16)
    dk_out[...] = dk_in[...]
    dv_out[...] = dv_in[...]


def shards(queries, keys, values, outputs, d_outputs, log_norm, rand_owner, rand_local, glob_blocks):
    tokens, features = queries.shape
    blocks = tokens // BLOCK
    factor = 1.0 / math.sqrt(features // log_norm.shape[0])
    queries, keys, values, outputs, d_outputs, log_norm, owner, local, glob_blocks = (
        pltpu.with_memory_space_constraint(array, pltpu.HBM)
        for array in (
            queries, keys, values, outputs, d_outputs, log_norm, rand_owner.T, rand_local.T, glob_blocks
        )
    )
    vmem = pl.BlockSpec(memory_space=pltpu.VMEM)
    smem = pl.BlockSpec(memory_space=pltpu.SMEM)
    anywhere = pl.BlockSpec(memory_space=pl.ANY)
    hbm = pl.BlockSpec(memory_space=pltpu.HBM)
    dma = pltpu.SemaphoreType.DMA

    slices = (8, BLOCK // 2, features)
    eighths = (8, BLOCK // 16, features)
    qd, kv, nd, rf, dq_own, dk_own, dv_own, part = pl.pallas_call(
        functools.partial(gather_kernel, factor=factor),
        out_shape=(
            jax.ShapeDtypeStruct((NZ, 2, tokens, features), BF16),
            jax.ShapeDtypeStruct((NY * NC, 2, tokens, features), BF16),
            jax.ShapeDtypeStruct((NZ, blocks // 2 + 1, 8, BLOCK), F32),
            jax.ShapeDtypeStruct((NZ, 8, BLOCK), jnp.int32),
            jax.ShapeDtypeStruct((tokens, features), F32),
            jax.ShapeDtypeStruct((tokens, features), F32),
            jax.ShapeDtypeStruct((tokens, features), F32),
            jax.ShapeDtypeStruct(eighths, F32),
        ),
        in_specs=[hbm] * 5 + [vmem] * 3 + [smem],
        out_specs=(anywhere,) * 2 + (vmem,) * 6,
        scratch_shapes=[
            pltpu.VMEM((tokens, features), BF16), pltpu.VMEM((tokens, features), BF16),
            pltpu.VMEM((tokens, features), BF16), pltpu.VMEM((tokens, features), BF16),
            pltpu.VMEM((tokens, features), BF16),
            pltpu.VMEM((blocks // 2 + 1, 8, BLOCK), F32), pltpu.VMEM(slices, BF16),
            pltpu.VMEM(slices, BF16), pltpu.VMEM(eighths, BF16), pltpu.VMEM(eighths, BF16),
            pltpu.VMEM(eighths[1:], BF16), pltpu.VMEM(eighths, BF16), pltpu.VMEM(eighths, BF16),
            pltpu.VMEM(slices, BF16), pltpu.VMEM(slices, F32), pltpu.VMEM(slices, F32),
            dma((2, 4, 5)), dma((2, 4, 5)), dma((2, 2, 2)), dma((2, 2, 2)),
            dma((NY, 2)), dma((NY, 2)), dma((5, 8)), dma((5, 8)), dma((10,)),
        ],
        compiler_params=pltpu.CompilerParams(collective_id=0, has_side_effects=True, vmem_limit_bytes=12 * MIB),
        name="gather",
    )(queries, d_outputs, keys, values, outputs, log_norm, owner, local, glob_blocks)

    dq_part, dkv_part = pl.pallas_call(
        functools.partial(pair_kernel, factor=factor),
        out_shape=(
            jax.ShapeDtypeStruct((NZ, tokens, features), BF16),
            jax.ShapeDtypeStruct((NY * NC, 2, tokens, features), BF16),
        ),
        in_specs=[anywhere, vmem, vmem, vmem],
        out_specs=(vmem, vmem),
        scratch_shapes=[
            pltpu.VMEM((NZ * blocks + 1, BLOCK, features), F32),
            pltpu.VMEM((NY * NC * blocks + 1, BLOCK, features), F32),
            pltpu.VMEM((NY * NC * blocks + 1, BLOCK, features), F32),
            pltpu.SMEM((NZ, 8, BLOCK), jnp.int32),
            pltpu.SMEM((256,), jnp.int32),
            dma,
        ],
        compiler_params=pltpu.CompilerParams(vmem_limit_bytes=16 * MIB),
        name="pairs",
    )(rf, qd, kv, nd)

    result = jax.ShapeDtypeStruct((tokens, features), BF16)
    arrived, dk, dv = pl.pallas_call(
        functools.partial(reduce_kernel, factor=factor),
        out_shape=(jax.ShapeDtypeStruct((2, tokens, features), BF16), result, result),
        in_specs=[vmem] * 5 + [smem],
        out_specs=(vmem,) * 3,
        scratch_shapes=[
            pltpu.VMEM((2, 4, tokens, features), BF16),
            pltpu.VMEM((2, 3, tokens, features), BF16),
            pltpu.VMEM((NY, 2, tokens, features), BF16),
            pltpu.VMEM((2, tokens, features), BF16),
            pltpu.VMEM((2, 2, tokens, features), BF16),
            pltpu.VMEM((2, 2, 2, tokens, features), BF16),
            pltpu.VMEM(eighths, F32),
            pltpu.VMEM(eighths[1:], F32),
            pltpu.VMEM(eighths, F32),
            pltpu.VMEM((8,) + eighths, F32),
            dma((2, 4, 2)), dma((2, 4, 2)), dma((2, 2, 2, 2)), dma((2, 2, 2, 2)),
            dma((NY, 2, 2)), dma((NY, 2, 2)), dma((3, 8)), dma((3, 8)),
        ],
        compiler_params=pltpu.CompilerParams(collective_id=1, has_side_effects=True, vmem_limit_bytes=24 * MIB),
        name="reduce",
    )(dq_part, dkv_part, dk_own, dv_own, part, glob_blocks)

    return tuple(pl.pallas_call(
        last_kernel,
        out_shape=(result,) * 3,
        in_specs=[vmem] * 5,
        out_specs=(vmem,) * 3,
        compiler_params=pltpu.CompilerParams(vmem_limit_bytes=8 * MIB),
        name="last",
    )(dq_part, dq_own, arrived, dk, dv))


def solution(mesh):
    placed = (
        P("seq", "head"), P("seq", "head"), P("seq", "head"), P("seq", "head"), P("seq", "head"),
        P("head", "seq"), P("seq", None), P("seq", None), P(),
    )
    return jax.shard_map(
        shards,
        mesh=mesh,
        in_specs=placed,
        out_specs=(P("seq", "head"), P("seq", "head"), P("seq", "head")),
        check_vma=False,
    )
```

```python
import functools
import math

import jax
import jax.numpy as jnp
from jax import lax
from jax.experimental import pallas as pl
from jax.experimental.pallas import tpu as pltpu
from jax.sharding import PartitionSpec as P

BLOCK = 128
NY, NZ, NC = 4, 8, 2
MESH = pl.DeviceIdType.MESH
F32 = jnp.float32
BF16 = jnp.bfloat16
MIB = 1024 * 1024
STEP = 4


def place():
    seq = lax.axis_index("seq")
    core = lax.rem(seq, NC)
    z = lax.rem(seq // NC, NZ)
    y = seq // (NC * NZ)
    return y, z, core


def device(y, z, core):
    return {"seq": (y * NZ + z) * NC + core}


def per_head(x):
    lane = lax.broadcasted_iota(jnp.int32, x.shape, 1)
    zero = jnp.zeros_like(x)
    low = lane < x.shape[1] // 2
    return jnp.concatenate([jnp.where(low, x, zero), jnp.where(low, zero, x)], axis=0)


def pair_terms(q2, d2, nd, k, v, factor):
    k = k * factor
    across = (((1,), (1,)), ((), ()))
    scores = lax.dot_general(k, q2, across, preferred_element_type=F32)
    grads = lax.dot_general(v, d2, across, preferred_element_type=F32)
    norm = jnp.concatenate([nd[0:1], nd[1:2]], axis=1)
    delta = jnp.concatenate([nd[2:3], nd[3:4]], axis=1)
    weights = jnp.exp(scores - norm)
    grad_scores = weights * (grads - delta)
    weights_low = weights.astype(BF16)
    scores_low = grad_scores.astype(BF16)
    dv = jnp.dot(weights_low, d2, preferred_element_type=F32)
    dk = jnp.dot(scores_low, q2, preferred_element_type=F32)
    turned = k.T
    half = turned.shape[0] // 2
    dq = jnp.concatenate(
        [
            jnp.dot(turned[:half], scores_low[:, :BLOCK], preferred_element_type=F32),
            jnp.dot(turned[half:], scores_low[:, BLOCK:], preferred_element_type=F32),
        ],
        axis=0,
    )
    return dq, dk, dv


def query_rows(nd_tile, b):
    return jnp.where(lax.rem(b, 2) == 0, nd_tile[0:4], nd_tile[4:8])


def gather_kernel(
    q_hbm, d_hbm, k_hbm, v_hbm, o_hbm, norm_ref, owner_ref, local_ref, glob_ref,
    qd_out, kv_out, nd_out, rf_out, dq_out, dk_out, dv_out, t1,
    q_ref, d_ref, k_ref, v_ref, o_ref, nd_ref, cand_ref,
    g1in, s1, g2in, s2, g3in, s3, gkv, gacc, r1in,
    zsend, zrecv, ysend, yrecv, csend, crecv, gsend, grecv, lsem,
    *, factor,
):
    y, z, c = place()
    tokens = q_ref.shape[0]
    blocks = tokens // BLOCK
    half = BLOCK // 2
    loads = [
        pltpu.make_async_copy(source, target, lsem.at[i])
        for i, (source, target) in enumerate(
            ((k_hbm, k_ref), (v_hbm, v_ref), (o_hbm, o_ref), (d_hbm, d_ref), (q_hbm, q_ref))
        )
    ]
    for copy in loads:
        copy.start()
    zdev = [device(y, lax.rem(z + 1, NZ), c), device(y, lax.rem(z + NZ - 1, NZ), c)]
    ydev = [device(lax.rem(y + 1, NY), z, c), device(lax.rem(y + NY - 1, NY), z, c)]
    cdev = device(y, z, 1 - c)
    me = y * NC + c

    def member(offset):
        return lax.rem(me + offset, NY * NC)

    def member_device(offset):
        other = member(offset)
        return device(other // NC, z, lax.rem(other, NC))

    def row_device(offset):
        return device(y, lax.rem(z + offset, NZ), c)

    barrier = pltpu.get_barrier_semaphore()
    for offset in range(1, 8):
        for target in (member_device(offset), row_device(offset)):
            pl.semaphore_signal(barrier, inc=1, device_id=target, device_id_type=MESH)
    pl.semaphore_wait(barrier, 14)

    def zwhere(part, slot):
        if part < 4:
            return qd_out.at[slot, part // 2, pl.ds((part % 2) * tokens // 2, tokens // 2)]
        return nd_out.at[slot]

    def zown(part):
        if part < 4:
            return (q_hbm, d_hbm)[part // 2].at[pl.ds((part % 2) * tokens // 2, tokens // 2)]
        return nd_ref

    def zcopy(way, step, part):
        slot = lax.rem(z + (NZ - step + 1 if way == 0 else step - 1), NZ)
        return pltpu.make_async_remote_copy(
            src_ref=zown(part) if step == 1 else zwhere(part, slot),
            dst_ref=zwhere(part, slot),
            send_sem=zsend.at[way, step - 1, part],
            recv_sem=zrecv.at[way, step - 1, part],
            device_id=zdev[way],
            device_id_type=MESH,
        )

    def zparts(way, step):
        if step < 4:
            return (0, 1, 2, 3, 4)
        return (0, 1, 4) if way == 0 else (2, 3)

    def ycopy(way, step, part):
        row = lax.rem(y + ((NY if step == 1 else NY - 1) if way == 0 else step - 1), NY)
        slot = row * NC + c
        return pltpu.make_async_remote_copy(
            src_ref=(k_hbm, v_hbm)[part] if step == 1 else kv_out.at[slot, part],
            dst_ref=kv_out.at[slot, part],
            send_sem=ysend.at[way, step - 1, part],
            recv_sem=yrecv.at[way, step - 1, part],
            device_id=ydev[way],
            device_id_type=MESH,
        )

    def ccopy(offset, part):
        slot = lax.rem(y + offset, NY) * NC + c
        return pltpu.make_async_remote_copy(
            src_ref=(k_hbm, v_hbm)[part] if offset == 0 else kv_out.at[slot, part],
            dst_ref=kv_out.at[slot, part],
            send_sem=csend.at[offset, part],
            recv_sem=crecv.at[offset, part],
            device_id=cdev,
            device_id_type=MESH,
        )

    def small(phase, offset):
        over_column = phase in (0, 3, 4)
        other = member(offset) if over_column else lax.rem(z + offset, NZ)
        source, target = (
            (cand_ref.at[other], g1in.at[offset]),
            (s1.at[other], g2in.at[offset]),
            (s2, g3in.at[offset]),
            (gkv.at[me], gkv.at[me]),
            (gacc.at[other], r1in.at[offset]),
        )[phase]
        return pltpu.make_async_remote_copy(
            src_ref=source,
            dst_ref=target,
            send_sem=gsend.at[phase, offset],
            recv_sem=grecv.at[phase, offset],
            device_id=member_device(offset) if over_column else row_device(offset),
            device_id_type=MESH,
        )

    def small_start(phase):
        for offset in range(1, 8):
            small(phase, offset).start()

    def small_wait(phase):
        for offset in range(1, 8):
            small(phase, offset).wait_recv()

    def zstart(step, parts):
        for part in parts:
            for way in (0, 1):
                if part in zparts(way, step):
                    zcopy(way, step, part).start()

    def zpass(step, parts):
        for part in parts:
            for way in (0, 1):
                if part in zparts(way, step):
                    zcopy(way, step, part).wait_recv()
                    if step < 4 and part in zparts(way, step + 1):
                        zcopy(way, step + 1, part).start()

    def block_rows(b):
        return pl.ds(pl.multiple_of(b * BLOCK, BLOCK), BLOCK)

    def window(first, end):
        @pl.loop(first, end)
        def _(i):
            up = (i >= blocks).astype(jnp.int32)
            down = (i >= 2 * blocks - 1).astype(jnp.int32)
            low = i - up * blocks - down * (blocks - 1)
            qb = low + down
            kb = low + up - down
            rows, krows = block_rows(qb), block_rows(kb)
            dq, dk, dv = pair_terms(
                per_head(q_ref[rows, :]), per_head(d_ref[rows, :]), query_rows(nd_ref[qb // 2], qb),
                k_ref[krows, :], v_ref[krows, :], factor,
            )
            dq_out[rows, :] += dq
            dk_out[krows, :] += dk
            dv_out[krows, :] += dv

    def whole(first, end):
        @pl.loop(first, end)
        def _(i):
            b, g = i // 2, lax.rem(i, 2)
            rows = block_rows(b)
            part = 4 * g
            dq, dk, dv = pair_terms(
                per_head(q_ref[rows, :]), per_head(d_ref[rows, :]), query_rows(nd_ref[b // 2], b),
                jnp.concatenate([gkv[part], gkv[part + 1]], axis=0),
                jnp.concatenate([gkv[part + 2], gkv[part + 3]], axis=0),
                factor,
            )
            dq_out[rows, :] += dq
            gacc[part] += dk[:half]
            gacc[part + 1] += dk[half:]
            gacc[part + 2] += dv[:half]
            gacc[part + 3] += dv[half:]

    def ystep1(part):
        for way in (0, 1):
            ycopy(way, 1, part).wait_recv()
            if part == way:
                ycopy(way, 2, part).start()
            ccopy(NY - 1 if way == 0 else 1, part).start()

    zstart(1, (0,))
    loads[0].wait()
    loads[1].wait()
    seq = lax.axis_index("seq")
    for g in range(2):
        local_block = glob_ref[g] - seq * blocks
        for i, ref in enumerate((k_ref, v_ref)):
            block = jnp.zeros((BLOCK, k_ref.shape[1]), BF16)
            for b in range(blocks):
                block = jnp.where(local_block == b, ref[pl.ds(b * BLOCK, BLOCK), :], block)
            cand_ref[4 * g + 2 * i] = block[:half]
            cand_ref[4 * g + 2 * i + 1] = block[half:]
    owner = owner_ref[...]
    column = jnp.bitwise_and(owner >> 1, NZ - 1)
    other = (owner >> 4) * NC + jnp.bitwise_and(owner, 1)
    nd_ref[blocks // 2] = jnp.zeros(nd_ref.shape[1:], F32)
    nd_ref[blocks // 2, 0:3, 0:blocks] = ((column * (NY * NC) + other) * blocks + local_ref[...]).astype(F32)
    loads[2].wait()
    loads[3].wait()

    def row_values(b):
        rows = pl.ds(b * BLOCK, BLOCK)
        turned = (o_ref[rows, :].astype(F32) * d_ref[rows, :].astype(F32)).T
        nd_ref[b // 2, 4 * (b % 2) : 4 * (b % 2) + 4, :] = jnp.concatenate(
            [
                norm_ref[:, rows],
                jnp.sum(turned[: turned.shape[0] // 2], axis=0, keepdims=True),
                jnp.sum(turned[turned.shape[0] // 2 :], axis=0, keepdims=True),
            ],
            axis=0,
        )

    row_values(0)
    small_start(0)
    zstart(1, (1,))
    for part in (0, 1):
        for way in (0, 1):
            ycopy(way, 1, part).start()
        ccopy(0, part).start()
    for b in range(1, blocks):
        row_values(b)
    loads[4].wait()
    local = [
        pltpu.make_async_copy(q_ref, qd_out.at[z, 0], lsem.at[5]),
        pltpu.make_async_copy(d_ref, qd_out.at[z, 1], lsem.at[6]),
        pltpu.make_async_copy(nd_ref, nd_out.at[z], lsem.at[7]),
        pltpu.make_async_copy(k_ref, kv_out.at[me, 0], lsem.at[8]),
        pltpu.make_async_copy(v_ref, kv_out.at[me, 1], lsem.at[9]),
    ]
    for copy in local:
        copy.start()

    @pl.loop(0, blocks)
    def _(b):
        zero = jnp.zeros((BLOCK, q_ref.shape[1]), F32)
        dq_out[block_rows(b), :] = zero
        dk_out[block_rows(b), :] = zero
        dv_out[block_rows(b), :] = zero
        gacc[b] = zero[:half]

    small_wait(0)
    slice_sum = cand_ref[me].astype(F32)
    for offset in range(1, 8):
        slice_sum = slice_sum + g1in[offset].astype(F32)
    s1[...] = slice_sum.astype(BF16).reshape(s1.shape)
    window(0, 2)
    small_start(1)
    zstart(1, (4, 2, 3))
    window(2, 4)
    zpass(1, (0,))
    window(4, 5)
    small_wait(1)
    part_sum = s1[z].astype(F32)
    for offset in range(1, 8):
        part_sum = part_sum + g2in[offset].astype(F32)
    s2[...] = part_sum.astype(BF16)
    window(5, 6)
    small_start(2)
    zpass(1, (1, 4))
    ystep1(0)
    window(6, 9)
    zpass(1, (2,))
    window(9, 10)
    zpass(1, (3,))
    ystep1(1)
    window(10, 11)
    zpass(2, (0,))
    small_wait(2)
    s3[z] = s2[...]
    for offset in range(1, 8):
        s3[lax.rem(z + NZ - offset, NZ)] = g3in[offset]
    gkv[me] = s3[...].reshape(gkv.shape[1:])
    window(11, 12)
    small_start(3)
    zpass(2, (1, 4))
    window(12, 16)
    zpass(2, (2,))
    for way in (0, 1):
        ycopy(way, 2, way).wait_recv()
        ccopy(2, way).start()
    small_wait(3)
    whole(0, 4)
    zpass(2, (3,))
    whole(4, 10)
    zpass(3, (0,))
    whole(10, 16)
    window(16, 17)
    small_start(4)
    zpass(3, (1, 4))
    window(17, 20)
    small_wait(4)
    slice_sum = gacc[me]
    for offset in range(1, 8):
        slice_sum = slice_sum + r1in[offset]
    t1[...] = slice_sum.astype(BF16).reshape(t1.shape)
    zpass(3, (2,))
    window(20, 22)
    zpass(3, (3,))
    zpass(4, (0, 2, 1, 4, 3))
    for offset in range(NY):
        for part in (0, 1):
            ccopy(offset, part).wait()
    for way in (0, 1):
        for step in range(1, 5):
            for part in zparts(way, step):
                zcopy(way, step, part).wait_send()
        for part in (0, 1):
            ycopy(way, 1, part).wait_send()
        ycopy(way, 2, way).wait_send()
    for phase in range(5):
        for offset in range(1, 8):
            small(phase, offset).wait_send()
    for copy in local:
        copy.wait()
    for slot in range(NZ):
        rf_out[slot] = nd_out[slot, blocks // 2].astype(jnp.int32)


def pair_kernel(
    rf_any, qd_ref, kv_ref, nd_ref, dq_out, dkv_out, dq_acc, dk_acc, dv_acc, rf_ref, list_ref, sem,
    *, factor,
):
    y, z, c = place()
    blocks = qd_ref.shape[2] // BLOCK
    grid = NZ * blocks
    refs = pltpu.make_async_copy(rf_any, rf_ref, sem)
    refs.start()

    def window_item(n, slot, b, seq, key_block, wanted):
        member = (seq // (NC * NZ)) * NC + lax.rem(seq, NC)
        list_ref[n] = ((slot * blocks + b) << 8) | ((member * blocks + key_block) << 1)
        return n + wanted.astype(jnp.int32)

    seq = (y * NZ + z) * NC + c
    nearby = jnp.where(c == 0, seq + 1, seq - 1)
    count = window_item(
        jnp.int32(0), z, jnp.where(c == 0, blocks - 1, 0), nearby, jnp.where(c == 0, 0, blocks - 1), seq >= 0
    )
    far_slot = jnp.where(c == 0, lax.rem(z + 1, NZ), lax.rem(z + NZ - 1, NZ))
    far_seq = (y * NZ + far_slot) * NC + c
    far_key = jnp.where(c == 0, far_seq - 1, far_seq + 1)
    inside = jnp.logical_and(far_key >= 0, far_key < NY * NZ * NC)
    count = window_item(
        count, far_slot, jnp.where(c == 0, 0, blocks - 1),
        jnp.clip(far_key, 0, NY * NZ * NC - 1), jnp.where(c == 0, blocks - 1, 0), inside,
    )

    refs.wait()

    def per_slot(slot, n):
        zero = jnp.zeros((BLOCK, qd_ref.shape[3]), F32)
        for b in range(blocks):
            dq_acc[slot * blocks + b] = zero
            dk_acc[slot * blocks + b] = zero
            dv_acc[slot * blocks + b] = zero
            for r in range(3):
                code = rf_ref[slot, r, b]
                list_ref[n] = ((slot * blocks + b) << 8) | ((code & (grid - 1)) << 1)
                n = n + ((code >> 6) == z).astype(jnp.int32)
        return n

    count = lax.fori_loop(0, NZ, per_slot, count)
    for i in range(STEP - 1):
        list_ref[count + i] = jnp.int32(1)

    def terms(item):
        query, key = item >> 8, (item >> 1) & (grid - 1)
        qs, qb = query >> 3, query & (blocks - 1)
        ks, kb = key >> 3, key & (blocks - 1)
        qrows = pl.ds(pl.multiple_of(qb * BLOCK, BLOCK), BLOCK)
        krows = pl.ds(pl.multiple_of(kb * BLOCK, BLOCK), BLOCK)
        return pair_terms(
            per_head(qd_ref[qs, 0, qrows, :]),
            per_head(qd_ref[qs, 1, qrows, :]),
            query_rows(nd_ref[qs, qb >> 1], qb),
            kv_ref[ks, 0, krows, :],
            kv_ref[ks, 1, krows, :],
            factor,
        )

    @pl.loop(0, (count + STEP - 1) // STEP)
    def _(i):
        items = [list_ref[STEP * i + j] for j in range(STEP)]
        sums = [terms(item) for item in items]
        for item, (dq, dk, dv) in zip(items, sums):
            spare = (item & 1) * grid
            dq_acc[(item >> 8) + spare] += dq
            dk_acc[((item >> 1) & (grid - 1)) + spare] += dk
            dv_acc[((item >> 1) & (grid - 1)) + spare] += dv

    @pl.loop(0, grid)
    def _(i):
        slot = i >> 3
        rows = pl.ds(pl.multiple_of((i & (blocks - 1)) * BLOCK, BLOCK), BLOCK)
        dq_out[slot, rows, :] = dq_acc[i].astype(BF16)
        dkv_out[slot, 0, rows, :] = (dk_acc[i] * factor).astype(BF16)
        dkv_out[slot, 1, rows, :] = dv_acc[i].astype(BF16)


def reduce_kernel(
    dq_in, dkv_in, dk_own, dv_own, part_in, glob_ref, dq_out, dk_out, dv_out,
    zbuf, zin, cin, ysum, ybuf, yin, r2in, t2, rin, totals,
    zsend, zrecv, ysend, yrecv, csend, crecv, gsend, grecv,
    *, factor,
):
    y, z, c = place()
    half = dk_out.shape[0] // 2
    me = y * NC + c
    zdev = [device(y, lax.rem(z + 1, NZ), c), device(y, lax.rem(z + NZ - 1, NZ), c)]
    ydev = [device(lax.rem(y + 1, NY), z, c), device(lax.rem(y + NY - 1, NY), z, c)]
    cdev = device(y, z, 1 - c)

    def member_device(offset):
        other = lax.rem(me + offset, NY * NC)
        return device(other // NC, z, lax.rem(other, NC))

    def row_device(offset):
        return device(y, lax.rem(z + offset, NZ), c)

    barrier = pltpu.get_barrier_semaphore()
    for offset in range(1, 8):
        for target in (member_device(offset), row_device(offset)):
            pl.semaphore_signal(barrier, inc=1, device_id=target, device_id_type=MESH)
    pl.semaphore_wait(barrier, 14)

    def halves(part):
        return pl.ds(part * half, half)

    def zparts(way, step):
        return (way,) if step == 1 else (1 - way, way)

    def zplain(way, step, part):
        return step == 1 or (step == 2 and part != way)

    def ztarget(way, step):
        return lax.rem(z + (5 - step if way == 0 else NZ - 5 + step), NZ)

    def zcopy(way, step, part):
        if zplain(way, step, part):
            source = dq_in.at[ztarget(way, step), halves(part)]
        else:
            source = zbuf.at[way, step - 1, halves(part)]
        return pltpu.make_async_remote_copy(
            src_ref=source,
            dst_ref=dq_out.at[way, halves(part)] if step == 4 else zin.at[way, step - 1, halves(part)],
            send_sem=zsend.at[way, step - 1, part],
            recv_sem=zrecv.at[way, step - 1, part],
            device_id=zdev[way],
            device_id_type=MESH,
        )

    def ccopy(offset, part, h):
        row = lax.rem(y + offset, NY)
        return pltpu.make_async_remote_copy(
            src_ref=dkv_in.at[row * NC + 1 - c, part, halves(h)],
            dst_ref=cin.at[offset, part, halves(h)],
            send_sem=csend.at[offset, part, h],
            recv_sem=crecv.at[offset, part, h],
            device_id=cdev,
            device_id_type=MESH,
        )

    def ycopy(way, step, part, h):
        return pltpu.make_async_remote_copy(
            src_ref=ysum.at[part, halves(h)] if step == 1 else ybuf.at[way, part, halves(h)],
            dst_ref=yin.at[way, step - 1, part, halves(h)],
            send_sem=ysend.at[way, step - 1, part, h],
            recv_sem=yrecv.at[way, step - 1, part, h],
            device_id=ydev[way],
            device_id_type=MESH,
        )

    def small(phase, offset):
        source, target = (
            (part_in.at[lax.rem(z + offset, NZ)], r2in.at[offset]),
            (t2, rin.at[offset]),
            (totals.at[me], totals.at[me]),
        )[phase]
        return pltpu.make_async_remote_copy(
            src_ref=source,
            dst_ref=target,
            send_sem=gsend.at[phase, offset],
            recv_sem=grecv.at[phase, offset],
            device_id=row_device(offset) if phase < 2 else member_device(offset),
            device_id_type=MESH,
        )

    for h in (0, 1):
        for part in (0, 1):
            ccopy(2, part, h).start()
    for way in (0, 1):
        zcopy(way, 1, way).start()
    for offset in range(1, 8):
        small(0, offset).start()
    for way in (0, 1):
        zcopy(way, 2, 1 - way).start()
    for h in (0, 1):
        for way in (0, 1):
            ccopy(1 if way == 0 else 3, 1 - way, h).start()
    for h in (0, 1):
        for way in (0, 1):
            ccopy(1 if way == 0 else 3, way, h).start()
    for h in (0, 1):
        for part in (0, 1):
            ccopy(0, part, h).start()

    def zround(step, late):
        for way in (0, 1):
            part = way if late else 1 - way
            zcopy(way, step, part).wait_recv()
            rows = halves(part)
            mine = dq_in[ztarget(way, step + 1), rows, :].astype(F32)
            zbuf[way, step, rows, :] = (mine + zin[way, step - 1, rows, :].astype(F32)).astype(BF16)
            zcopy(way, step + 1, part).start()

    def cadd(offset, part, h):
        ccopy(offset, part, h).wait_recv()
        row = lax.rem(y + offset, NY)
        return dkv_in[row * NC + c, part, halves(h), :].astype(F32) + cin[offset, part, halves(h), :].astype(F32)

    def ypass(way, part, h):
        total = cadd(1 if way == 0 else 3, part, h)
        if part == way:
            ycopy(way, 1, part, h).wait_recv()
            total = total + yin[way, 0, part, halves(h), :].astype(F32)
        ybuf[way, part, halves(h), :] = total.astype(BF16)
        ycopy(way, 2, part, h).start()

    for h in (0, 1):
        for part in (0, 1):
            ysum[part, halves(h), :] = cadd(2, part, h).astype(BF16)
            ycopy(part, 1, part, h).start()
    ypass(0, 1, 0)
    ypass(1, 0, 0)
    zround(1, True)
    for offset in range(1, 8):
        small(0, offset).wait_recv()
    total = part_in[z].astype(F32)
    for offset in range(1, 8):
        total = total + r2in[offset].astype(F32)
    t2[...] = total.astype(BF16)
    ypass(0, 1, 1)
    ypass(1, 0, 1)
    for offset in range(1, 8):
        small(1, offset).start()
    ypass(0, 0, 0)
    ypass(1, 1, 0)
    zround(2, False)
    zround(2, True)
    ypass(0, 0, 1)
    ypass(1, 1, 1)
    zround(3, False)
    for offset in range(1, 8):
        small(1, offset).wait_recv()
    totals[me, z] = t2[...]
    for offset in range(1, 8):
        totals[me, lax.rem(z + NZ - offset, NZ)] = rin[offset]
    zround(3, True)
    for offset in range(1, 8):
        small(2, offset).start()
    for offset in range(1, 8):
        small(2, offset).wait_recv()
    seq = lax.axis_index("seq")
    per_half = half // BLOCK
    for part, out, own in ((1, dv_out, dv_own), (0, dk_out, dk_own)):
        for h in (0, 1):
            total = cadd(0, part, h)
            for way in (0, 1):
                ycopy(way, 2, part, h).wait_recv()
                total = total + yin[way, 1, part, halves(h), :].astype(F32)
            for i in range(per_half):
                b = h * per_half + i
                rows = pl.ds(b * BLOCK, BLOCK)
                more = own[rows, :]
                for g in range(2):
                    whole = totals[pl.ds(4 * g + 2 * part, 2)].astype(F32).reshape(more.shape)
                    more = more + jnp.where(glob_ref[g] == seq * 2 * per_half + b, whole, jnp.zeros_like(whole))
                if part == 0:
                    more = more * factor
                out[rows, :] = (total[i * BLOCK : (i + 1) * BLOCK] + more).astype(BF16)
    for part in (0, 1):
        for way in (0, 1):
            zcopy(way, 4, part).wait_recv()
    for way in (0, 1):
        for step in range(1, 5):
            for part in zparts(way, step):
                zcopy(way, step, part).wait_send()
        for h in (0, 1):
            ycopy(way, 1, way, h).wait_send()
            for part in (0, 1):
                ycopy(way, 2, part, h).wait_send()
    for offset in range(NY):
        for part in (0, 1):
            for h in (0, 1):
                ccopy(offset, part, h).wait_send()
    for phase in range(3):
        for offset in range(1, 8):
            small(phase, offset).wait_send()


def last_kernel(part_ref, own_ref, arrived_ref, dk_in, dv_in, dq_out, dk_out, dv_out):
    y, z, c = place()
    for b in range(own_ref.shape[0] // BLOCK):
        rows = pl.ds(b * BLOCK, BLOCK)
        total = part_ref[z, rows, :].astype(F32) + own_ref[rows, :]
        total = total + arrived_ref[0, rows, :].astype(F32) + arrived_ref[1, rows, :].astype(F32)
        dq_out[rows, :] = total.T.astype(BF16)
    dk_out[...] = dk_in[...]
    dv_out[...] = dv_in[...]


def shards(queries, keys, values, outputs, d_outputs, log_norm, rand_owner, rand_local, glob_blocks):
    tokens, features = queries.shape
    blocks = tokens // BLOCK
    factor = 1.0 / math.sqrt(features // log_norm.shape[0])
    queries, keys, values, outputs, d_outputs, log_norm, owner, local, glob_blocks = (
        pltpu.with_memory_space_constraint(array, pltpu.HBM)
        for array in (
            queries, keys, values, outputs, d_outputs, log_norm, rand_owner.T, rand_local.T, glob_blocks
        )
    )
    vmem = pl.BlockSpec(memory_space=pltpu.VMEM)
    smem = pl.BlockSpec(memory_space=pltpu.SMEM)
    anywhere = pl.BlockSpec(memory_space=pl.ANY)
    hbm = pl.BlockSpec(memory_space=pltpu.HBM)
    dma = pltpu.SemaphoreType.DMA

    slices = (8, BLOCK // 2, features)
    eighths = (8, BLOCK // 16, features)
    qd, kv, nd, rf, dq_own, dk_own, dv_own, part = pl.pallas_call(
        functools.partial(gather_kernel, factor=factor),
        out_shape=(
            jax.ShapeDtypeStruct((NZ, 2, tokens, features), BF16),
            jax.ShapeDtypeStruct((NY * NC, 2, tokens, features), BF16),
            jax.ShapeDtypeStruct((NZ, blocks // 2 + 1, 8, BLOCK), F32),
            jax.ShapeDtypeStruct((NZ, 8, BLOCK), jnp.int32),
            jax.ShapeDtypeStruct((tokens, features), F32),
            jax.ShapeDtypeStruct((tokens, features), F32),
            jax.ShapeDtypeStruct((tokens, features), F32),
            jax.ShapeDtypeStruct(eighths, BF16),
        ),
        in_specs=[hbm] * 5 + [vmem] * 3 + [smem],
        out_specs=(anywhere,) * 2 + (vmem,) * 6,
        scratch_shapes=[
            pltpu.VMEM((tokens, features), BF16), pltpu.VMEM((tokens, features), BF16),
            pltpu.VMEM((tokens, features), BF16), pltpu.VMEM((tokens, features), BF16),
            pltpu.VMEM((tokens, features), BF16),
            pltpu.VMEM((blocks // 2 + 1, 8, BLOCK), F32), pltpu.VMEM(slices, BF16),
            pltpu.VMEM(slices, BF16), pltpu.VMEM(eighths, BF16), pltpu.VMEM(eighths, BF16),
            pltpu.VMEM(eighths[1:], BF16), pltpu.VMEM(eighths, BF16), pltpu.VMEM(eighths, BF16),
            pltpu.VMEM(slices, BF16), pltpu.VMEM(slices, F32), pltpu.VMEM(slices, F32),
            dma((2, 4, 5)), dma((2, 4, 5)), dma((2, 2, 2)), dma((2, 2, 2)),
            dma((NY, 2)), dma((NY, 2)), dma((5, 8)), dma((5, 8)), dma((10,)),
        ],
        compiler_params=pltpu.CompilerParams(collective_id=0, has_side_effects=True, vmem_limit_bytes=12 * MIB),
        name="gather",
    )(queries, d_outputs, keys, values, outputs, log_norm, owner, local, glob_blocks)

    dq_part, dkv_part = pl.pallas_call(
        functools.partial(pair_kernel, factor=factor),
        out_shape=(
            jax.ShapeDtypeStruct((NZ, tokens, features), BF16),
            jax.ShapeDtypeStruct((NY * NC, 2, tokens, features), BF16),
        ),
        in_specs=[anywhere, vmem, vmem, vmem],
        out_specs=(vmem, vmem),
        scratch_shapes=[
            pltpu.VMEM((NZ * blocks + 1, BLOCK, features), F32),
            pltpu.VMEM((NY * NC * blocks + 1, BLOCK, features), F32),
            pltpu.VMEM((NY * NC * blocks + 1, BLOCK, features), F32),
            pltpu.SMEM((NZ, 8, BLOCK), jnp.int32),
            pltpu.SMEM((256,), jnp.int32),
            dma,
        ],
        compiler_params=pltpu.CompilerParams(vmem_limit_bytes=16 * MIB),
        name="pairs",
    )(rf, qd, kv, nd)

    result = jax.ShapeDtypeStruct((tokens, features), BF16)
    arrived, dk, dv = pl.pallas_call(
        functools.partial(reduce_kernel, factor=factor),
        out_shape=(jax.ShapeDtypeStruct((2, tokens, features), BF16), result, result),
        in_specs=[vmem] * 5 + [smem],
        out_specs=(vmem,) * 3,
        scratch_shapes=[
            pltpu.VMEM((2, 4, tokens, features), BF16),
            pltpu.VMEM((2, 3, tokens, features), BF16),
            pltpu.VMEM((NY, 2, tokens, features), BF16),
            pltpu.VMEM((2, tokens, features), BF16),
            pltpu.VMEM((2, 2, tokens, features), BF16),
            pltpu.VMEM((2, 2, 2, tokens, features), BF16),
            pltpu.VMEM(eighths, BF16),
            pltpu.VMEM(eighths[1:], BF16),
            pltpu.VMEM(eighths, BF16),
            pltpu.VMEM((8,) + eighths, BF16),
            dma((2, 4, 2)), dma((2, 4, 2)), dma((2, 2, 2, 2)), dma((2, 2, 2, 2)),
            dma((NY, 2, 2)), dma((NY, 2, 2)), dma((3, 8)), dma((3, 8)),
        ],
        compiler_params=pltpu.CompilerParams(collective_id=1, has_side_effects=True, vmem_limit_bytes=24 * MIB),
        name="reduce",
    )(dq_part, dkv_part, dk_own, dv_own, part, glob_blocks)

    return tuple(pl.pallas_call(
        last_kernel,
        out_shape=(result,) * 3,
        in_specs=[vmem] * 5,
        out_specs=(vmem,) * 3,
        compiler_params=pltpu.CompilerParams(vmem_limit_bytes=8 * MIB),
        name="last",
    )(dq_part, dq_own, arrived, dk, dv))


def solution(mesh):
    placed = (
        P("seq", "head"), P("seq", "head"), P("seq", "head"), P("seq", "head"), P("seq", "head"),
        P("head", "seq"), P("seq", None), P("seq", None), P(),
    )
    return jax.shard_map(
        shards,
        mesh=mesh,
        in_specs=placed,
        out_specs=(P("seq", "head"), P("seq", "head"), P("seq", "head")),
        check_vma=False,
    )
```

```python
import functools
import math

import jax
import jax.numpy as jnp
from jax import lax
from jax.experimental import pallas as pl
from jax.experimental.pallas import tpu as pltpu
from jax.sharding import PartitionSpec as P

BLOCK = 128
NY, NZ, NC = 4, 8, 2
MESH = pl.DeviceIdType.MESH
F32 = jnp.float32
BF16 = jnp.bfloat16
MIB = 1024 * 1024
STEP = 6


def place():
    seq = lax.axis_index("seq")
    core = lax.rem(seq, NC)
    z = lax.rem(seq // NC, NZ)
    y = seq // (NC * NZ)
    return y, z, core


def device(y, z, core):
    return {"seq": (y * NZ + z) * NC + core}


def per_head(x):
    lane = lax.broadcasted_iota(jnp.int32, x.shape, 1)
    zero = jnp.zeros_like(x)
    low = lane < x.shape[1] // 2
    return jnp.concatenate([jnp.where(low, x, zero), jnp.where(low, zero, x)], axis=0)


def pair_terms(q2, d2, nd, k, v, factor):
    k = k * factor
    across = (((1,), (1,)), ((), ()))
    scores = lax.dot_general(k, q2, across, preferred_element_type=F32)
    grads = lax.dot_general(v, d2, across, preferred_element_type=F32)
    norm = jnp.concatenate([nd[0:1], nd[1:2]], axis=1)
    delta = jnp.concatenate([nd[2:3], nd[3:4]], axis=1)
    weights = jnp.exp(scores - norm)
    grad_scores = weights * (grads - delta)
    weights_low = weights.astype(BF16)
    scores_low = grad_scores.astype(BF16)
    dv = jnp.dot(weights_low, d2, preferred_element_type=F32)
    dk = jnp.dot(scores_low, q2, preferred_element_type=F32)
    turned = k.T
    half = turned.shape[0] // 2
    dq = jnp.concatenate(
        [
            jnp.dot(turned[:half], scores_low[:, :BLOCK], preferred_element_type=F32),
            jnp.dot(turned[half:], scores_low[:, BLOCK:], preferred_element_type=F32),
        ],
        axis=0,
    )
    return dq, dk, dv


def query_rows(nd_tile, b):
    return jnp.where(lax.rem(b, 2) == 0, nd_tile[0:4], nd_tile[4:8])


def gather_kernel(
    q_hbm, d_hbm, k_hbm, v_hbm, o_hbm, norm_ref, owner_ref, local_ref, glob_ref,
    qd_out, kv_out, nd_out, rf_out, dq_out, dk_out, dv_out, t1,
    q_ref, d_ref, k_ref, v_ref, o_ref, nd_ref, cand_ref,
    g1in, s1, g2in, s2, g3in, s3, gkv, gacc, r1in,
    zsend, zrecv, ysend, yrecv, csend, crecv, gsend, grecv, lsem,
    *, factor,
):
    y, z, c = place()
    tokens = q_ref.shape[0]
    blocks = tokens // BLOCK
    half = BLOCK // 2
    loads = [
        pltpu.make_async_copy(source, target, lsem.at[i])
        for i, (source, target) in enumerate(
            ((k_hbm, k_ref), (v_hbm, v_ref), (o_hbm, o_ref), (d_hbm, d_ref), (q_hbm, q_ref))
        )
    ]
    for copy in loads:
        copy.start()
    zdev = [device(y, lax.rem(z + 1, NZ), c), device(y, lax.rem(z + NZ - 1, NZ), c)]
    ydev = [device(lax.rem(y + 1, NY), z, c), device(lax.rem(y + NY - 1, NY), z, c)]
    cdev = device(y, z, 1 - c)
    me = y * NC + c

    def member(offset):
        return lax.rem(me + offset, NY * NC)

    def member_device(offset):
        other = member(offset)
        return device(other // NC, z, lax.rem(other, NC))

    def row_device(offset):
        return device(y, lax.rem(z + offset, NZ), c)

    barrier = pltpu.get_barrier_semaphore()
    for offset in range(1, 8):
        for target in (member_device(offset), row_device(offset)):
            pl.semaphore_signal(barrier, inc=1, device_id=target, device_id_type=MESH)
    pl.semaphore_wait(barrier, 14)

    def zwhere(part, slot):
        if part < 4:
            return qd_out.at[slot, part // 2, pl.ds((part % 2) * tokens // 2, tokens // 2)]
        return nd_out.at[slot]

    def zown(part):
        if part < 4:
            return (q_hbm, d_hbm)[part // 2].at[pl.ds((part % 2) * tokens // 2, tokens // 2)]
        return nd_ref

    def zcopy(way, step, part):
        slot = lax.rem(z + (NZ - step + 1 if way == 0 else step - 1), NZ)
        return pltpu.make_async_remote_copy(
            src_ref=zown(part) if step == 1 else zwhere(part, slot),
            dst_ref=zwhere(part, slot),
            send_sem=zsend.at[way, step - 1, part],
            recv_sem=zrecv.at[way, step - 1, part],
            device_id=zdev[way],
            device_id_type=MESH,
        )

    def zparts(way, step):
        if step < 4:
            return (0, 1, 2, 3, 4)
        return (0, 1, 4) if way == 0 else (2, 3)

    def ycopy(way, step, part):
        row = lax.rem(y + ((NY if step == 1 else NY - 1) if way == 0 else step - 1), NY)
        slot = row * NC + c
        return pltpu.make_async_remote_copy(
            src_ref=(k_hbm, v_hbm)[part] if step == 1 else kv_out.at[slot, part],
            dst_ref=kv_out.at[slot, part],
            send_sem=ysend.at[way, step - 1, part],
            recv_sem=yrecv.at[way, step - 1, part],
            device_id=ydev[way],
            device_id_type=MESH,
        )

    def ccopy(offset, part):
        slot = lax.rem(y + offset, NY) * NC + c
        return pltpu.make_async_remote_copy(
            src_ref=(k_hbm, v_hbm)[part] if offset == 0 else kv_out.at[slot, part],
            dst_ref=kv_out.at[slot, part],
            send_sem=csend.at[offset, part],
            recv_sem=crecv.at[offset, part],
            device_id=cdev,
            device_id_type=MESH,
        )

    def small(phase, offset):
        over_column = phase in (0, 3, 4)
        other = member(offset) if over_column else lax.rem(z + offset, NZ)
        source, target = (
            (cand_ref.at[other], g1in.at[offset]),
            (s1.at[other], g2in.at[offset]),
            (s2, g3in.at[offset]),
            (gkv.at[me], gkv.at[me]),
            (gacc.at[other], r1in.at[offset]),
        )[phase]
        return pltpu.make_async_remote_copy(
            src_ref=source,
            dst_ref=target,
            send_sem=gsend.at[phase, offset],
            recv_sem=grecv.at[phase, offset],
            device_id=member_device(offset) if over_column else row_device(offset),
            device_id_type=MESH,
        )

    def small_start(phase):
        for offset in range(1, 8):
            small(phase, offset).start()

    def small_wait(phase):
        for offset in range(1, 8):
            small(phase, offset).wait_recv()

    def zstart(step, parts):
        for part in parts:
            for way in (0, 1):
                if part in zparts(way, step):
                    zcopy(way, step, part).start()

    def zpass(step, parts):
        for part in parts:
            for way in (0, 1):
                if part in zparts(way, step):
                    zcopy(way, step, part).wait_recv()
                    if step < 4 and part in zparts(way, step + 1):
                        zcopy(way, step + 1, part).start()

    def block_rows(b):
        return pl.ds(pl.multiple_of(b * BLOCK, BLOCK), BLOCK)

    def window(first, end):
        @pl.loop(first, end)
        def _(i):
            up = (i >= blocks).astype(jnp.int32)
            down = (i >= 2 * blocks - 1).astype(jnp.int32)
            low = i - up * blocks - down * (blocks - 1)
            qb = low + down
            kb = low + up - down
            rows, krows = block_rows(qb), block_rows(kb)
            dq, dk, dv = pair_terms(
                per_head(q_ref[rows, :]), per_head(d_ref[rows, :]), query_rows(nd_ref[qb // 2], qb),
                k_ref[krows, :], v_ref[krows, :], factor,
            )
            dq_out[rows, :] += dq
            dk_out[krows, :] += dk
            dv_out[krows, :] += dv

    def whole(first, end):
        @pl.loop(first, end)
        def _(i):
            b, g = i // 2, lax.rem(i, 2)
            rows = block_rows(b)
            part = 4 * g
            dq, dk, dv = pair_terms(
                per_head(q_ref[rows, :]), per_head(d_ref[rows, :]), query_rows(nd_ref[b // 2], b),
                jnp.concatenate([gkv[part], gkv[part + 1]], axis=0),
                jnp.concatenate([gkv[part + 2], gkv[part + 3]], axis=0),
                factor,
            )
            dq_out[rows, :] += dq
            gacc[part] += dk[:half]
            gacc[part + 1] += dk[half:]
            gacc[part + 2] += dv[:half]
            gacc[part + 3] += dv[half:]

    def ystep1(part):
        for way in (0, 1):
            ycopy(way, 1, part).wait_recv()
            if part == way:
                ycopy(way, 2, part).start()
            ccopy(NY - 1 if way == 0 else 1, part).start()

    zstart(1, (0,))
    loads[0].wait()
    loads[1].wait()
    seq = lax.axis_index("seq")
    for g in range(2):
        local_block = glob_ref[g] - seq * blocks
        for i, ref in enumerate((k_ref, v_ref)):
            block = jnp.zeros((BLOCK, k_ref.shape[1]), BF16)
            for b in range(blocks):
                block = jnp.where(local_block == b, ref[pl.ds(b * BLOCK, BLOCK), :], block)
            cand_ref[4 * g + 2 * i] = block[:half]
            cand_ref[4 * g + 2 * i + 1] = block[half:]
    owner = owner_ref[...]
    column = jnp.bitwise_and(owner >> 1, NZ - 1)
    other = (owner >> 4) * NC + jnp.bitwise_and(owner, 1)
    nd_ref[blocks // 2] = jnp.zeros(nd_ref.shape[1:], F32)
    nd_ref[blocks // 2, 0:3, 0:blocks] = ((column * (NY * NC) + other) * blocks + local_ref[...]).astype(F32)
    loads[2].wait()
    loads[3].wait()

    def row_values(b):
        rows = pl.ds(b * BLOCK, BLOCK)
        turned = (o_ref[rows, :].astype(F32) * d_ref[rows, :].astype(F32)).T
        nd_ref[b // 2, 4 * (b % 2) : 4 * (b % 2) + 4, :] = jnp.concatenate(
            [
                norm_ref[:, rows],
                jnp.sum(turned[: turned.shape[0] // 2], axis=0, keepdims=True),
                jnp.sum(turned[turned.shape[0] // 2 :], axis=0, keepdims=True),
            ],
            axis=0,
        )

    row_values(0)
    small_start(0)
    zstart(1, (1,))
    for part in (0, 1):
        for way in (0, 1):
            ycopy(way, 1, part).start()
        ccopy(0, part).start()
    for b in range(1, blocks):
        row_values(b)
    loads[4].wait()
    local = [
        pltpu.make_async_copy(q_ref, qd_out.at[z, 0], lsem.at[5]),
        pltpu.make_async_copy(d_ref, qd_out.at[z, 1], lsem.at[6]),
        pltpu.make_async_copy(nd_ref, nd_out.at[z], lsem.at[7]),
        pltpu.make_async_copy(k_ref, kv_out.at[me, 0], lsem.at[8]),
        pltpu.make_async_copy(v_ref, kv_out.at[me, 1], lsem.at[9]),
    ]
    for copy in local:
        copy.start()

    @pl.loop(0, blocks)
    def _(b):
        zero = jnp.zeros((BLOCK, q_ref.shape[1]), F32)
        dq_out[block_rows(b), :] = zero
        dk_out[block_rows(b), :] = zero
        dv_out[block_rows(b), :] = zero
        gacc[b] = zero[:half]

    small_wait(0)
    slice_sum = cand_ref[me].astype(F32)
    for offset in range(1, 8):
        slice_sum = slice_sum + g1in[offset].astype(F32)
    s1[...] = slice_sum.astype(BF16).reshape(s1.shape)
    window(0, 2)
    small_start(1)
    zstart(1, (4, 2, 3))
    window(2, 4)
    zpass(1, (0,))
    window(4, 5)
    small_wait(1)
    part_sum = s1[z].astype(F32)
    for offset in range(1, 8):
        part_sum = part_sum + g2in[offset].astype(F32)
    s2[...] = part_sum.astype(BF16)
    window(5, 6)
    small_start(2)
    zpass(1, (1, 4))
    ystep1(0)
    window(6, 9)
    zpass(1, (2,))
    window(9, 10)
    zpass(1, (3,))
    ystep1(1)
    window(10, 11)
    zpass(2, (0,))
    small_wait(2)
    s3[z] = s2[...]
    for offset in range(1, 8):
        s3[lax.rem(z + NZ - offset, NZ)] = g3in[offset]
    gkv[me] = s3[...].reshape(gkv.shape[1:])
    window(11, 12)
    small_start(3)
    zpass(2, (1, 4))
    window(12, 16)
    zpass(2, (2,))
    for way in (0, 1):
        ycopy(way, 2, way).wait_recv()
        ccopy(2, way).start()
    small_wait(3)
    whole(0, 4)
    zpass(2, (3,))
    whole(4, 10)
    zpass(3, (0,))
    whole(10, 16)
    window(16, 17)
    small_start(4)
    zpass(3, (1, 4))
    window(17, 20)
    small_wait(4)
    slice_sum = gacc[me]
    for offset in range(1, 8):
        slice_sum = slice_sum + r1in[offset]
    t1[...] = slice_sum.astype(BF16).reshape(t1.shape)
    zpass(3, (2,))
    window(20, 22)
    zpass(3, (3,))
    zpass(4, (0, 2, 1, 4, 3))
    for offset in range(NY):
        for part in (0, 1):
            ccopy(offset, part).wait()
    for way in (0, 1):
        for step in range(1, 5):
            for part in zparts(way, step):
                zcopy(way, step, part).wait_send()
        for part in (0, 1):
            ycopy(way, 1, part).wait_send()
        ycopy(way, 2, way).wait_send()
    for phase in range(5):
        for offset in range(1, 8):
            small(phase, offset).wait_send()
    for copy in local:
        copy.wait()
    for slot in range(NZ):
        rf_out[slot] = nd_out[slot, blocks // 2].astype(jnp.int32)


def pair_kernel(
    rf_any, qd_ref, kv_ref, nd_ref, dq_out, dkv_out, dq_acc, dk_acc, dv_acc, rf_ref, list_ref, sem,
    *, factor,
):
    y, z, c = place()
    blocks = qd_ref.shape[2] // BLOCK
    grid = NZ * blocks
    refs = pltpu.make_async_copy(rf_any, rf_ref, sem)
    refs.start()

    def window_item(n, slot, b, seq, key_block, wanted):
        member = (seq // (NC * NZ)) * NC + lax.rem(seq, NC)
        list_ref[n] = ((slot * blocks + b) << 8) | ((member * blocks + key_block) << 1)
        return n + wanted.astype(jnp.int32)

    seq = (y * NZ + z) * NC + c
    nearby = jnp.where(c == 0, seq + 1, seq - 1)
    count = window_item(
        jnp.int32(0), z, jnp.where(c == 0, blocks - 1, 0), nearby, jnp.where(c == 0, 0, blocks - 1), seq >= 0
    )
    far_slot = jnp.where(c == 0, lax.rem(z + 1, NZ), lax.rem(z + NZ - 1, NZ))
    far_seq = (y * NZ + far_slot) * NC + c
    far_key = jnp.where(c == 0, far_seq - 1, far_seq + 1)
    inside = jnp.logical_and(far_key >= 0, far_key < NY * NZ * NC)
    count = window_item(
        count, far_slot, jnp.where(c == 0, 0, blocks - 1),
        jnp.clip(far_key, 0, NY * NZ * NC - 1), jnp.where(c == 0, blocks - 1, 0), inside,
    )

    refs.wait()

    def per_slot(slot, n):
        zero = jnp.zeros((BLOCK, qd_ref.shape[3]), F32)
        for b in range(blocks):
            dq_acc[slot * blocks + b] = zero
            dk_acc[slot * blocks + b] = zero
            dv_acc[slot * blocks + b] = zero
            for r in range(3):
                code = rf_ref[slot, r, b]
                list_ref[n] = ((slot * blocks + b) << 8) | ((code & (grid - 1)) << 1)
                n = n + ((code >> 6) == z).astype(jnp.int32)
        return n

    count = lax.fori_loop(0, NZ, per_slot, count)
    for i in range(STEP - 1):
        list_ref[count + i] = jnp.int32(1)

    def terms(item):
        query, key = item >> 8, (item >> 1) & (grid - 1)
        qs, qb = query >> 3, query & (blocks - 1)
        ks, kb = key >> 3, key & (blocks - 1)
        qrows = pl.ds(pl.multiple_of(qb * BLOCK, BLOCK), BLOCK)
        krows = pl.ds(pl.multiple_of(kb * BLOCK, BLOCK), BLOCK)
        return pair_terms(
            per_head(qd_ref[qs, 0, qrows, :]),
            per_head(qd_ref[qs, 1, qrows, :]),
            query_rows(nd_ref[qs, qb >> 1], qb),
            kv_ref[ks, 0, krows, :],
            kv_ref[ks, 1, krows, :],
            factor,
        )

    @pl.loop(0, (count + STEP - 1) // STEP)
    def _(i):
        items = [list_ref[STEP * i + j] for j in range(STEP)]
        sums = [terms(item) for item in items]
        for item, (dq, dk, dv) in zip(items, sums):
            spare = (item & 1) * grid
            dq_acc[(item >> 8) + spare] += dq
            dk_acc[((item >> 1) & (grid - 1)) + spare] += dk
            dv_acc[((item >> 1) & (grid - 1)) + spare] += dv

    @pl.loop(0, grid)
    def _(i):
        slot = i >> 3
        rows = pl.ds(pl.multiple_of((i & (blocks - 1)) * BLOCK, BLOCK), BLOCK)
        dq_out[slot, rows, :] = dq_acc[i].astype(BF16)
        dkv_out[slot, 0, rows, :] = (dk_acc[i] * factor).astype(BF16)
        dkv_out[slot, 1, rows, :] = dv_acc[i].astype(BF16)


def reduce_kernel(
    dq_in, dkv_in, dk_own, dv_own, part_in, glob_ref, dq_out, dk_out, dv_out,
    zbuf, zin, cin, ysum, ybuf, yin, r2in, t2, rin, totals,
    zsend, zrecv, ysend, yrecv, csend, crecv, gsend, grecv,
    *, factor,
):
    y, z, c = place()
    half = dk_out.shape[0] // 2
    me = y * NC + c
    zdev = [device(y, lax.rem(z + 1, NZ), c), device(y, lax.rem(z + NZ - 1, NZ), c)]
    ydev = [device(lax.rem(y + 1, NY), z, c), device(lax.rem(y + NY - 1, NY), z, c)]
    cdev = device(y, z, 1 - c)

    def member_device(offset):
        other = lax.rem(me + offset, NY * NC)
        return device(other // NC, z, lax.rem(other, NC))

    def row_device(offset):
        return device(y, lax.rem(z + offset, NZ), c)

    barrier = pltpu.get_barrier_semaphore()
    for offset in range(1, 8):
        for target in (member_device(offset), row_device(offset)):
            pl.semaphore_signal(barrier, inc=1, device_id=target, device_id_type=MESH)
    pl.semaphore_wait(barrier, 14)

    def halves(part):
        return pl.ds(part * half, half)

    def zparts(way, step):
        return (way,) if step == 1 else (1 - way, way)

    def zplain(way, step, part):
        return step == 1 or (step == 2 and part != way)

    def ztarget(way, step):
        return lax.rem(z + (5 - step if way == 0 else NZ - 5 + step), NZ)

    def zcopy(way, step, part):
        if zplain(way, step, part):
            source = dq_in.at[ztarget(way, step), halves(part)]
        else:
            source = zbuf.at[way, step - 1, halves(part)]
        return pltpu.make_async_remote_copy(
            src_ref=source,
            dst_ref=dq_out.at[way, halves(part)] if step == 4 else zin.at[way, step - 1, halves(part)],
            send_sem=zsend.at[way, step - 1, part],
            recv_sem=zrecv.at[way, step - 1, part],
            device_id=zdev[way],
            device_id_type=MESH,
        )

    def ccopy(offset, part, h):
        row = lax.rem(y + offset, NY)
        return pltpu.make_async_remote_copy(
            src_ref=dkv_in.at[row * NC + 1 - c, part, halves(h)],
            dst_ref=cin.at[offset, part, halves(h)],
            send_sem=csend.at[offset, part, h],
            recv_sem=crecv.at[offset, part, h],
            device_id=cdev,
            device_id_type=MESH,
        )

    def ycopy(way, step, part, h):
        return pltpu.make_async_remote_copy(
            src_ref=ysum.at[part, halves(h)] if step == 1 else ybuf.at[way, part, halves(h)],
            dst_ref=yin.at[way, step - 1, part, halves(h)],
            send_sem=ysend.at[way, step - 1, part, h],
            recv_sem=yrecv.at[way, step - 1, part, h],
            device_id=ydev[way],
            device_id_type=MESH,
        )

    def small(phase, offset):
        source, target = (
            (part_in.at[lax.rem(z + offset, NZ)], r2in.at[offset]),
            (t2, rin.at[offset]),
            (totals.at[me], totals.at[me]),
        )[phase]
        return pltpu.make_async_remote_copy(
            src_ref=source,
            dst_ref=target,
            send_sem=gsend.at[phase, offset],
            recv_sem=grecv.at[phase, offset],
            device_id=row_device(offset) if phase < 2 else member_device(offset),
            device_id_type=MESH,
        )

    for h in (0, 1):
        for part in (0, 1):
            ccopy(2, part, h).start()
    for way in (0, 1):
        zcopy(way, 1, way).start()
    for offset in range(1, 8):
        small(0, offset).start()
    for way in (0, 1):
        zcopy(way, 2, 1 - way).start()
    for h in (0, 1):
        for way in (0, 1):
            ccopy(1 if way == 0 else 3, 1 - way, h).start()
    for h in (0, 1):
        for way in (0, 1):
            ccopy(1 if way == 0 else 3, way, h).start()
    for h in (0, 1):
        for part in (0, 1):
            ccopy(0, part, h).start()

    def zround(step, late):
        for way in (0, 1):
            part = way if late else 1 - way
            zcopy(way, step, part).wait_recv()
            rows = halves(part)
            mine = dq_in[ztarget(way, step + 1), rows, :].astype(F32)
            zbuf[way, step, rows, :] = (mine + zin[way, step - 1, rows, :].astype(F32)).astype(BF16)
            zcopy(way, step + 1, part).start()

    def cadd(offset, part, h):
        ccopy(offset, part, h).wait_recv()
        row = lax.rem(y + offset, NY)
        return dkv_in[row * NC + c, part, halves(h), :].astype(F32) + cin[offset, part, halves(h), :].astype(F32)

    def ypass(way, part, h):
        total = cadd(1 if way == 0 else 3, part, h)
        if part == way:
            ycopy(way, 1, part, h).wait_recv()
            total = total + yin[way, 0, part, halves(h), :].astype(F32)
        ybuf[way, part, halves(h), :] = total.astype(BF16)
        ycopy(way, 2, part, h).start()

    for h in (0, 1):
        for part in (0, 1):
            ysum[part, halves(h), :] = cadd(2, part, h).astype(BF16)
            ycopy(part, 1, part, h).start()
    ypass(0, 1, 0)
    ypass(1, 0, 0)
    zround(1, True)
    for offset in range(1, 8):
        small(0, offset).wait_recv()
    total = part_in[z].astype(F32)
    for offset in range(1, 8):
        total = total + r2in[offset].astype(F32)
    t2[...] = total.astype(BF16)
    ypass(0, 1, 1)
    ypass(1, 0, 1)
    for offset in range(1, 8):
        small(1, offset).start()
    ypass(0, 0, 0)
    ypass(1, 1, 0)
    zround(2, False)
    zround(2, True)
    ypass(0, 0, 1)
    ypass(1, 1, 1)
    zround(3, False)
    for offset in range(1, 8):
        small(1, offset).wait_recv()
    totals[me, z] = t2[...]
    for offset in range(1, 8):
        totals[me, lax.rem(z + NZ - offset, NZ)] = rin[offset]
    zround(3, True)
    for offset in range(1, 8):
        small(2, offset).start()
    for offset in range(1, 8):
        small(2, offset).wait_recv()
    seq = lax.axis_index("seq")
    per_half = half // BLOCK
    for part, out, own in ((1, dv_out, dv_own), (0, dk_out, dk_own)):
        for h in (0, 1):
            total = cadd(0, part, h)
            for way in (0, 1):
                ycopy(way, 2, part, h).wait_recv()
                total = total + yin[way, 1, part, halves(h), :].astype(F32)
            for i in range(per_half):
                b = h * per_half + i
                rows = pl.ds(b * BLOCK, BLOCK)
                more = own[rows, :]
                for g in range(2):
                    whole = totals[pl.ds(4 * g + 2 * part, 2)].astype(F32).reshape(more.shape)
                    more = more + jnp.where(glob_ref[g] == seq * 2 * per_half + b, whole, jnp.zeros_like(whole))
                if part == 0:
                    more = more * factor
                out[rows, :] = (total[i * BLOCK : (i + 1) * BLOCK] + more).astype(BF16)
    for part in (0, 1):
        for way in (0, 1):
            zcopy(way, 4, part).wait_recv()
    for way in (0, 1):
        for step in range(1, 5):
            for part in zparts(way, step):
                zcopy(way, step, part).wait_send()
        for h in (0, 1):
            ycopy(way, 1, way, h).wait_send()
            for part in (0, 1):
                ycopy(way, 2, part, h).wait_send()
    for offset in range(NY):
        for part in (0, 1):
            for h in (0, 1):
                ccopy(offset, part, h).wait_send()
    for phase in range(3):
        for offset in range(1, 8):
            small(phase, offset).wait_send()


def last_kernel(part_ref, own_ref, arrived_ref, dk_in, dv_in, dq_out, dk_out, dv_out):
    y, z, c = place()
    for b in range(own_ref.shape[0] // BLOCK):
        rows = pl.ds(b * BLOCK, BLOCK)
        total = part_ref[z, rows, :].astype(F32) + own_ref[rows, :]
        total = total + arrived_ref[0, rows, :].astype(F32) + arrived_ref[1, rows, :].astype(F32)
        dq_out[rows, :] = total.T.astype(BF16)
    dk_out[...] = dk_in[...]
    dv_out[...] = dv_in[...]


def shards(queries, keys, values, outputs, d_outputs, log_norm, rand_owner, rand_local, glob_blocks):
    tokens, features = queries.shape
    blocks = tokens // BLOCK
    factor = 1.0 / math.sqrt(features // log_norm.shape[0])
    queries, keys, values, outputs, d_outputs, log_norm, owner, local, glob_blocks = (
        pltpu.with_memory_space_constraint(array, pltpu.HBM)
        for array in (
            queries, keys, values, outputs, d_outputs, log_norm, rand_owner.T, rand_local.T, glob_blocks
        )
    )
    vmem = pl.BlockSpec(memory_space=pltpu.VMEM)
    smem = pl.BlockSpec(memory_space=pltpu.SMEM)
    anywhere = pl.BlockSpec(memory_space=pl.ANY)
    hbm = pl.BlockSpec(memory_space=pltpu.HBM)
    dma = pltpu.SemaphoreType.DMA

    slices = (8, BLOCK // 2, features)
    eighths = (8, BLOCK // 16, features)
    qd, kv, nd, rf, dq_own, dk_own, dv_own, part = pl.pallas_call(
        functools.partial(gather_kernel, factor=factor),
        out_shape=(
            jax.ShapeDtypeStruct((NZ, 2, tokens, features), BF16),
            jax.ShapeDtypeStruct((NY * NC, 2, tokens, features), BF16),
            jax.ShapeDtypeStruct((NZ, blocks // 2 + 1, 8, BLOCK), F32),
            jax.ShapeDtypeStruct((NZ, 8, BLOCK), jnp.int32),
            jax.ShapeDtypeStruct((tokens, features), F32),
            jax.ShapeDtypeStruct((tokens, features), F32),
            jax.ShapeDtypeStruct((tokens, features), F32),
            jax.ShapeDtypeStruct(eighths, BF16),
        ),
        in_specs=[hbm] * 5 + [vmem] * 3 + [smem],
        out_specs=(anywhere,) * 2 + (vmem,) * 6,
        scratch_shapes=[
            pltpu.VMEM((tokens, features), BF16), pltpu.VMEM((tokens, features), BF16),
            pltpu.VMEM((tokens, features), BF16), pltpu.VMEM((tokens, features), BF16),
            pltpu.VMEM((tokens, features), BF16),
            pltpu.VMEM((blocks // 2 + 1, 8, BLOCK), F32), pltpu.VMEM(slices, BF16),
            pltpu.VMEM(slices, BF16), pltpu.VMEM(eighths, BF16), pltpu.VMEM(eighths, BF16),
            pltpu.VMEM(eighths[1:], BF16), pltpu.VMEM(eighths, BF16), pltpu.VMEM(eighths, BF16),
            pltpu.VMEM(slices, BF16), pltpu.VMEM(slices, F32), pltpu.VMEM(slices, F32),
            dma((2, 4, 5)), dma((2, 4, 5)), dma((2, 2, 2)), dma((2, 2, 2)),
            dma((NY, 2)), dma((NY, 2)), dma((5, 8)), dma((5, 8)), dma((10,)),
        ],
        compiler_params=pltpu.CompilerParams(collective_id=0, has_side_effects=True, vmem_limit_bytes=12 * MIB),
        name="gather",
    )(queries, d_outputs, keys, values, outputs, log_norm, owner, local, glob_blocks)

    dq_part, dkv_part = pl.pallas_call(
        functools.partial(pair_kernel, factor=factor),
        out_shape=(
            jax.ShapeDtypeStruct((NZ, tokens, features), BF16),
            jax.ShapeDtypeStruct((NY * NC, 2, tokens, features), BF16),
        ),
        in_specs=[anywhere, vmem, vmem, vmem],
        out_specs=(vmem, vmem),
        scratch_shapes=[
            pltpu.VMEM((NZ * blocks + 1, BLOCK, features), F32),
            pltpu.VMEM((NY * NC * blocks + 1, BLOCK, features), F32),
            pltpu.VMEM((NY * NC * blocks + 1, BLOCK, features), F32),
            pltpu.SMEM((NZ, 8, BLOCK), jnp.int32),
            pltpu.SMEM((256,), jnp.int32),
            dma,
        ],
        compiler_params=pltpu.CompilerParams(vmem_limit_bytes=16 * MIB),
        name="pairs",
    )(rf, qd, kv, nd)

    result = jax.ShapeDtypeStruct((tokens, features), BF16)
    arrived, dk, dv = pl.pallas_call(
        functools.partial(reduce_kernel, factor=factor),
        out_shape=(jax.ShapeDtypeStruct((2, tokens, features), BF16), result, result),
        in_specs=[vmem] * 5 + [smem],
        out_specs=(vmem,) * 3,
        scratch_shapes=[
            pltpu.VMEM((2, 4, tokens, features), BF16),
            pltpu.VMEM((2, 3, tokens, features), BF16),
            pltpu.VMEM((NY, 2, tokens, features), BF16),
            pltpu.VMEM((2, tokens, features), BF16),
            pltpu.VMEM((2, 2, tokens, features), BF16),
            pltpu.VMEM((2, 2, 2, tokens, features), BF16),
            pltpu.VMEM(eighths, BF16),
            pltpu.VMEM(eighths[1:], BF16),
            pltpu.VMEM(eighths, BF16),
            pltpu.VMEM((8,) + eighths, BF16),
            dma((2, 4, 2)), dma((2, 4, 2)), dma((2, 2, 2, 2)), dma((2, 2, 2, 2)),
            dma((NY, 2, 2)), dma((NY, 2, 2)), dma((3, 8)), dma((3, 8)),
        ],
        compiler_params=pltpu.CompilerParams(collective_id=1, has_side_effects=True, vmem_limit_bytes=24 * MIB),
        name="reduce",
    )(dq_part, dkv_part, dk_own, dv_own, part, glob_blocks)

    return tuple(pl.pallas_call(
        last_kernel,
        out_shape=(result,) * 3,
        in_specs=[vmem] * 5,
        out_specs=(vmem,) * 3,
        compiler_params=pltpu.CompilerParams(vmem_limit_bytes=8 * MIB),
        name="last",
    )(dq_part, dq_own, arrived, dk, dv))


def solution(mesh):
    placed = (
        P("seq", "head"), P("seq", "head"), P("seq", "head"), P("seq", "head"), P("seq", "head"),
        P("head", "seq"), P("seq", None), P("seq", None), P(),
    )
    return jax.shard_map(
        shards,
        mesh=mesh,
        in_specs=placed,
        out_specs=(P("seq", "head"), P("seq", "head"), P("seq", "head")),
        check_vma=False,
    )
```
